32 devices in a mesh: dp: 8 (over z, x), tok: 4 (over y, core).
Axes of the slice: x: 2, y: 2, z: 4, core: 2. Of those that a mesh axis runs over, the one named last changes fastest.
Arguments:
- inputs: bfloat16 [32, 1024, 768], P('dp', 'tok'), may hold values from -6 to 6
- history: bfloat16 [24, 32, 1024, 768], P(None, 'dp', 'tok'), may hold values from -6 to 6
- document_lengths: int32 [32, 8], P('dp'), may hold values from 1 to 512, 1024 in all within a row
- cotangent: bfloat16 [32, 1024, 768], P('dp', 'tok')
- attention_params: float32 [2363904], P(('dp', 'tok'))
- attention_first: float32 [2363904], P(('dp', 'tok')), may hold values from -0.078125 to 0.078125
- attention_second: float32 [2363904], P(('dp', 'tok')), may hold values from 3.0517579e-06 to 0.00030517578
- feedforward_params: float32 [4723968], P(('dp', 'tok'))
- feedforward_first: float32 [4723968], P(('dp', 'tok')), may hold values from -0.078125 to 0.078125
- feedforward_second: float32 [4723968], P(('dp', 'tok')), may hold values from 3.0517579e-06 to 0.00030517578
- mixing_offsets: float32 [25], replicated, may hold values from -0.5 to 0.5
- mixing_first: float32 [25], replicated, may hold values from -2.5 to 2.5
- mixing_second: float32 [25], replicated, may hold values from 0.0030517578 to 0.30517578
- step_count: int32 [1], replicated, may hold values from 1 to 5
Outputs:
- mixed: bfloat16 [32, 1024, 768], P('dp', 'tok')
- grad_inputs: float32 [32, 1024, 768], P('dp', 'tok')
- grad_history: float32 [24, 32, 1024, 768], P(None, 'dp', 'tok')
- attention_new: float32 [2363904], P(('dp', 'tok'))
- attention_first_new: float32 [2363904], P(('dp', 'tok'))
- attention_second_new: float32 [2363904], P(('dp', 'tok'))
- feedforward_new: float32 [4723968], P(('dp', 'tok'))
- feedforward_first_new: float32 [4723968], P(('dp', 'tok'))
- feedforward_second_new: float32 [4723968], P(('dp', 'tok'))
- mixing_new: float32 [25], replicated
- mixing_first_new: float32 [25], replicated
- mixing_second_new: float32 [25], replicated
The draws below stay inside these ranges and needn't reach their ends.
Inputs may be any that keep to these rules, and one draw needn't show every extreme that they name: `document_lengths`: in each row the first 7 entries are document lengths in order and the last is the padding at the row's end; a row's entries sum to 1024, and its largest is exactly 512.
All inputs are finite; a program needn't handle non-finite values.
Results may differ from the reference program's by a relative error of at most 0.008.
The reference program's roundings to bfloat16 on the way count: a program that leaves them out, or rounds other values in their place, can miss the bound.
Values may be sent and summed in bfloat16 or wider, within the bound.
A program may use at most 384 MiB of HBM per device.

```python
import math
import jax
import jax.numpy as jnp
import numpy as np
from jax import lax

D = 768
HEADS = 12
HEAD_DIM = 64
FF = 3072
LEN = 1024
DOCS = 7
HIST = 24
TERMS = 25
ROWS = 32
TOKENS = 32768
NATT = 2363904
NMLP = 4723968


def rough_values(seed_key, entry_count, scale_value):
    return jax.random.normal(seed_key, (entry_count,), jnp.float32) * scale_value


def draw_cotangent(key, part):
    seed_keys = jax.random.split(jax.random.fold_in(key, 37), 2)
    fresh = jnp.clip(jax.random.normal(seed_keys[0], (ROWS, LEN, D), jnp.float32), -6.0, 6.0)
    shared = jnp.clip(jax.random.normal(seed_keys[1], (D,), jnp.float32), -4.0, 4.0) * 0.1
    return (fresh + shared[None, None, :]).astype(jnp.bfloat16)


def draw_attention_params(key, part):
    seed_keys = jax.random.split(jax.random.fold_in(key, 11), 6)
    return jnp.concatenate([jnp.exp(rough_values(seed_keys[0], D, 0.3)), rough_values(seed_keys[1], D, 0.3), rough_values(seed_keys[2], 3 * D * D, D ** (-0.5)), rough_values(seed_keys[3], 3 * D, 0.3), rough_values(seed_keys[4], D * D, 4.0 * D ** (-0.5)), rough_values(seed_keys[5], D, 0.3)])


def draw_feedforward_params(key, part):
    seed_keys = jax.random.split(jax.random.fold_in(key, 23), 6)
    return jnp.concatenate([jnp.exp(rough_values(seed_keys[0], D, 0.3)), rough_values(seed_keys[1], D, 0.3), rough_values(seed_keys[2], D * FF, D ** (-0.5)), rough_values(seed_keys[3], FF, 0.3), rough_values(seed_keys[4], FF * D, 1.5 * FF ** (-0.5)), rough_values(seed_keys[5], D, 0.3)])


def block_levels(key, shape, cuts, least, high):
    def one(dim, parts):
        heights = jax.random.uniform(jax.random.fold_in(jax.random.fold_in(key, 6), dim), (parts,), jnp.float32, least / len(cuts), high / len(cuts))
        return jnp.repeat(jnp.exp(heights), shape[dim] // parts).reshape((-1,) + (1,) * (len(shape) - dim - 1))

    factor_of = one(*cuts[0])
    for cut in cuts[1:]:
        factor_of = factor_of * one(*cut)
    return factor_of


def profile(number_of, total, reach, skew):
    loads = [(1 << 20) // math.isqrt(standing ** skew) + 1 for standing in range(2, number_of + 1)]
    spare, given = total - reach - (number_of - 1), [1] * (number_of - 1)
    while spare > 0:
        candidates = [i for i in range(number_of - 1) if given[i] < reach]
        whole, remaining = sum([loads[i] for i in candidates]), spare
        for i in candidates:
            addition = min(reach - given[i], max(1, remaining * loads[i] // whole), spare)
            given[i] = given[i] + addition
            spare = spare - addition
    return np.array([reach] + given)


def ragged_sizes(key, amount, total, reach, lean):
    if amount == 2:
        one = jax.random.randint(key, (), max(1, total - reach), min(reach, total - 1) + 1)
        return jnp.stack([one, total - one])
    tallies = jnp.asarray(profile(amount, total, reach, lean), jnp.int32)
    twos = (amount - 1) // 2
    giver, taker = tallies[1:1 + 2 * twos:2], tallies[2:2 + 2 * twos:2]
    room = jnp.minimum(giver - 1, reach - taker)
    shifted = jax.random.randint(jax.random.fold_in(key, 1), (twos,), 0, 1 << 20) % (room + 1)
    tallies = tallies.at[1:1 + 2 * twos:2].set(giver - shifted).at[2:2 + 2 * twos:2].set(taker + shifted)
    return tallies[jax.random.permutation(jax.random.fold_in(key, 2), amount)]


def noise(key, shape, deviation, limit, cuts=(), kind=jnp.bfloat16):
    loudness = block_levels(key, shape, cuts, -0.22, 0.18) if cuts else 1.0
    values = jax.random.normal(key, shape, jnp.float32) * deviation * loudness
    return jnp.minimum(jnp.maximum(values, -limit), limit).astype(kind)


def setup_inputs(seed: int = 0) -> dict:
    key_of = jax.random.split(jax.random.key(seed), 15)
    return {
        "inputs": noise(key_of[0], (ROWS, LEN, D), 1.0, 6.0, ((0, 8), (1, 4))),
        "history": noise(key_of[1], (HIST, ROWS, LEN, D), 1.0, 6.0, ((1, 8), (2, 4))),
        "document_lengths": jax.vmap(lambda own: ragged_sizes(own, DOCS + 1, LEN, LEN // 2, 2))(jax.random.split(key_of[2], ROWS)).reshape((ROWS, DOCS + 1)).astype(jnp.int32),
        "cotangent": draw_cotangent(jax.random.fold_in(key_of[14], 71), 0),
        "attention_params": draw_attention_params(jax.random.fold_in(key_of[14], 71), 0),
        "attention_first": noise(key_of[5], (NATT,), ((ROWS * LEN) ** -0.5), 0.078125, ((0, 32),), jnp.float32),
        "attention_second": jnp.clip(jnp.exp(math.log(0.00030517578) - 4.6051702 * jax.random.uniform(key_of[6], (NATT,), jnp.float32) ** block_levels(key_of[6], (NATT,), ((0, 32),), -0.2, 0.2)), 3.051757857974735e-06, 0.00030517578),
        "feedforward_params": draw_feedforward_params(jax.random.fold_in(key_of[14], 71), 0),
        "feedforward_first": noise(key_of[8], (NMLP,), ((ROWS * LEN) ** -0.5), 0.078125, ((0, 32),), jnp.float32),
        "feedforward_second": jnp.clip(jnp.exp(math.log(0.00030517578) - 4.6051702 * jax.random.uniform(key_of[9], (NMLP,), jnp.float32) ** block_levels(key_of[9], (NMLP,), ((0, 32),), -0.2, 0.2)), 3.051757857974735e-06, 0.00030517578),
        "mixing_offsets": jnp.clip(jax.random.uniform(key_of[10], (TERMS,), jnp.float32, -0.5, 0.5), -0.5, 0.5),
        "mixing_first": noise(key_of[11], (TERMS,), (30 * (ROWS * LEN) ** -0.5), 2.5, (), jnp.float32),
        "mixing_second": jnp.clip(jnp.exp(jax.random.uniform(key_of[12], (TERMS,), jnp.float32, math.log(0.0030517578), math.log(0.30517578))), 0.0030517578, 0.30517578),
        "step_count": jax.random.randint(key_of[13], (1,), 1, 6).astype(jnp.int32),
    }


@jax.custom_vjp
def low(v):
    return lax.optimization_barrier(v.astype(jnp.bfloat16)).astype(jnp.float32)

@jax.custom_vjp
def low_back(v):
    return v

def low_keep(v):
    return (low(v), None)

def low_pass(kept, grad):
    return (grad,)

def back_keep(v):
    return (v, None)

def back_low(kept, grad):
    return (low(grad),)
low.defvjp(low_keep, low_pass)
low_back.defvjp(back_keep, back_low)
beta_first = 0.9
beta_second = 0.95
learning_rate = 0.05
decay_rate = 0.1
adam_epsilon = 1e-08
norm_epsilon = 1e-05
masked_score = -1e+30

def layer_norm(values, gain, shift):
    centered = values - lax.optimization_barrier(jnp.mean(values, axis=-1, keepdims=True))
    variance = lax.optimization_barrier(jnp.mean(centered * centered, axis=-1, keepdims=True))
    return centered * lax.rsqrt(variance + norm_epsilon) * gain + shift

def rotate(values, position):
    half_dim = values.shape[-1] // 2
    frequency = jnp.exp(jnp.arange(half_dim, dtype=jnp.float32) * (-2.0 * math.log(10000.0) / values.shape[-1]))
    angle = position.astype(jnp.float32)[..., None] * frequency
    cosine = jnp.cos(angle)[..., None, :]
    sine = jnp.sin(angle)[..., None, :]
    first_half = values[..., :half_dim]
    second_half = values[..., half_dim:]
    return jnp.concatenate([first_half * cosine - second_half * sine, second_half * cosine + first_half * sine], axis=-1)

def layout(lengths_rows, places):
    ends = jnp.cumsum(lengths_rows, axis=1).astype(jnp.int32)
    starts = ends - lengths_rows
    doc_count = lengths_rows.shape[1] - 1
    inside = places[None, :, None] >= ends[:, None, :doc_count]
    segment = lax.optimization_barrier(jnp.sum(inside.astype(jnp.int32), axis=2)).astype(jnp.int32)
    labels = jnp.arange(doc_count + 1, dtype=jnp.int32)
    chosen = segment[:, :, None] == labels[None, None, :]
    begin = lax.optimization_barrier(jnp.sum(jnp.where(chosen, starts[:, None, :], 0), axis=2)).astype(jnp.int32)
    return (segment, places[None, :] - begin)

def allowed_mask(segment_row, first_row, query_count):
    query_place = first_row + jnp.arange(query_count, dtype=jnp.int32)
    key_place = jnp.arange(segment_row.shape[0], dtype=jnp.int32)
    query_segment = lax.dynamic_slice_in_dim(segment_row, first_row, query_count, 0)
    earlier = key_place[None, :] <= query_place[:, None]
    same_doc = segment_row[None, :] == query_segment[:, None]
    real_key = (segment_row[None, :] < DOCS) | (key_place[None, :] == query_place[:, None])
    return earlier & same_doc & real_key

def attention_shapes():
    return [(D,), (D,), (D, 3 * D), (3 * D,), (D, D), (D,)]

def feedforward_shapes():
    return [(D,), (D,), (D, FF), (FF,), (FF, D), (D,)]

def unpack(flat_vector, shape_list):
    pieces = []
    offset_at = 0
    for piece_shape in shape_list:
        piece_size = math.prod(piece_shape)
        pieces.append(flat_vector[offset_at:offset_at + piece_size].reshape(piece_shape))
        offset_at = offset_at + piece_size
    return pieces

def decay_mask(places, shape_list):
    mask_values = jnp.zeros(places.shape, jnp.float32)
    offset_at = 0
    for piece_shape in shape_list:
        piece_size = math.prod(piece_shape)
        if len(piece_shape) == 2:
            inside = (places >= offset_at) & (places < offset_at + piece_size)
            mask_values = mask_values + inside.astype(jnp.float32)
        offset_at = offset_at + piece_size
    return mask_values * decay_rate

def adam_update(values, gradient, moment_one, moment_two, step_number, decay_values):
    first_new = beta_first * moment_one + (1.0 - beta_first) * gradient
    second_new = beta_second * moment_two + (1.0 - beta_second) * gradient * gradient
    power_now = step_number.astype(jnp.float32)
    fix_one = 1.0 - jnp.power(beta_first, power_now)
    fix_two = 1.0 - jnp.power(beta_second, power_now)
    step_size = first_new / fix_one / (jnp.sqrt(second_new / fix_two) + adam_epsilon)
    return (values - learning_rate * (step_size + decay_values * values), first_new, second_new)

def block(rows_in, rows_lengths, attention_parts, feedforward_parts):
    gain_one, shift_one, w_qkv, b_qkv, w_out, b_out = attention_parts
    gain_two, shift_two, w_up, b_up, w_down, b_down = feedforward_parts
    highest = lax.Precision.HIGHEST
    group_rows = rows_in.shape[0]
    segment, position = layout(rows_lengths, jnp.arange(LEN, dtype=jnp.int32))
    normed_one = low(layer_norm(rows_in, gain_one, shift_one))
    project = low_back(jnp.einsum('gtd,de->gte', normed_one, w_qkv, precision=highest) + b_qkv)
    project = project.reshape(group_rows, LEN, 3, HEADS, HEAD_DIM)
    queries = low(low_back(rotate(project[:, :, 0], position)))
    keys_all = low(low_back(rotate(project[:, :, 1], position)))
    values_all = low(low_back(project[:, :, 2]))
    scores = low_back(jnp.einsum('gqhd,gkhd->ghqk', queries, keys_all, precision=highest) * HEAD_DIM ** (-0.5))
    allowed = jax.vmap(lambda segment_row: allowed_mask(segment_row, 0, LEN))(segment)
    masked = jnp.where(allowed[:, None], scores, masked_score)
    top_score = lax.optimization_barrier(jnp.max(masked, axis=3, keepdims=True))
    exponent = jnp.exp(masked - top_score)
    soft_weights = exponent / lax.optimization_barrier(jnp.sum(exponent, axis=3, keepdims=True))
    attended = jnp.einsum('ghqk,gkhd->gqhd', low(soft_weights), values_all, precision=highest)
    attended = low(low_back(attended)).reshape(group_rows, LEN, D)
    hidden = rows_in + low_back(jnp.einsum('gtd,de->gte', attended, w_out, precision=highest) + b_out)
    normed_two = low(layer_norm(hidden, gain_two, shift_two))
    up_value = low_back(jnp.einsum('gtd,df->gtf', normed_two, w_up, precision=highest) + b_up)
    active = low(jax.nn.gelu(up_value))
    return hidden + low_back(jnp.einsum('gtf,fd->gtd', active, w_down, precision=highest) + b_down)

def reference(inputs, history, document_lengths, cotangent, attention_params, attention_first, attention_second, feedforward_params, feedforward_first, feedforward_second, mixing_offsets, mixing_first, mixing_second, step_count):

    def forward(attention_flat, feedforward_flat, offsets_now, current, earlier):
        attention_parts = unpack(low(attention_flat), attention_shapes())
        feedforward_parts = unpack(low(feedforward_flat), feedforward_shapes())

        def group_block(pieces):
            return block(pieces[0], pieces[1], attention_parts, feedforward_parts)
        outputs = lax.map(jax.checkpoint(group_block), (current.reshape(ROWS // 4, 4, LEN, D), document_lengths.reshape(ROWS // 4, 4, DOCS + 1)))
        block_out = outputs.reshape(ROWS, LEN, D)
        coefficient = offsets_now + (jnp.arange(HIST + 1) == HIST).astype(offsets_now.dtype)
        history_part = jnp.einsum('j,jrtd->rtd', coefficient[:HIST], earlier, precision=lax.Precision.HIGHEST)
        return history_part + coefficient[HIST] * block_out
    mixed, backward = jax.vjp(forward, attention_params, feedforward_params, mixing_offsets, inputs.astype(jnp.float32), history.astype(jnp.float32))
    gradients = backward(cotangent.astype(jnp.float32))
    count_now = step_count[0]
    attention_places = jnp.arange(NATT, dtype=jnp.int32)
    feedforward_places = jnp.arange(NMLP, dtype=jnp.int32)
    attention_step = adam_update(attention_params, gradients[0] / TOKENS, attention_first, attention_second, count_now, decay_mask(attention_places, attention_shapes()))
    feedforward_step = adam_update(feedforward_params, gradients[1] / TOKENS, feedforward_first, feedforward_second, count_now, decay_mask(feedforward_places, feedforward_shapes()))
    mixing_step = adam_update(mixing_offsets, gradients[2] / TOKENS, mixing_first, mixing_second, count_now, 0.0)
    return (mixed.astype(jnp.bfloat16), gradients[3], gradients[4], attention_step[0], attention_step[1], attention_step[2], feedforward_step[0], feedforward_step[1], feedforward_step[2], mixing_step[0], mixing_step[1], mixing_step[2])
```

```python
from functools import partial
import math

import jax
import jax.numpy as jnp
from jax import lax
from jax.experimental import pallas as pl
from jax.experimental.pallas import tpu as pltpu
from jax.sharding import PartitionSpec as P

D = 768
HEADS = 12
HEAD_DIM = 64
FF = 3072
DOCS = 7


beta_first = 0.9
beta_second = 0.95
learning_rate = 0.05
decay_rate = 0.1
adam_epsilon = 1e-08
norm_epsilon = 1e-05
masked_score = -1e30


def layer_norm(values, gain, shift):
    centered = values - jnp.mean(values, axis=-1, keepdims=True)
    variance = jnp.mean(centered * centered, axis=-1, keepdims=True)
    return centered * lax.rsqrt(variance + norm_epsilon) * gain + shift


def rotate(values, position):
    half_dim = values.shape[-1] // 2
    frequency = jnp.exp(
        jnp.arange(half_dim, dtype=jnp.float32) * (-2.0 * math.log(10000.0) / values.shape[-1])
    )
    angle = position.astype(jnp.float32)[..., None] * frequency
    cosine = jnp.cos(angle)[..., None, :]
    sine = jnp.sin(angle)[..., None, :]
    first_half = values[..., :half_dim]
    second_half = values[..., half_dim:]
    return jnp.concatenate(
        [first_half * cosine - second_half * sine, second_half * cosine + first_half * sine],
        axis=-1,
    )


def turn_back(gradient_part, position):
    return jax.vjp(partial(rotate, position=position), gradient_part)[1](gradient_part)[0]


def layout(lengths_rows, places):
    ends = jnp.cumsum(lengths_rows, axis=1)
    starts = ends - lengths_rows
    doc_count = lengths_rows.shape[1] - 1
    inside = places[None, :, None] >= ends[:, None, :doc_count]
    segment = jnp.sum(inside.astype(jnp.int32), axis=2)
    labels = jnp.arange(doc_count + 1, dtype=jnp.int32)
    chosen = segment[:, :, None] == labels[None, None, :]
    begin = jnp.sum(jnp.where(chosen, starts[:, None, :], 0), axis=2)
    return (segment, places[None, :] - begin)


def allowed_mask(segment_row, first_row, query_count):
    query_place = first_row + jnp.arange(query_count, dtype=jnp.int32)
    key_place = jnp.arange(segment_row.shape[0], dtype=jnp.int32)
    query_segment = lax.dynamic_slice_in_dim(segment_row, first_row, query_count, 0)
    earlier = key_place[None, :] <= query_place[:, None]
    same_doc = segment_row[None, :] == query_segment[:, None]
    real_key = (segment_row[None, :] < DOCS) | (key_place[None, :] == query_place[:, None])
    return earlier & same_doc & real_key


def block_scores(queries, keys_all, segment_row, first_row):
    scores = jnp.einsum(
        "qhd,khd->hqk", queries, keys_all, preferred_element_type=jnp.float32
    ) * HEAD_DIM ** (-0.5)
    allowed = allowed_mask(segment_row, first_row, queries.shape[0])
    return jnp.where(allowed[None], scores, masked_score)


def attention_shapes():
    return [(D,), (D,), (D, 3 * D), (3 * D,), (D, D), (D,)]


def feedforward_shapes():
    return [(D,), (D,), (D, FF), (FF,), (FF, D), (D,)]


def unpack(flat_vector, shape_list):
    pieces = []
    offset_at = 0
    for piece_shape in shape_list:
        piece_size = math.prod(piece_shape)
        pieces.append(flat_vector[offset_at : offset_at + piece_size].reshape(piece_shape))
        offset_at = offset_at + piece_size
    return pieces


def decay_mask(places, shape_list):
    mask_values = jnp.zeros(places.shape, jnp.float32)
    offset_at = 0
    for piece_shape in shape_list:
        piece_size = math.prod(piece_shape)
        if len(piece_shape) == 2:
            inside = (places >= offset_at) & (places < offset_at + piece_size)
            mask_values = mask_values + inside.astype(jnp.float32)
        offset_at = offset_at + piece_size
    return mask_values * decay_rate


def adam_update(values, gradient, moment_one, moment_two, step_number, decay_values):
    first_new = beta_first * moment_one + (1.0 - beta_first) * gradient
    second_new = beta_second * moment_two + (1.0 - beta_second) * gradient * gradient
    power_now = step_number.astype(jnp.float32)
    fix_one = 1.0 - jnp.power(beta_first, power_now)
    fix_two = 1.0 - jnp.power(beta_second, power_now)
    step_size = first_new / fix_one / (jnp.sqrt(second_new / fix_two) + adam_epsilon)
    return (values - learning_rate * (step_size + decay_values * values), first_new, second_new)


def to_groups(values, subsets):
    full_shape = values.shape
    row_total = full_shape[0]
    half_width = full_shape[-1] // 2
    split_view = values.reshape(
        (subsets, row_total // subsets) + full_shape[1:-1] + (2, half_width)
    )
    moved = jnp.moveaxis(split_view, -2, 0)
    return moved.reshape((2 * subsets, row_total // subsets) + full_shape[1:-1] + (half_width,))


def from_groups(values, subsets):
    full_shape = values.shape
    split_view = values.reshape((2, subsets) + full_shape[1:])
    moved = jnp.moveaxis(split_view, 0, -2)
    return moved.reshape((subsets * full_shape[1],) + full_shape[2:-1] + (2 * full_shape[-1],))


def attend_rows(head_qkv, head_segment):
    item_count = head_qkv.shape[1]
    length_all = head_qkv.shape[2]
    group_width = head_qkv.shape[4]
    head_count = group_width // HEAD_DIM
    block_rows = min(512, length_all)
    block_count = length_all // block_rows
    rows_qkv = head_qkv.reshape(item_count, length_all, 3, head_count, HEAD_DIM)
    rows_segment = head_segment.reshape(item_count, length_all)

    def attend_one_block(block_index):
        row_index = block_index // block_count
        first_row = block_index % block_count * block_rows
        current = rows_qkv[row_index]
        queries = lax.dynamic_slice_in_dim(current[:, 0], first_row, block_rows, 0)
        masked = block_scores(queries, current[:, 1], rows_segment[row_index], first_row)
        top_score = jnp.max(masked, axis=2, keepdims=True)
        exponent = jnp.exp(masked - top_score)
        total_weight = jnp.sum(exponent, axis=2, keepdims=True)
        soft_weights = (exponent / total_weight).astype(jnp.bfloat16)
        attended = jnp.einsum(
            "hqk,khd->qhd", soft_weights, current[:, 2], preferred_element_type=jnp.float32
        )
        log_total = (top_score + jnp.log(total_weight))[:, :, 0]
        return (attended.reshape(block_rows, group_width).astype(jnp.bfloat16), log_total)

    outputs, log_totals = lax.map(
        attend_one_block, jnp.arange(item_count * block_count, dtype=jnp.int32)
    )
    return (
        outputs.reshape(1, item_count, length_all, group_width),
        log_totals.reshape(1, item_count, block_count, head_count, block_rows),
    )


def attend_back(head_qkv, head_segment, log_totals, head_grads):
    item_count = head_qkv.shape[1]
    length_all = head_qkv.shape[2]
    group_width = head_qkv.shape[4]
    head_count = group_width // HEAD_DIM
    block_rows = min(512, length_all)
    block_count = length_all // block_rows
    scale_value = HEAD_DIM ** (-0.5)

    def one_row(pieces):
        current, segment_row, log_row, grad_row = pieces
        keys_all = current[:, 1]
        values_all = current[:, 2]

        def one_one_block(carried, block_index):
            first_row = block_index * block_rows
            queries = lax.dynamic_slice_in_dim(current[:, 0], first_row, block_rows, 0)
            grad_block = lax.dynamic_slice_in_dim(grad_row, first_row, block_rows, 0)
            masked = block_scores(queries, keys_all, segment_row, first_row)
            soft_weights = jnp.exp(masked - log_row[block_index][:, :, None])
            grad_weights = jnp.einsum(
                "qhd,khd->hqk", grad_block, values_all, preferred_element_type=jnp.float32
            )
            inner_sum = jnp.sum(soft_weights * grad_weights, axis=2, keepdims=True)
            grad_scores = (soft_weights * (grad_weights - inner_sum)).astype(jnp.bfloat16)
            grad_query = (
                jnp.einsum(
                    "hqk,khd->qhd", grad_scores, keys_all, preferred_element_type=jnp.float32
                )
                * scale_value
            )
            grad_key = (
                carried[0]
                + jnp.einsum(
                    "hqk,qhd->khd", grad_scores, queries, preferred_element_type=jnp.float32
                )
                * scale_value
            )
            grad_value = carried[1] + jnp.einsum(
                "hqk,qhd->khd",
                soft_weights.astype(jnp.bfloat16),
                grad_block,
                preferred_element_type=jnp.float32,
            )
            return ((grad_key, grad_value), grad_query)

        empty_grad = jnp.zeros((length_all, head_count, HEAD_DIM), jnp.float32)
        (grad_key, grad_value), grad_query = lax.scan(
            one_one_block, (empty_grad, empty_grad), jnp.arange(block_count, dtype=jnp.int32)
        )
        grad_query = grad_query.reshape(length_all, head_count, HEAD_DIM)
        return jnp.stack([grad_query, grad_key, grad_value], axis=1).astype(jnp.bfloat16)

    row_grads = lax.map(
        one_row,
        (
            head_qkv.reshape(item_count, length_all, 3, head_count, HEAD_DIM),
            head_segment.reshape(item_count, length_all),
            log_totals.reshape(item_count, block_count, head_count, block_rows),
            head_grads.reshape(item_count, length_all, head_count, HEAD_DIM),
        ),
    )
    return row_grads.reshape(1, item_count, length_all, 3, group_width)


def general_shards(
    inputs,
    history,
    document_lengths,
    cotangent,
    attention_params,
    attention_first,
    attention_second,
    feedforward_params,
    feedforward_first,
    feedforward_second,
    mixing_offsets,
    mixing_first,
    mixing_second,
    step_count,
):
    row_count, token_span, model_width = inputs.shape
    subsets = lax.axis_size("tok") // 2
    per_device = row_count // subsets
    tokens_all = row_count * token_span * lax.axis_size("dp") * lax.axis_size("tok")
    attention_flat, feedforward_flat = (
        lax.all_gather(attention_params.astype(jnp.bfloat16), ("dp", "tok"), axis=0, tiled=True),
        lax.all_gather(feedforward_params.astype(jnp.bfloat16), ("dp", "tok"), axis=0, tiled=True),
    )
    gain_one, shift_one, w_qkv, b_qkv, w_out, b_out = unpack(attention_flat, attention_shapes())
    gain_two, shift_two, w_up, b_up, w_down, b_down = unpack(feedforward_flat, feedforward_shapes())
    gain_one = gain_one.astype(jnp.float32)
    shift_one = shift_one.astype(jnp.float32)
    gain_two = gain_two.astype(jnp.float32)
    shift_two = shift_two.astype(jnp.float32)
    places = lax.axis_index("tok") * token_span + jnp.arange(token_span, dtype=jnp.int32)
    segment, position = layout(document_lengths, places)
    current = inputs.astype(jnp.float32)
    normed_one = layer_norm(current, gain_one, shift_one).astype(jnp.bfloat16)
    project = jnp.dot(normed_one, w_qkv, preferred_element_type=jnp.float32) + b_qkv.astype(
        jnp.float32
    )
    project = project.reshape(row_count, token_span, 3, HEADS, HEAD_DIM)
    queries = rotate(project[:, :, 0], position)
    keys_all = rotate(project[:, :, 1], position)
    packed = jnp.stack([queries, keys_all, project[:, :, 2]], axis=2).astype(jnp.bfloat16)
    send_qkv = to_groups(packed.reshape(row_count, token_span, 3, model_width), subsets)
    send_segment = jnp.broadcast_to(
        segment.reshape(1, subsets, per_device, token_span), (2, subsets, per_device, token_span)
    ).reshape(2 * subsets, per_device, token_span)
    head_qkv = lax.all_to_all(send_qkv, "tok", split_axis=0, concat_axis=2, tiled=True)
    head_segment = lax.all_to_all(send_segment, "tok", split_axis=0, concat_axis=2, tiled=True)
    outputs, log_totals = attend_rows(head_qkv, head_segment)
    returned = lax.all_to_all(outputs, "tok", split_axis=2, concat_axis=0, tiled=True)
    returned, head_qkv, head_segment, log_totals = (returned, head_qkv, head_segment, log_totals)
    attended = from_groups(returned, subsets)
    hidden = (
        current
        + jnp.dot(attended, w_out, preferred_element_type=jnp.float32)
        + b_out.astype(jnp.float32)
    )
    normed_two = layer_norm(hidden, gain_two, shift_two).astype(jnp.bfloat16)
    up_value = jnp.dot(normed_two, w_up, preferred_element_type=jnp.float32) + b_up.astype(
        jnp.float32
    )
    active = jax.nn.gelu(up_value).astype(jnp.bfloat16)
    block_out = (
        hidden
        + jnp.dot(active, w_down, preferred_element_type=jnp.float32)
        + b_down.astype(jnp.float32)
    )
    term_count = mixing_offsets.shape[0]
    coefficient = mixing_offsets + (jnp.arange(term_count) == term_count - 1).astype(jnp.float32)
    history_part = jnp.einsum(
        "j,jrtd->rtd", coefficient[:-1], history, preferred_element_type=jnp.float32
    )
    mixed = (history_part + coefficient[-1] * block_out).astype(jnp.bfloat16)
    grad_mixed = cotangent.astype(jnp.float32)
    grad_history = coefficient[:-1, None, None, None] * grad_mixed[None]
    history_terms = jnp.einsum(
        "jrtd,rtd->j", history, grad_mixed, preferred_element_type=jnp.float32
    )
    mixing_terms = jnp.concatenate([history_terms, jnp.sum(block_out * grad_mixed)[None]])
    mixing_grad = lax.psum(mixing_terms, ("dp", "tok")) / tokens_all
    grad_block = coefficient[-1] * grad_mixed
    grad_branch = grad_block.astype(jnp.bfloat16)
    grad_w_down = jnp.einsum("rtf,rtd->fd", active, grad_branch, preferred_element_type=jnp.float32)
    grad_b_down = jnp.sum(grad_branch.astype(jnp.float32), axis=(0, 1))
    grad_active = jnp.einsum("rtd,fd->rtf", grad_branch, w_down, preferred_element_type=jnp.float32)
    grad_up = jax.vjp(jax.nn.gelu, up_value)[1](grad_active)[0].astype(jnp.bfloat16)
    grad_w_up = jnp.einsum("rtd,rtf->df", normed_two, grad_up, preferred_element_type=jnp.float32)
    grad_b_up = jnp.sum(grad_up.astype(jnp.float32), axis=(0, 1))
    grad_normed_two = jnp.einsum("rtf,df->rtd", grad_up, w_up, preferred_element_type=jnp.float32)
    grad_hidden_norm, grad_gain_two, grad_shift_two = jax.vjp(
        layer_norm, hidden, gain_two, shift_two
    )[1](grad_normed_two)
    grad_hidden = grad_block + grad_hidden_norm
    feedforward_grad = jnp.concatenate(
        [
            grad_gain_two,
            grad_shift_two,
            grad_w_up.reshape(-1),
            grad_b_up,
            grad_w_down.reshape(-1),
            grad_b_down,
        ]
    )
    feedforward_share = lax.psum_scatter(
        feedforward_grad, ("dp", "tok"), scatter_dimension=0, tiled=True
    )
    grad_attn = grad_hidden.astype(jnp.bfloat16)
    grad_w_out = jnp.einsum("rtd,rte->de", attended, grad_attn, preferred_element_type=jnp.float32)
    grad_b_out = jnp.sum(grad_attn.astype(jnp.float32), axis=(0, 1))
    grad_attended = jnp.einsum(
        "rte,de->rtd", grad_attn, w_out, preferred_element_type=jnp.float32
    ).astype(jnp.bfloat16)
    head_grads = lax.all_to_all(
        to_groups(grad_attended, subsets), "tok", split_axis=0, concat_axis=2, tiled=True
    )
    head_back = attend_back(head_qkv, head_segment, log_totals, head_grads)
    token_back = from_groups(
        lax.all_to_all(head_back, "tok", split_axis=2, concat_axis=0, tiled=True), subsets
    )
    token_back = token_back.astype(jnp.float32).reshape(row_count, token_span, 3, HEADS, HEAD_DIM)
    grad_project = jnp.stack(
        [
            turn_back(token_back[:, :, 0], position),
            turn_back(token_back[:, :, 1], position),
            token_back[:, :, 2],
        ],
        axis=2,
    )
    grad_project = grad_project.reshape(row_count, token_span, 3 * model_width).astype(jnp.bfloat16)
    grad_w_qkv = jnp.einsum(
        "rtd,rte->de", normed_one, grad_project, preferred_element_type=jnp.float32
    )
    grad_b_qkv = jnp.sum(grad_project.astype(jnp.float32), axis=(0, 1))
    grad_normed_one = jnp.einsum(
        "rte,de->rtd", grad_project, w_qkv, preferred_element_type=jnp.float32
    )
    grad_current, grad_gain_one, grad_shift_one = jax.vjp(layer_norm, current, gain_one, shift_one)[
        1
    ](grad_normed_one)
    grad_inputs = grad_hidden + grad_current
    attention_grad = jnp.concatenate(
        [
            grad_gain_one,
            grad_shift_one,
            grad_w_qkv.reshape(-1),
            grad_b_qkv,
            grad_w_out.reshape(-1),
            grad_b_out,
        ]
    )
    attention_share = lax.psum_scatter(
        attention_grad, ("dp", "tok"), scatter_dimension=0, tiled=True
    )
    count_now = step_count[0]
    shard_index = lax.axis_index(("dp", "tok"))
    attention_places = shard_index * attention_params.shape[0] + jnp.arange(
        attention_params.shape[0], dtype=jnp.int32
    )
    feedforward_places = shard_index * feedforward_params.shape[0] + jnp.arange(
        feedforward_params.shape[0], dtype=jnp.int32
    )
    attention_step = adam_update(
        attention_params,
        attention_share / tokens_all,
        attention_first,
        attention_second,
        count_now,
        decay_mask(attention_places, attention_shapes()),
    )
    feedforward_step = adam_update(
        feedforward_params,
        feedforward_share / tokens_all,
        feedforward_first,
        feedforward_second,
        count_now,
        decay_mask(feedforward_places, feedforward_shapes()),
    )
    mixing_step = adam_update(
        mixing_offsets, mixing_grad, mixing_first, mixing_second, count_now, 0.0
    )
    return (
        mixed,
        grad_inputs,
        grad_history,
        attention_step[0],
        attention_step[1],
        attention_step[2],
        feedforward_step[0],
        feedforward_step[1],
        feedforward_step[2],
        mixing_step[0],
        mixing_step[1],
        mixing_step[2],
    )


VMEM_LIMIT = 58 * 1024 * 1024
BF = jnp.bfloat16
F32 = jnp.float32


def cols(ref, first, count):
    lead = math.prod(ref.shape[:-3]) * ref.shape[-2]
    pieces = []
    for at in range(first, first + count):
        index = (slice(None),) * (len(ref.shape) - 3) + (at,)
        pieces.append(ref[index].reshape(lead, 128))
    return pieces[0] if count == 1 else jnp.concatenate(pieces, axis=1)


def put_tiles(ref, row_at, col_at, value):
    rows, width = value.shape
    for at in range(width // 128):
        ref[pl.ds(row_at, rows // 16), col_at + at] = value[:, 128 * at : 128 * at + 128].reshape(
            rows // 16, 16, 128
        )


def norm_parts(values):
    mean = jnp.mean(values, axis=1, keepdims=True)
    centered = values - mean
    inverse = lax.rsqrt(jnp.mean(centered * centered, axis=1, keepdims=True) + norm_epsilon)
    return centered, inverse


def nt_dot(left, right):
    return lax.dot_general(left, right, (((1,), (1,)), ((), ())), preferred_element_type=F32)


def nn_dot(left, right):
    return lax.dot_general(left, right, (((1,), (0,)), ((), ())), preferred_element_type=F32)


def swap_halves(values):
    width = values.shape[1]
    lane = lax.broadcasted_iota(jnp.int32, values.shape, 1)
    return jnp.where(
        lane % HEAD_DIM < HEAD_DIM // 2,
        pltpu.roll(values, width - HEAD_DIM // 2, 1),
        pltpu.roll(values, HEAD_DIM // 2, 1),
    )


def project_kernel(x_ref, w_ref, vec_ref, cos_ref, sin_ref, n1_ref, q_ref, k_ref, v_ref):
    width = x_ref.shape[1]
    centered, inverse = norm_parts(x_ref[...].astype(F32))
    normed = (centered * inverse * vec_ref[0:1, :width] + vec_ref[1:2, :width]).astype(BF)
    n1_ref[...] = normed
    cosine = jnp.concatenate([cos_ref[...]] * 2, axis=1)
    sine = jnp.concatenate([sin_ref[...]] * 2, axis=1)
    per_part = width // 256
    for at in range(3 * per_part):
        part = nn_dot(normed, cols(w_ref, 2 * at, 2)) + vec_ref[2:3, 256 * at : 256 * at + 256]
        spot = slice(256 * (at % per_part), 256 * (at % per_part) + 256)
        if at < 2 * per_part:
            part = part * cosine + swap_halves(part) * sine
        if at < per_part:
            q_ref[:, spot] = (part * HEAD_DIM ** (-0.5)).astype(BF)
        elif at < 2 * per_part:
            k_ref[:, spot] = part.astype(BF)
        else:
            v_ref[:, spot] = part.astype(BF)


def project(x_row, w_qkv, vectors, cosine, sine):
    length, width = x_row.shape
    tile = 256
    whole = pl.BlockSpec(w_qkv.shape, lambda i: (0,) * w_qkv.ndim)
    rows = pl.BlockSpec((tile, width), lambda i: (i, 0))
    trig = pl.BlockSpec((tile, 128), lambda i: (i, 0))
    out = jax.ShapeDtypeStruct((length, width), BF)
    return pl.pallas_call(
        project_kernel,
        grid=(length // tile,),
        in_specs=[rows, whole, pl.BlockSpec(vectors.shape, lambda i: (0, 0)), trig, trig],
        out_specs=[rows] * 4,
        out_shape=[out] * 4,
        compiler_params=pltpu.CompilerParams(vmem_limit_bytes=VMEM_LIMIT),
        name="project",
    )(x_row, w_qkv, vectors, cosine, sine)


def key_range(block, block_rows, reach):
    return max(0, block * block_rows - reach), (block + 1) * block_rows


def fill_bias(bias_ref, seg_col_ref, seg_row_ref, block_rows, reach):
    length = seg_row_ref.shape[1]
    at = 0
    for block in range(length // block_rows):
        low, high = key_range(block, block_rows, reach)
        shape = (high - low, block_rows)
        key_place = low + lax.broadcasted_iota(jnp.int32, shape, 0)
        query_place = block * block_rows + lax.broadcasted_iota(jnp.int32, shape, 1)
        key_seg = seg_col_ref[low:high, :]
        query_seg = seg_row_ref[:, block * block_rows : (block + 1) * block_rows]
        allowed = (key_place <= query_place) & (key_seg == query_seg)
        allowed = allowed & ((key_seg < DOCS) | (key_place == query_place))
        bias_ref[at : at + high - low, :] = jnp.where(allowed, 0.0, masked_score)
        at = at + high - low


def bias_rows(length, block_rows, reach):
    return sum(
        high - low
        for low, high in (key_range(b, block_rows, reach) for b in range(length // block_rows))
    )


def head_mask(values, head):
    lane = lax.broadcasted_iota(jnp.int32, values.shape, 1)
    keep = lane < HEAD_DIM if head == 0 else lane >= HEAD_DIM
    return jnp.where(keep, values, jnp.zeros_like(values))


def attend_kernel(block_rows, reach, q_ref, k_ref, v_ref, sc_ref, sr_ref, o_ref, lse_ref, bias_ref):
    length = q_ref.shape[0]

    @pl.when(pl.program_id(0) == 0)
    def _():
        fill_bias(bias_ref, sc_ref, sr_ref, block_rows, reach)

    keys = k_ref[...]
    key_heads = [head_mask(keys, 0), head_mask(keys, 1)]
    value_turned = v_ref[...].T
    at = 0
    for block in range(length // block_rows):
        low, high = key_range(block, block_rows, reach)
        spot = slice(block * block_rows, (block + 1) * block_rows)
        queries = q_ref[spot, :]
        bias = bias_ref[at : at + high - low, :]
        at = at + high - low
        halves = []
        for head in range(2):
            scores = nt_dot(key_heads[head][low:high], queries) + bias
            top = jnp.max(scores, axis=0, keepdims=True)
            exponent = jnp.exp(scores - top)
            total = jnp.sum(exponent, axis=0, keepdims=True)
            probs = (exponent * (1.0 / total)).astype(BF)
            lse_ref[0, head : head + 1, spot] = top + jnp.log(total)
            turned = value_turned[HEAD_DIM * head : HEAD_DIM * head + HEAD_DIM, low:high]
            halves.append(nn_dot(turned, probs))
        o_ref[spot, :] = jnp.concatenate(halves, axis=0).T.astype(BF)


def row_attend(queries, keys, values, seg_col, seg_row, reach):
    length, width = queries.shape
    block_rows = 256
    pairs = width // 128
    pair = pl.BlockSpec((length, 128), lambda p: (0, p))
    return pl.pallas_call(
        partial(attend_kernel, block_rows, reach),
        grid=(pairs,),
        in_specs=[
            pair,
            pair,
            pair,
            pl.BlockSpec(seg_col.shape, lambda p: (0, 0)),
            pl.BlockSpec(seg_row.shape, lambda p: (0, 0)),
        ],
        out_specs=[pair, pl.BlockSpec((1, 2, length), lambda p: (p, 0, 0))],
        out_shape=[
            jax.ShapeDtypeStruct((length, width), BF),
            jax.ShapeDtypeStruct((pairs, 2, length), F32),
        ],
        scratch_shapes=[pltpu.VMEM((bias_rows(length, block_rows, reach), block_rows), F32)],
        compiler_params=pltpu.CompilerParams(vmem_limit_bytes=VMEM_LIMIT),
        name="attend",
    )(queries, keys, values, seg_col, seg_row)


def attend_back_kernel(
    block_rows, reach, q_ref, k_ref, v_ref, g_ref, lse_ref, sc_ref, sr_ref, cos_ref, sin_ref,
    gq_ref, gk_ref, gv_ref, bias_ref, dq_acc, dk_acc, dv_acc,
):
    length = q_ref.shape[0]

    @pl.when(pl.program_id(0) == 0)
    def _():
        fill_bias(bias_ref, sc_ref, sr_ref, block_rows, reach)

    keys = k_ref[...]
    key_heads = [head_mask(keys, 0), head_mask(keys, 1)]
    key_turned = keys.T
    vals = v_ref[...]
    value_heads = [head_mask(vals, 0), head_mask(vals, 1)]
    dk_acc[...] = jnp.zeros_like(dk_acc)
    dv_acc[...] = jnp.zeros_like(dv_acc)
    at = 0
    for block in range(length // block_rows):
        low, high = key_range(block, block_rows, reach)
        spot = slice(block * block_rows, (block + 1) * block_rows)
        queries = q_ref[spot, :]
        grads = g_ref[spot, :]
        bias = bias_ref[at : at + high - low, :]
        at = at + high - low
        halves = []
        for head in range(2):
            scores = nt_dot(key_heads[head][low:high], queries) + bias
            probs = jnp.exp(scores - lse_ref[0, head : head + 1, spot])
            dprobs = nt_dot(value_heads[head][low:high], grads)
            inner = jnp.sum(probs * dprobs, axis=0, keepdims=True)
            dscores = (probs * (dprobs - inner)).astype(BF)
            turned = key_turned[HEAD_DIM * head : HEAD_DIM * head + HEAD_DIM, low:high]
            halves.append(nn_dot(turned, dscores))
            dk_acc[low:high, :] += nn_dot(dscores, head_mask(queries, head))
            dv_acc[low:high, :] += nn_dot(probs.astype(BF), head_mask(grads, head))
        dq_acc[spot, :] = jnp.concatenate(halves, axis=0).T * HEAD_DIM ** (-0.5)
    cosine = cos_ref[...]
    sine = sin_ref[...]
    grad_query = dq_acc[...].astype(BF).astype(F32)
    grad_key = dk_acc[...].astype(BF).astype(F32)
    gq_ref[...] = (grad_query * cosine - swap_halves(grad_query) * sine).astype(BF)
    gk_ref[...] = (grad_key * cosine - swap_halves(grad_key) * sine).astype(BF)
    gv_ref[...] = dv_acc[...].astype(BF)


def row_attend_back(queries, keys, values, grads, lse, seg_col, seg_row, cosine, sine, reach):
    length, width = queries.shape
    block_rows = 256
    pair = pl.BlockSpec((length, 128), lambda p: (0, p))
    trig = pl.BlockSpec((length, 128), lambda p: (0, 0))
    out = jax.ShapeDtypeStruct((length, width), BF)
    return pl.pallas_call(
        partial(attend_back_kernel, block_rows, reach),
        grid=(width // 128,),
        in_specs=[
            pair, pair, pair, pair,
            pl.BlockSpec((1, 2, length), lambda p: (p, 0, 0)),
            pl.BlockSpec(seg_col.shape, lambda p: (0, 0)),
            pl.BlockSpec(seg_row.shape, lambda p: (0, 0)),
            trig, trig,
        ],
        out_specs=[pair] * 3,
        out_shape=[out] * 3,
        scratch_shapes=[pltpu.VMEM((bias_rows(length, block_rows, reach), block_rows), F32)]
        + [pltpu.VMEM((length, 128), F32)] * 3,
        compiler_params=pltpu.CompilerParams(vmem_limit_bytes=VMEM_LIMIT),
        name="attend_back",
    )(queries, keys, values, grads, lse, seg_col, seg_row, cosine, sine)


gelu_root = math.sqrt(2.0 / math.pi)


def middle_kernel(
    x_ref, att_ref, cot_ref, wout_ref, wup_ref, wdown_ref, vec_ref, bup_ref, c_ref,
    bout_ref, gatt_ref, ghid_ref, gwup_ref, gwdown_ref, gwout_ref, gbup_ref, gvec_ref,
    hidden_ref, n2_ref, n2t_ref, gb_ref, acc_out, acc_gn, act_ref, gup_ref,
):
    step = pl.program_id(0)
    steps = pl.num_programs(0)
    length, width = x_ref.shape
    tile = 256
    tiles = length // tile
    mix = c_ref[0]

    @pl.when(step == 0)
    def _():
        @pl.loop(0, tiles)
        def _(t):
            rows = pl.ds(pl.multiple_of(t * tile, tile), tile)
            attended = att_ref[rows, :]
            hidden = x_ref[rows, :].astype(F32) + nn_dot(attended, cols(wout_ref, 0, width // 128))
            hidden = hidden + vec_ref[2:3, :]
            hidden_ref[rows, :] = hidden
            centered, inverse = norm_parts(hidden)
            normed = (centered * inverse * vec_ref[0:1, :] + vec_ref[1:2, :]).astype(BF)
            n2_ref[rows, :] = normed
            n2t_ref[:, rows] = normed.T
            gb_ref[rows, :] = (mix * cot_ref[rows, :].astype(F32)).astype(BF)
            acc_out[rows, :] = jnp.zeros((tile, width), F32)
            acc_gn[rows, :] = jnp.zeros((tile, width), F32)

        gvec_ref[...] = jnp.zeros_like(gvec_ref)

    w_up = cols(wup_ref, 0, 2)
    w_down = cols(wdown_ref, 0, width // 128)
    gbup_ref[...] = jnp.zeros_like(gbup_ref)

    @pl.loop(0, tiles)
    def _(t):
        rows = pl.ds(pl.multiple_of(t * tile, tile), tile)
        up = nn_dot(n2_ref[rows, :], w_up) + bup_ref[0:1, :]
        square = up * up
        turn = jnp.tanh(gelu_root * up * (1.0 + 0.044715 * square))
        half = 0.5 * (1.0 + turn)
        active = (up * half).astype(BF)
        act_ref[rows, :] = active
        acc_out[rows, :] += nn_dot(active, w_down)
        slope = half + (0.5 * gelu_root) * up * (1.0 - turn * turn) * (
            1.0 + (3.0 * 0.044715) * square
        )
        grad_up = (nt_dot(gb_ref[rows, :], w_down) * slope).astype(BF)
        gup_ref[rows, :] = grad_up
        acc_gn[rows, :] += nt_dot(grad_up, w_up)
        gbup_ref[0:1, :] += jnp.sum(grad_up.astype(F32), axis=0, keepdims=True)

    grad_up_all = gup_ref[...]
    for r in range(width // 256):
        put_tiles(
            gwup_ref, 16 * r, 0, nn_dot(n2t_ref[256 * r : 256 * r + 256, :], grad_up_all).astype(BF)
        )
    active_turned = act_ref[...].T
    for r in range(width // 256):
        put_tiles(
            gwdown_ref, 0, 2 * r, nn_dot(active_turned, gb_ref[:, 256 * r : 256 * r + 256]).astype(BF)
        )

    @pl.when(step == steps - 1)
    def _():
        @pl.loop(0, tiles)
        def _(t):
            rows = pl.ds(pl.multiple_of(t * tile, tile), tile)
            hidden = hidden_ref[rows, :]
            cot = cot_ref[rows, :].astype(F32)
            block_out = hidden + acc_out[rows, :] + vec_ref[3:4, :]
            bout_ref[rows, :] = block_out.astype(bout_ref.dtype)
            gvec_ref[4:5, :] += jnp.sum(block_out * cot, axis=0, keepdims=True)
            centered, inverse = norm_parts(hidden)
            normed = centered * inverse
            grad_norm = acc_gn[rows, :]
            gvec_ref[0:1, :] += jnp.sum(normed * grad_norm, axis=0, keepdims=True)
            gvec_ref[1:2, :] += jnp.sum(grad_norm, axis=0, keepdims=True)
            scaled = grad_norm * vec_ref[0:1, :]
            grad_value = inverse * (
                scaled
                - jnp.mean(scaled, axis=1, keepdims=True)
                - normed * jnp.mean(scaled * normed, axis=1, keepdims=True)
            )
            grad_hidden = mix * cot + grad_value
            ghid_ref[rows, :] = grad_hidden
            grad_attn = grad_hidden.astype(BF)
            n2_ref[rows, :] = grad_attn
            n2t_ref[:, rows] = att_ref[rows, :].T
            gvec_ref[2:3, :] += jnp.sum(grad_attn.astype(F32), axis=0, keepdims=True)
            gvec_ref[3:4, :] += jnp.sum(gb_ref[rows, :].astype(F32), axis=0, keepdims=True)
            gatt_ref[rows, :] = nt_dot(grad_attn, cols(wout_ref, 0, width // 128)).astype(BF)

        grad_attn_all = n2_ref[...]
        for r in range(width // 256):
            for k in range(width // 256):
                put_tiles(
                    gwout_ref, 16 * r, 2 * k,
                    nn_dot(
                        n2t_ref[256 * r : 256 * r + 256, :],
                        grad_attn_all[:, 256 * k : 256 * k + 256],
                    ).astype(BF),
                )


def middle(x_row, attended, cot_row, w_out, w_up, w_down, vectors, b_up, mix):
    length, width = x_row.shape
    (up_array, up_rows), (down_array, down_first) = w_up, w_down
    inner = b_up.shape[1]
    steps = inner // 256
    once = pl.Buffered(1)

    def const(shape):
        return pl.BlockSpec(shape, lambda i: (0,) * len(shape), pipeline_mode=once)

    rows = const((length, width))
    row_tiles, col_tiles = width // 16, width // 128
    return pl.pallas_call(
        middle_kernel,
        grid=(steps,),
        in_specs=[
            rows, rows, rows, const(w_out.shape),
            pl.BlockSpec((up_rows, up_array.shape[1], 2, 16, 128), lambda i: (0, 0, i, 0, 0)),
            pl.BlockSpec((16, col_tiles, 16, 128), lambda i: (i + down_first, 0, 0, 0)),
            const(vectors.shape),
            pl.BlockSpec((1, 256), lambda i: (0, i)),
            pl.BlockSpec(memory_space=pltpu.SMEM),
        ],
        out_specs=[
            rows, rows, rows,
            pl.BlockSpec((row_tiles, 2, 16, 128), lambda i: (0, i, 0, 0)),
            pl.BlockSpec((16, col_tiles, 16, 128), lambda i: (i, 0, 0, 0)),
            const((row_tiles, col_tiles, 16, 128)),
            pl.BlockSpec((8, 256), lambda i: (0, i)),
            const((8, width)),
        ],
        out_shape=[
            jax.ShapeDtypeStruct((length, width), BF),
            jax.ShapeDtypeStruct((length, width), BF),
            jax.ShapeDtypeStruct((length, width), F32),
            jax.ShapeDtypeStruct((row_tiles, inner // 128, 16, 128), BF),
            jax.ShapeDtypeStruct((inner // 16, col_tiles, 16, 128), BF),
            jax.ShapeDtypeStruct((row_tiles, col_tiles, 16, 128), BF),
            jax.ShapeDtypeStruct((8, inner), F32),
            jax.ShapeDtypeStruct((8, width), F32),
        ],
        scratch_shapes=[
            pltpu.VMEM((length, width), F32),
            pltpu.VMEM((length, width), BF),
            pltpu.VMEM((width, length), BF),
            pltpu.VMEM((length, width), BF),
            pltpu.VMEM((length, width), F32),
            pltpu.VMEM((length, width), F32),
            pltpu.VMEM((length, 256), BF),
            pltpu.VMEM((length, 256), BF),
        ],
        compiler_params=pltpu.CompilerParams(vmem_limit_bytes=VMEM_LIMIT),
        name="middle",
    )(x_row, attended, cot_row, w_out, up_array, down_array, vectors, b_up, mix)


def last_kernel(
    x_ref, n1_ref, ghid_ref, gq_ref, gk_ref, gv_ref, w_ref, vec_ref,
    gx_ref, gw_ref, gb_ref, gvec_ref, n1t_ref, acc_ref,
):
    step = pl.program_id(0)
    steps = pl.num_programs(0)
    length, width = x_ref.shape
    tile = 256
    tiles = length // tile
    per_part = steps // 3

    @pl.when(step == 0)
    def _():
        @pl.loop(0, tiles)
        def _(t):
            rows = pl.ds(pl.multiple_of(t * tile, tile), tile)
            n1t_ref[:, rows] = n1_ref[rows, :].T
            acc_ref[rows, :] = jnp.zeros((tile, width), F32)

        gvec_ref[...] = jnp.zeros_like(gvec_ref)

    def one(grad_ref):
        grads = grad_ref[...]
        for r in range(width // 256):
            put_tiles(gw_ref, 16 * r, 0, nn_dot(n1t_ref[256 * r : 256 * r + 256, :], grads).astype(BF))
        gb_ref[0:1, :] = jnp.sum(grads.astype(F32), axis=0, keepdims=True)
        weight = cols(w_ref, 0, 2)

        @pl.loop(0, tiles)
        def _(t):
            rows = pl.ds(pl.multiple_of(t * tile, tile), tile)
            acc_ref[rows, :] += nt_dot(grad_ref[rows, :], weight)

    for part, grad_ref in enumerate((gq_ref, gk_ref, gv_ref)):
        pl.when(step // per_part == part)(partial(one, grad_ref))

    @pl.when(step == steps - 1)
    def _():
        @pl.loop(0, tiles)
        def _(t):
            rows = pl.ds(pl.multiple_of(t * tile, tile), tile)
            centered, inverse = norm_parts(x_ref[rows, :].astype(F32))
            normed = centered * inverse
            grad_norm = acc_ref[rows, :]
            gvec_ref[0:1, :] += jnp.sum(normed * grad_norm, axis=0, keepdims=True)
            gvec_ref[1:2, :] += jnp.sum(grad_norm, axis=0, keepdims=True)
            scaled = grad_norm * vec_ref[0:1, :]
            grad_value = inverse * (
                scaled
                - jnp.mean(scaled, axis=1, keepdims=True)
                - normed * jnp.mean(scaled * normed, axis=1, keepdims=True)
            )
            gx_ref[rows, :] = (ghid_ref[rows, :] + grad_value).astype(gx_ref.dtype)


def last(x_row, n1, grad_hidden, gq, gk, gv, w_qkv, vectors):
    length, width = x_row.shape
    array, lead = w_qkv
    steps = 3 * width // 256
    per_part = width // 256
    once = pl.Buffered(1)

    def const(shape):
        return pl.BlockSpec(shape, lambda i: (0,) * len(shape), pipeline_mode=once)

    def part_spec(part):
        return pl.BlockSpec(
            (length, 256), lambda i: (0, jnp.clip(i - part * per_part, 0, per_part - 1))
        )

    rows = const((length, width))
    row_tiles = width // 16
    return pl.pallas_call(
        last_kernel,
        grid=(steps,),
        in_specs=[
            rows, rows, rows, part_spec(0), part_spec(1), part_spec(2),
            pl.BlockSpec((lead, array.shape[1], 2, 16, 128), lambda i: (0, 0, i, 0, 0)),
            const(vectors.shape),
        ],
        out_specs=[
            rows,
            pl.BlockSpec((row_tiles, 2, 16, 128), lambda i: (0, i, 0, 0)),
            pl.BlockSpec((8, 256), lambda i: (0, i)),
            const((8, width)),
        ],
        out_shape=[
            jax.ShapeDtypeStruct((length, width), BF),
            jax.ShapeDtypeStruct((row_tiles, 3 * width // 128, 16, 128), BF),
            jax.ShapeDtypeStruct((8, 3 * width), F32),
            jax.ShapeDtypeStruct((8, width), F32),
        ],
        scratch_shapes=[pltpu.VMEM((width, length), BF), pltpu.VMEM((length, width), F32)],
        compiler_params=pltpu.CompilerParams(vmem_limit_bytes=VMEM_LIMIT),
        name="last",
    )(x_row, n1, grad_hidden, gq, gk, gv, array, vectors)


def history_kernel(hist_ref, cot_ref, c_ref, part_ref, grad_ref, dots_ref):
    group = hist_ref.shape[0]
    first = pl.program_id(1) * group
    cot = cot_ref[...].astype(F32)
    rows, width = cot.shape

    @pl.when(pl.program_id(1) == 0)
    def _():
        part_ref[...] = jnp.zeros_like(part_ref)

    total = part_ref[...]
    for j in range(group):
        mix = c_ref[first + j]
        past = hist_ref[j].astype(F32)
        total = total + mix * past
        grad_ref[j] = mix * cot
        dots = jnp.sum((past * cot).reshape(rows // 8, 8, width), axis=0)
        dots_ref[0, 8 * j : 8 * j + 8, :] = sum(
            dots[:, 128 * k : 128 * k + 128] for k in range(width // 128)
        )
    part_ref[...] = total


def history_pass(history, cotangent, coefficient):
    terms, tokens, width = history.shape
    tile, group = 128, 6
    return pl.pallas_call(
        history_kernel,
        grid=(tokens // tile, terms // group),
        in_specs=[
            pl.BlockSpec((group, tile, width), lambda t, j: (j, t, 0)),
            pl.BlockSpec((tile, width), lambda t, j: (t, 0)),
            pl.BlockSpec(memory_space=pltpu.SMEM),
        ],
        out_specs=[
            pl.BlockSpec((tile, width), lambda t, j: (t, 0)),
            pl.BlockSpec((group, tile, width), lambda t, j: (j, t, 0)),
            pl.BlockSpec((1, 8 * group, 128), lambda t, j: (t, j, 0)),
        ],
        out_shape=[
            jax.ShapeDtypeStruct((tokens, width), F32),
            jax.ShapeDtypeStruct((terms, tokens, width), F32),
            jax.ShapeDtypeStruct((tokens // tile, 8 * terms, 128), F32),
        ],
        compiler_params=pltpu.CompilerParams(vmem_limit_bytes=VMEM_LIMIT),
        name="history",
    )(history, cotangent, coefficient)


HALO = 2048


class Plan:
    def __init__(self, devices, shape_list):
        sizes = [math.prod(shape) for shape in shape_list]
        starts = [sum(sizes[:i]) for i in range(len(sizes))]
        self.total = sum(sizes)
        self.devices = devices
        self.own = self.total // devices
        self.matrices = [(starts[i], shape_list[i]) for i in (2, 4)]
        self.vectors = [(0, sizes[0] + sizes[1]), (starts[3], sizes[3]), (starts[5], sizes[5])]
        first, second = (math.prod(shape) for _, shape in self.matrices)
        self.block = (first + second) // devices
        self.split = devices * first // (first + second)
        self.rows = [
            shape[0] // n if n else 0
            for (_, shape), n in zip(self.matrices, (self.split, devices - self.split))
        ]
        self.fits = self.total % devices == 0 and (first + second) % devices == 0
        for (_, shape), n, rows in zip(
            self.matrices, (self.split, devices - self.split), self.rows
        ):
            self.fits = self.fits and n > 0 and rows * n == shape[0] and rows % 16 == 0
            self.fits = self.fits and rows * shape[1] == self.block
        self.owners = [at // self.own for at, _ in self.vectors]
        if self.fits:
            for s in range(devices):
                shift = self.block_start(s) - self.own * s
                self.fits = self.fits and -HALO <= shift <= HALO
                self.fits = self.fits and shift + self.block - self.own <= HALO
                self.fits = self.fits and self.own - self.block - shift <= HALO
            for (at, size), owner in zip(self.vectors, self.owners):
                self.fits = self.fits and at + size <= self.own * (owner + 1) + HALO
            self.fits = self.fits and len(set(self.owners)) == len(self.owners)

    def block_start(self, s):
        (first, _), (second, _) = self.matrices
        if isinstance(s, int):
            return first + self.block * s if s < self.split else second + self.block * (s - self.split)
        return jnp.where(
            s < self.split, first + self.block * s, second + self.block * (s - self.split)
        )

    def tile_shapes(self):
        return [
            (rows // 16, shape[1] // 128) for (_, shape), rows in zip(self.matrices, self.rows)
        ]

    def to_tiles(self, flat, s):
        forms = [
            flat.reshape(rt, 16, ct, 128).transpose(0, 2, 1, 3).reshape(rt * ct, 16, 128)
            for rt, ct in self.tile_shapes()
        ]
        return jnp.where(s < self.split, forms[0], forms[1])

    def from_tiles(self, tiles, s):
        forms = [
            tiles.reshape(rt, ct, 16, 128).transpose(0, 2, 1, 3).reshape(-1)
            for rt, ct in self.tile_shapes()
        ]
        return jnp.where(s < self.split, forms[0], forms[1])

    def vector_rows(self):
        return -(-max(size for _, size in self.vectors) // 1024) * 8

    def blocks(self, flat, before, after, s):
        room = self.vector_rows() * 128
        joined = jnp.concatenate([before, flat, after, jnp.zeros((room,), flat.dtype)])
        aligned = lax.dynamic_slice(
            joined, (HALO + self.block_start(s) - self.own * s,), (self.block,)
        )
        place = jnp.int32(0)
        for (at, _), owner in zip(self.vectors, self.owners):
            place = jnp.where(s == owner, at - self.own * owner, place)
        extra = lax.dynamic_slice(joined, (HALO + place,), (room,))
        return self.to_tiles(aligned, s), extra.reshape(-1, 128)

    def shard(self, aligned, before, after, vectors, s):
        room = self.vector_rows() * 128
        edge = jnp.zeros((room,), aligned.dtype)
        joined = jnp.concatenate([edge, before, aligned, after, edge])
        begin = self.block_start(s)
        for (at, size), value in zip(self.vectors, vectors):
            place = jnp.clip(room + HALO + at - begin, 0, joined.shape[0] - size)
            joined = lax.dynamic_update_slice(joined, value, (place,))
        return lax.dynamic_slice(joined, (room + HALO + self.own * s - begin,), (self.own,))


def neighbour_edges(values_list, count):
    axes = ("dp", "tok")
    tails = jnp.stack([v[-HALO:] for v in values_list])
    heads = jnp.stack([v[:HALO] for v in values_list])
    before = lax.ppermute(tails, axes, [(i, (i + 1) % count) for i in range(count)])
    after = lax.ppermute(heads, axes, [(i, (i - 1) % count) for i in range(count)])
    return before, after


def plans(devices):
    return Plan(devices, attention_shapes()), Plan(devices, feedforward_shapes())


def row_tables(lengths_row, length):
    places = jnp.arange(length, dtype=jnp.int32)
    segment, position = layout(lengths_row[None], places)
    lane = jnp.arange(128, dtype=jnp.int32) % HEAD_DIM
    half_dim = HEAD_DIM // 2
    frequency = jnp.exp(
        (lane % half_dim).astype(jnp.float32) * (-2.0 * math.log(10000.0) / HEAD_DIM)
    )
    angle = position[0].astype(jnp.float32)[:, None] * frequency[None, :]
    sine = jnp.where(lane < half_dim, -1.0, 1.0)[None, :] * jnp.sin(angle)
    return segment[0], jnp.cos(angle), sine


def row_shards(
    inputs,
    history,
    document_lengths,
    cotangent,
    attention_params,
    attention_first,
    attention_second,
    feedforward_params,
    feedforward_first,
    feedforward_second,
    mixing_offsets,
    mixing_first,
    mixing_second,
    step_count,
):
    row_count, span, width = inputs.shape
    tok_size = lax.axis_size("tok")
    devices = lax.axis_size("dp") * tok_size
    length = span * tok_size
    tokens_all = row_count * span * devices
    axes = ("dp", "tok")
    s = lax.axis_index(axes)
    plan_a, plan_f = plans(devices)
    reach = length // 2

    low_a, low_f = attention_params.astype(BF), feedforward_params.astype(BF)
    before, after = neighbour_edges([low_a, low_f], devices)
    tiles_a, extra_a = plan_a.blocks(low_a, before[0], after[0], s)
    tiles_f, extra_f = plan_f.blocks(low_f, before[1], after[1], s)
    extra = jnp.concatenate([extra_a, extra_f]).reshape(-1, 16, 128)
    count_a, count_f = tiles_a.shape[0], tiles_f.shape[0]
    got_a = lax.all_gather(jnp.concatenate([tiles_a, extra]), axes, axis=0, tiled=False)
    got_f = lax.all_gather(tiles_f, axes, axis=0, tiled=False)
    extras = got_a[:, count_a:].reshape(devices, -1).astype(F32)
    room_a = plan_a.vector_rows() * 128

    def pick(plan, which, at):
        return extras[plan.owners[which], at : at + plan.vectors[which][1]]

    gain_one, shift_one = jnp.split(pick(plan_a, 0, 0), 2)
    b_qkv, b_out = pick(plan_a, 1, 0), pick(plan_a, 2, 0)
    gain_two, shift_two = jnp.split(pick(plan_f, 0, room_a), 2)
    b_up, b_down = pick(plan_f, 1, room_a), pick(plan_f, 2, room_a)
    (rq, cq), (ro, co) = plan_a.tile_shapes()
    (ru, cu), (rd, cd) = plan_f.tile_shapes()
    w_qkv = got_a[: plan_a.split, :count_a].reshape(plan_a.split, rq, cq, 16, 128)
    w_out = got_a[plan_a.split :, :count_a].reshape(devices - plan_a.split, ro, co, 16, 128)
    w_up = (got_f.reshape(devices * ru * cu // (ru * cu), ru, cu, 16, 128), plan_f.split)
    w_down = (got_f.reshape(devices * rd, cd, 16, 128), plan_f.split * rd // 16)

    def stack(vectors, wide):
        vectors = [jnp.pad(v, (0, wide - v.shape[0])) for v in vectors]
        vectors = vectors + [jnp.zeros((wide,), F32)] * (8 - len(vectors))
        return jnp.stack(vectors)

    def to_row(values):
        return lax.all_to_all(values, "tok", split_axis=0, concat_axis=1, tiled=True).reshape(
            length, width
        )

    def from_row(values):
        return lax.all_to_all(
            values.reshape(1, length, width), "tok", split_axis=1, concat_axis=0, tiled=True
        )

    x_row, cot_row = to_row(inputs), to_row(cotangent)
    own_lengths = lax.dynamic_index_in_dim(document_lengths, lax.axis_index("tok"), 0, False)
    segment, cosine, sine = row_tables(own_lengths, length)
    seg_col, seg_row = segment[:, None], segment[None, :]

    term_count = mixing_offsets.shape[0]
    coefficient = mixing_offsets + (jnp.arange(term_count) == term_count - 1).astype(F32)
    tokens = row_count * span
    history_part, grad_history, history_dots = history_pass(
        history.reshape(term_count - 1, tokens, width), cotangent.reshape(tokens, width), coefficient
    )

    normed_one, queries, keys, values = project(
        x_row, w_qkv, stack([gain_one, shift_one, b_qkv], 3 * width), cosine, sine
    )
    attended, lse = row_attend(queries, keys, values, seg_col, seg_row, reach)
    block_out, grad_attended, grad_hidden, gw_up, gw_down, gw_out, gb_up, gvec_two = middle(
        x_row, attended, cot_row, w_out, w_up, w_down,
        stack([gain_two, shift_two, b_out, b_down], width), b_up[None, :], coefficient[-1:],
    )
    gq, gk, gv = row_attend_back(
        queries, keys, values, grad_attended, lse, seg_col, seg_row, cosine, sine, reach
    )
    grad_row, gw_qkv, gb_qkv, gvec_one = last(
        x_row, normed_one, grad_hidden, gq, gk, gv, (w_qkv, plan_a.split), stack([gain_one], width)
    )
    mixed = history_part.reshape(row_count, span, width) + coefficient[-1] * from_row(
        block_out
    ).astype(F32)
    grad_inputs = from_row(grad_row).astype(F32)

    small = jnp.concatenate(
        [
            gvec_one[0], gvec_one[1], gb_qkv[0], gvec_two[2],
            gvec_two[0], gvec_two[1], gb_up[0], gvec_two[3],
            jnp.sum(history_dots.reshape(-1, term_count - 1, 8 * 128), axis=(0, 2)),
            jnp.sum(gvec_two[4])[None],
        ]
    )
    small = lax.psum(small, axes) / tokens_all
    scale = 1.0 / tokens_all
    sent_a = jnp.concatenate(
        [gw_qkv.reshape(plan_a.split, -1, 16, 128), gw_out.reshape(devices - plan_a.split, -1, 16, 128)]
    )
    sent_f = jnp.concatenate(
        [gw_up.reshape(plan_f.split, -1, 16, 128), gw_down.reshape(devices - plan_f.split, -1, 16, 128)]
    )
    sum_a = lax.psum_scatter(sent_a, axes, scatter_dimension=0, tiled=False)
    sum_f = lax.psum_scatter(sent_f, axes, scatter_dimension=0, tiled=False)
    flat_a = plan_a.from_tiles(sum_a.astype(F32) * scale, s)
    flat_f = plan_f.from_tiles(sum_f.astype(F32) * scale, s)
    before, after = neighbour_edges([flat_a, flat_f], devices)
    at = 0
    parts = []
    for plan in (plan_a, plan_f):
        for _, size in plan.vectors:
            parts.append(small[at : at + size])
            at = at + size
    attention_share = plan_a.shard(flat_a, before[0], after[0], parts[:3], s)
    feedforward_share = plan_f.shard(flat_f, before[1], after[1], parts[3:], s)
    mixing_grad = small[at:]

    count_now = step_count[0]
    attention_places = s * plan_a.own + jnp.arange(plan_a.own, dtype=jnp.int32)
    feedforward_places = s * plan_f.own + jnp.arange(plan_f.own, dtype=jnp.int32)
    attention_step = adam_update(
        attention_params, attention_share, attention_first, attention_second, count_now,
        decay_mask(attention_places, attention_shapes()),
    )
    feedforward_step = adam_update(
        feedforward_params, feedforward_share, feedforward_first, feedforward_second, count_now,
        decay_mask(feedforward_places, feedforward_shapes()),
    )
    mixing_step = adam_update(
        mixing_offsets, mixing_grad, mixing_first, mixing_second, count_now, 0.0
    )
    return (
        mixed.astype(BF),
        grad_inputs,
        grad_history.reshape(history.shape),
        *attention_step,
        *feedforward_step,
        *mixing_step,
    )


def shards(inputs, *others):
    row_count, span, width = inputs.shape
    tok_size = lax.axis_size("tok")
    devices = lax.axis_size("dp") * tok_size
    by_rows = row_count == tok_size and width == D and (span * tok_size) % 256 == 0
    if by_rows and all(plan.fits for plan in plans(devices)):
        return row_shards(inputs, *others)
    return general_shards(inputs, *others)


def solution(mesh):
    in_specs = (
        P("dp", "tok", None),
        P(None, "dp", "tok", None),
        P("dp", None),
        P("dp", "tok", None),
        P(("dp", "tok")),
        P(("dp", "tok")),
        P(("dp", "tok")),
        P(("dp", "tok")),
        P(("dp", "tok")),
        P(("dp", "tok")),
        P(),
        P(),
        P(),
        P(),
    )
    out_specs = (
        P("dp", "tok", None),
        P("dp", "tok", None),
        P(None, "dp", "tok", None),
        P(("dp", "tok")),
        P(("dp", "tok")),
        P(("dp", "tok")),
        P(("dp", "tok")),
        P(("dp", "tok")),
        P(("dp", "tok")),
        P(),
        P(),
        P(),
    )
    return jax.shard_map(shards, mesh=mesh, in_specs=in_specs, out_specs=out_specs, check_vma=False)
```

```python
from functools import partial
import math

import jax
import jax.numpy as jnp
from jax import lax
from jax.experimental import pallas as pl
from jax.experimental.pallas import tpu as pltpu
from jax.sharding import PartitionSpec as P

D = 768
HEADS = 12
HEAD_DIM = 64
FF = 3072
DOCS = 7


beta_first = 0.9
beta_second = 0.95
learning_rate = 0.05
decay_rate = 0.1
adam_epsilon = 1e-08
norm_epsilon = 1e-05
masked_score = -1e30


def layer_norm(values, gain, shift):
    centered = values - jnp.mean(values, axis=-1, keepdims=True)
    variance = jnp.mean(centered * centered, axis=-1, keepdims=True)
    return centered * lax.rsqrt(variance + norm_epsilon) * gain + shift


def rotate(values, position):
    half_dim = values.shape[-1] // 2
    frequency = jnp.exp(
        jnp.arange(half_dim, dtype=jnp.float32) * (-2.0 * math.log(10000.0) / values.shape[-1])
    )
    angle = position.astype(jnp.float32)[..., None] * frequency
    cosine = jnp.cos(angle)[..., None, :]
    sine = jnp.sin(angle)[..., None, :]
    first_half = values[..., :half_dim]
    second_half = values[..., half_dim:]
    return jnp.concatenate(
        [first_half * cosine - second_half * sine, second_half * cosine + first_half * sine],
        axis=-1,
    )


def turn_back(gradient_part, position):
    return jax.vjp(partial(rotate, position=position), gradient_part)[1](gradient_part)[0]


def layout(lengths_rows, places):
    ends = jnp.cumsum(lengths_rows, axis=1)
    starts = ends - lengths_rows
    doc_count = lengths_rows.shape[1] - 1
    inside = places[None, :, None] >= ends[:, None, :doc_count]
    segment = jnp.sum(inside.astype(jnp.int32), axis=2)
    labels = jnp.arange(doc_count + 1, dtype=jnp.int32)
    chosen = segment[:, :, None] == labels[None, None, :]
    begin = jnp.sum(jnp.where(chosen, starts[:, None, :], 0), axis=2)
    return (segment, places[None, :] - begin)


def allowed_mask(segment_row, first_row, query_count):
    query_place = first_row + jnp.arange(query_count, dtype=jnp.int32)
    key_place = jnp.arange(segment_row.shape[0], dtype=jnp.int32)
    query_segment = lax.dynamic_slice_in_dim(segment_row, first_row, query_count, 0)
    earlier = key_place[None, :] <= query_place[:, None]
    same_doc = segment_row[None, :] == query_segment[:, None]
    real_key = (segment_row[None, :] < DOCS) | (key_place[None, :] == query_place[:, None])
    return earlier & same_doc & real_key


def block_scores(queries, keys_all, segment_row, first_row):
    scores = jnp.einsum(
        "qhd,khd->hqk", queries, keys_all, preferred_element_type=jnp.float32
    ) * HEAD_DIM ** (-0.5)
    allowed = allowed_mask(segment_row, first_row, queries.shape[0])
    return jnp.where(allowed[None], scores, masked_score)


def attention_shapes():
    return [(D,), (D,), (D, 3 * D), (3 * D,), (D, D), (D,)]


def feedforward_shapes():
    return [(D,), (D,), (D, FF), (FF,), (FF, D), (D,)]


def unpack(flat_vector, shape_list):
    pieces = []
    offset_at = 0
    for piece_shape in shape_list:
        piece_size = math.prod(piece_shape)
        pieces.append(flat_vector[offset_at : offset_at + piece_size].reshape(piece_shape))
        offset_at = offset_at + piece_size
    return pieces


def decay_mask(places, shape_list):
    mask_values = jnp.zeros(places.shape, jnp.float32)
    offset_at = 0
    for piece_shape in shape_list:
        piece_size = math.prod(piece_shape)
        if len(piece_shape) == 2:
            inside = (places >= offset_at) & (places < offset_at + piece_size)
            mask_values = mask_values + inside.astype(jnp.float32)
        offset_at = offset_at + piece_size
    return mask_values * decay_rate


def adam_update(values, gradient, moment_one, moment_two, step_number, decay_values):
    first_new = beta_first * moment_one + (1.0 - beta_first) * gradient
    second_new = beta_second * moment_two + (1.0 - beta_second) * gradient * gradient
    power_now = step_number.astype(jnp.float32)
    fix_one = 1.0 - jnp.power(beta_first, power_now)
    fix_two = 1.0 - jnp.power(beta_second, power_now)
    step_size = first_new / fix_one / (jnp.sqrt(second_new / fix_two) + adam_epsilon)
    return (values - learning_rate * (step_size + decay_values * values), first_new, second_new)


def to_groups(values, subsets):
    full_shape = values.shape
    row_total = full_shape[0]
    half_width = full_shape[-1] // 2
    split_view = values.reshape(
        (subsets, row_total // subsets) + full_shape[1:-1] + (2, half_width)
    )
    moved = jnp.moveaxis(split_view, -2, 0)
    return moved.reshape((2 * subsets, row_total // subsets) + full_shape[1:-1] + (half_width,))


def from_groups(values, subsets):
    full_shape = values.shape
    split_view = values.reshape((2, subsets) + full_shape[1:])
    moved = jnp.moveaxis(split_view, 0, -2)
    return moved.reshape((subsets * full_shape[1],) + full_shape[2:-1] + (2 * full_shape[-1],))


def attend_rows(head_qkv, head_segment):
    item_count = head_qkv.shape[1]
    length_all = head_qkv.shape[2]
    group_width = head_qkv.shape[4]
    head_count = group_width // HEAD_DIM
    block_rows = min(512, length_all)
    block_count = length_all // block_rows
    rows_qkv = head_qkv.reshape(item_count, length_all, 3, head_count, HEAD_DIM)
    rows_segment = head_segment.reshape(item_count, length_all)

    def attend_one_block(block_index):
        row_index = block_index // block_count
        first_row = block_index % block_count * block_rows
        current = rows_qkv[row_index]
        queries = lax.dynamic_slice_in_dim(current[:, 0], first_row, block_rows, 0)
        masked = block_scores(queries, current[:, 1], rows_segment[row_index], first_row)
        top_score = jnp.max(masked, axis=2, keepdims=True)
        exponent = jnp.exp(masked - top_score)
        total_weight = jnp.sum(exponent, axis=2, keepdims=True)
        soft_weights = (exponent / total_weight).astype(jnp.bfloat16)
        attended = jnp.einsum(
            "hqk,khd->qhd", soft_weights, current[:, 2], preferred_element_type=jnp.float32
        )
        log_total = (top_score + jnp.log(total_weight))[:, :, 0]
        return (attended.reshape(block_rows, group_width).astype(jnp.bfloat16), log_total)

    outputs, log_totals = lax.map(
        attend_one_block, jnp.arange(item_count * block_count, dtype=jnp.int32)
    )
    return (
        outputs.reshape(1, item_count, length_all, group_width),
        log_totals.reshape(1, item_count, block_count, head_count, block_rows),
    )


def attend_back(head_qkv, head_segment, log_totals, head_grads):
    item_count = head_qkv.shape[1]
    length_all = head_qkv.shape[2]
    group_width = head_qkv.shape[4]
    head_count = group_width // HEAD_DIM
    block_rows = min(512, length_all)
    block_count = length_all // block_rows
    scale_value = HEAD_DIM ** (-0.5)

    def one_row(pieces):
        current, segment_row, log_row, grad_row = pieces
        keys_all = current[:, 1]
        values_all = current[:, 2]

        def one_one_block(carried, block_index):
            first_row = block_index * block_rows
            queries = lax.dynamic_slice_in_dim(current[:, 0], first_row, block_rows, 0)
            grad_block = lax.dynamic_slice_in_dim(grad_row, first_row, block_rows, 0)
            masked = block_scores(queries, keys_all, segment_row, first_row)
            soft_weights = jnp.exp(masked - log_row[block_index][:, :, None])
            grad_weights = jnp.einsum(
                "qhd,khd->hqk", grad_block, values_all, preferred_element_type=jnp.float32
            )
            inner_sum = jnp.sum(soft_weights * grad_weights, axis=2, keepdims=True)
            grad_scores = (soft_weights * (grad_weights - inner_sum)).astype(jnp.bfloat16)
            grad_query = (
                jnp.einsum(
                    "hqk,khd->qhd", grad_scores, keys_all, preferred_element_type=jnp.float32
                )
                * scale_value
            )
            grad_key = (
                carried[0]
                + jnp.einsum(
                    "hqk,qhd->khd", grad_scores, queries, preferred_element_type=jnp.float32
                )
                * scale_value
            )
            grad_value = carried[1] + jnp.einsum(
                "hqk,qhd->khd",
                soft_weights.astype(jnp.bfloat16),
                grad_block,
                preferred_element_type=jnp.float32,
            )
            return ((grad_key, grad_value), grad_query)

        empty_grad = jnp.zeros((length_all, head_count, HEAD_DIM), jnp.float32)
        (grad_key, grad_value), grad_query = lax.scan(
            one_one_block, (empty_grad, empty_grad), jnp.arange(block_count, dtype=jnp.int32)
        )
        grad_query = grad_query.reshape(length_all, head_count, HEAD_DIM)
        return jnp.stack([grad_query, grad_key, grad_value], axis=1).astype(jnp.bfloat16)

    row_grads = lax.map(
        one_row,
        (
            head_qkv.reshape(item_count, length_all, 3, head_count, HEAD_DIM),
            head_segment.reshape(item_count, length_all),
            log_totals.reshape(item_count, block_count, head_count, block_rows),
            head_grads.reshape(item_count, length_all, head_count, HEAD_DIM),
        ),
    )
    return row_grads.reshape(1, item_count, length_all, 3, group_width)


def general_shards(
    inputs,
    history,
    document_lengths,
    cotangent,
    attention_params,
    attention_first,
    attention_second,
    feedforward_params,
    feedforward_first,
    feedforward_second,
    mixing_offsets,
    mixing_first,
    mixing_second,
    step_count,
):
    row_count, token_span, model_width = inputs.shape
    subsets = lax.axis_size("tok") // 2
    per_device = row_count // subsets
    tokens_all = row_count * token_span * lax.axis_size("dp") * lax.axis_size("tok")
    attention_flat, feedforward_flat = (
        lax.all_gather(attention_params.astype(jnp.bfloat16), ("dp", "tok"), axis=0, tiled=True),
        lax.all_gather(feedforward_params.astype(jnp.bfloat16), ("dp", "tok"), axis=0, tiled=True),
    )
    gain_one, shift_one, w_qkv, b_qkv, w_out, b_out = unpack(attention_flat, attention_shapes())
    gain_two, shift_two, w_up, b_up, w_down, b_down = unpack(feedforward_flat, feedforward_shapes())
    gain_one = gain_one.astype(jnp.float32)
    shift_one = shift_one.astype(jnp.float32)
    gain_two = gain_two.astype(jnp.float32)
    shift_two = shift_two.astype(jnp.float32)
    places = lax.axis_index("tok") * token_span + jnp.arange(token_span, dtype=jnp.int32)
    segment, position = layout(document_lengths, places)
    current = inputs.astype(jnp.float32)
    normed_one = layer_norm(current, gain_one, shift_one).astype(jnp.bfloat16)
    project = jnp.dot(normed_one, w_qkv, preferred_element_type=jnp.float32) + b_qkv.astype(
        jnp.float32
    )
    project = project.reshape(row_count, token_span, 3, HEADS, HEAD_DIM)
    queries = rotate(project[:, :, 0], position)
    keys_all = rotate(project[:, :, 1], position)
    packed = jnp.stack([queries, keys_all, project[:, :, 2]], axis=2).astype(jnp.bfloat16)
    send_qkv = to_groups(packed.reshape(row_count, token_span, 3, model_width), subsets)
    send_segment = jnp.broadcast_to(
        segment.reshape(1, subsets, per_device, token_span), (2, subsets, per_device, token_span)
    ).reshape(2 * subsets, per_device, token_span)
    head_qkv = lax.all_to_all(send_qkv, "tok", split_axis=0, concat_axis=2, tiled=True)
    head_segment = lax.all_to_all(send_segment, "tok", split_axis=0, concat_axis=2, tiled=True)
    outputs, log_totals = attend_rows(head_qkv, head_segment)
    returned = lax.all_to_all(outputs, "tok", split_axis=2, concat_axis=0, tiled=True)
    returned, head_qkv, head_segment, log_totals = (returned, head_qkv, head_segment, log_totals)
    attended = from_groups(returned, subsets)
    hidden = (
        current
        + jnp.dot(attended, w_out, preferred_element_type=jnp.float32)
        + b_out.astype(jnp.float32)
    )
    normed_two = layer_norm(hidden, gain_two, shift_two).astype(jnp.bfloat16)
    up_value = jnp.dot(normed_two, w_up, preferred_element_type=jnp.float32) + b_up.astype(
        jnp.float32
    )
    active = jax.nn.gelu(up_value).astype(jnp.bfloat16)
    block_out = (
        hidden
        + jnp.dot(active, w_down, preferred_element_type=jnp.float32)
        + b_down.astype(jnp.float32)
    )
    term_count = mixing_offsets.shape[0]
    coefficient = mixing_offsets + (jnp.arange(term_count) == term_count - 1).astype(jnp.float32)
    history_part = jnp.einsum(
        "j,jrtd->rtd", coefficient[:-1], history, preferred_element_type=jnp.float32
    )
    mixed = (history_part + coefficient[-1] * block_out).astype(jnp.bfloat16)
    grad_mixed = cotangent.astype(jnp.float32)
    grad_history = coefficient[:-1, None, None, None] * grad_mixed[None]
    history_terms = jnp.einsum(
        "jrtd,rtd->j", history, grad_mixed, preferred_element_type=jnp.float32
    )
    mixing_terms = jnp.concatenate([history_terms, jnp.sum(block_out * grad_mixed)[None]])
    mixing_grad = lax.psum(mixing_terms, ("dp", "tok")) / tokens_all
    grad_block = coefficient[-1] * grad_mixed
    grad_branch = grad_block.astype(jnp.bfloat16)
    grad_w_down = jnp.einsum("rtf,rtd->fd", active, grad_branch, preferred_element_type=jnp.float32)
    grad_b_down = jnp.sum(grad_branch.astype(jnp.float32), axis=(0, 1))
    grad_active = jnp.einsum("rtd,fd->rtf", grad_branch, w_down, preferred_element_type=jnp.float32)
    grad_up = jax.vjp(jax.nn.gelu, up_value)[1](grad_active)[0].astype(jnp.bfloat16)
    grad_w_up = jnp.einsum("rtd,rtf->df", normed_two, grad_up, preferred_element_type=jnp.float32)
    grad_b_up = jnp.sum(grad_up.astype(jnp.float32), axis=(0, 1))
    grad_normed_two = jnp.einsum("rtf,df->rtd", grad_up, w_up, preferred_element_type=jnp.float32)
    grad_hidden_norm, grad_gain_two, grad_shift_two = jax.vjp(
        layer_norm, hidden, gain_two, shift_two
    )[1](grad_normed_two)
    grad_hidden = grad_block + grad_hidden_norm
    feedforward_grad = jnp.concatenate(
        [
            grad_gain_two,
            grad_shift_two,
            grad_w_up.reshape(-1),
            grad_b_up,
            grad_w_down.reshape(-1),
            grad_b_down,
        ]
    )
    feedforward_share = lax.psum_scatter(
        feedforward_grad, ("dp", "tok"), scatter_dimension=0, tiled=True
    )
    grad_attn = grad_hidden.astype(jnp.bfloat16)
    grad_w_out = jnp.einsum("rtd,rte->de", attended, grad_attn, preferred_element_type=jnp.float32)
    grad_b_out = jnp.sum(grad_attn.astype(jnp.float32), axis=(0, 1))
    grad_attended = jnp.einsum(
        "rte,de->rtd", grad_attn, w_out, preferred_element_type=jnp.float32
    ).astype(jnp.bfloat16)
    head_grads = lax.all_to_all(
        to_groups(grad_attended, subsets), "tok", split_axis=0, concat_axis=2, tiled=True
    )
    head_back = attend_back(head_qkv, head_segment, log_totals, head_grads)
    token_back = from_groups(
        lax.all_to_all(head_back, "tok", split_axis=2, concat_axis=0, tiled=True), subsets
    )
    token_back = token_back.astype(jnp.float32).reshape(row_count, token_span, 3, HEADS, HEAD_DIM)
    grad_project = jnp.stack(
        [
            turn_back(token_back[:, :, 0], position),
            turn_back(token_back[:, :, 1], position),
            token_back[:, :, 2],
        ],
        axis=2,
    )
    grad_project = grad_project.reshape(row_count, token_span, 3 * model_width).astype(jnp.bfloat16)
    grad_w_qkv = jnp.einsum(
        "rtd,rte->de", normed_one, grad_project, preferred_element_type=jnp.float32
    )
    grad_b_qkv = jnp.sum(grad_project.astype(jnp.float32), axis=(0, 1))
    grad_normed_one = jnp.einsum(
        "rte,de->rtd", grad_project, w_qkv, preferred_element_type=jnp.float32
    )
    grad_current, grad_gain_one, grad_shift_one = jax.vjp(layer_norm, current, gain_one, shift_one)[
        1
    ](grad_normed_one)
    grad_inputs = grad_hidden + grad_current
    attention_grad = jnp.concatenate(
        [
            grad_gain_one,
            grad_shift_one,
            grad_w_qkv.reshape(-1),
            grad_b_qkv,
            grad_w_out.reshape(-1),
            grad_b_out,
        ]
    )
    attention_share = lax.psum_scatter(
        attention_grad, ("dp", "tok"), scatter_dimension=0, tiled=True
    )
    count_now = step_count[0]
    shard_index = lax.axis_index(("dp", "tok"))
    attention_places = shard_index * attention_params.shape[0] + jnp.arange(
        attention_params.shape[0], dtype=jnp.int32
    )
    feedforward_places = shard_index * feedforward_params.shape[0] + jnp.arange(
        feedforward_params.shape[0], dtype=jnp.int32
    )
    attention_step = adam_update(
        attention_params,
        attention_share / tokens_all,
        attention_first,
        attention_second,
        count_now,
        decay_mask(attention_places, attention_shapes()),
    )
    feedforward_step = adam_update(
        feedforward_params,
        feedforward_share / tokens_all,
        feedforward_first,
        feedforward_second,
        count_now,
        decay_mask(feedforward_places, feedforward_shapes()),
    )
    mixing_step = adam_update(
        mixing_offsets, mixing_grad, mixing_first, mixing_second, count_now, 0.0
    )
    return (
        mixed,
        grad_inputs,
        grad_history,
        attention_step[0],
        attention_step[1],
        attention_step[2],
        feedforward_step[0],
        feedforward_step[1],
        feedforward_step[2],
        mixing_step[0],
        mixing_step[1],
        mixing_step[2],
    )


VMEM_LIMIT = 58 * 1024 * 1024
BF = jnp.bfloat16
F32 = jnp.float32


def cols(ref, first, count):
    lead = math.prod(ref.shape[:-3]) * ref.shape[-2]
    pieces = []
    for at in range(first, first + count):
        index = (slice(None),) * (len(ref.shape) - 3) + (at,)
        pieces.append(ref[index].reshape(lead, 128))
    return pieces[0] if count == 1 else jnp.concatenate(pieces, axis=1)


def put_tiles(ref, row_at, col_at, value):
    rows, width = value.shape
    for at in range(width // 128):
        ref[pl.ds(row_at, rows // 16), col_at + at] = value[:, 128 * at : 128 * at + 128].reshape(
            rows // 16, 16, 128
        )


def norm_parts(values):
    mean = jnp.mean(values, axis=1, keepdims=True)
    centered = values - mean
    inverse = lax.rsqrt(jnp.mean(centered * centered, axis=1, keepdims=True) + norm_epsilon)
    return centered, inverse


def nt_dot(left, right):
    return lax.dot_general(left, right, (((1,), (1,)), ((), ())), preferred_element_type=F32)


def nn_dot(left, right):
    return lax.dot_general(left, right, (((1,), (0,)), ((), ())), preferred_element_type=F32)


def swap_halves(values):
    width = values.shape[1]
    lane = lax.broadcasted_iota(jnp.int32, values.shape, 1)
    return jnp.where(
        lane % HEAD_DIM < HEAD_DIM // 2,
        pltpu.roll(values, width - HEAD_DIM // 2, 1),
        pltpu.roll(values, HEAD_DIM // 2, 1),
    )


def project_kernel(x_ref, w_ref, vec_ref, cos_ref, sin_ref, n1_ref, q_ref, k_ref, v_ref):
    width = x_ref.shape[1]
    centered, inverse = norm_parts(x_ref[...].astype(F32))
    normed = (centered * inverse * vec_ref[0:1, :width] + vec_ref[1:2, :width]).astype(BF)
    n1_ref[...] = normed
    cosine = jnp.concatenate([cos_ref[...]] * 2, axis=1)
    sine = jnp.concatenate([sin_ref[...]] * 2, axis=1)
    per_part = width // 256
    for at in range(3 * per_part):
        part = nn_dot(normed, cols(w_ref, 2 * at, 2)) + vec_ref[2:3, 256 * at : 256 * at + 256]
        spot = slice(256 * (at % per_part), 256 * (at % per_part) + 256)
        if at < 2 * per_part:
            part = part * cosine + swap_halves(part) * sine
        if at < per_part:
            q_ref[:, spot] = (part * HEAD_DIM ** (-0.5)).astype(BF)
        elif at < 2 * per_part:
            k_ref[:, spot] = part.astype(BF)
        else:
            v_ref[:, spot] = part.astype(BF)


def project(x_row, w_qkv, vectors, cosine, sine):
    length, width = x_row.shape
    array, lead = w_qkv
    tile = 256
    whole = pl.BlockSpec(
        (lead,) + array.shape[1:], lambda i: (0,) * array.ndim, pipeline_mode=pl.Buffered(1)
    )
    rows = pl.BlockSpec((tile, width), lambda i: (i, 0))
    trig = pl.BlockSpec((tile, 128), lambda i: (i, 0))
    out = jax.ShapeDtypeStruct((length, width), BF)
    return pl.pallas_call(
        project_kernel,
        grid=(length // tile,),
        in_specs=[rows, whole, pl.BlockSpec(vectors.shape, lambda i: (0, 0)), trig, trig],
        out_specs=[rows] * 4,
        out_shape=[out] * 4,
        compiler_params=pltpu.CompilerParams(vmem_limit_bytes=VMEM_LIMIT),
        name="project",
    )(x_row, array, vectors, cosine, sine)


def key_range(block, block_rows, reach):
    return max(0, block * block_rows - reach), (block + 1) * block_rows


def fill_bias(bias_ref, seg_col_ref, seg_row_ref, block_rows, reach):
    length = seg_row_ref.shape[1]
    at = 0
    for block in range(length // block_rows):
        low, high = key_range(block, block_rows, reach)
        shape = (high - low, block_rows)
        key_place = low + lax.broadcasted_iota(jnp.int32, shape, 0)
        query_place = block * block_rows + lax.broadcasted_iota(jnp.int32, shape, 1)
        key_seg = seg_col_ref[low:high, :]
        query_seg = seg_row_ref[:, block * block_rows : (block + 1) * block_rows]
        allowed = (key_place <= query_place) & (key_seg == query_seg)
        allowed = allowed & ((key_seg < DOCS) | (key_place == query_place))
        bias_ref[at : at + high - low, :] = jnp.where(allowed, 0.0, masked_score)
        at = at + high - low


def bias_rows(length, block_rows, reach):
    return sum(
        high - low
        for low, high in (key_range(b, block_rows, reach) for b in range(length // block_rows))
    )


def head_mask(values, head):
    lane = lax.broadcasted_iota(jnp.int32, values.shape, 1)
    keep = lane < HEAD_DIM if head == 0 else lane >= HEAD_DIM
    return jnp.where(keep, values, jnp.zeros_like(values))


def attend_kernel(block_rows, reach, q_ref, k_ref, v_ref, sc_ref, sr_ref, o_ref, lse_ref, bias_ref):
    length = q_ref.shape[0]

    @pl.when(pl.program_id(0) == 0)
    def _():
        fill_bias(bias_ref, sc_ref, sr_ref, block_rows, reach)

    keys = k_ref[...]
    key_heads = [head_mask(keys, 0), head_mask(keys, 1)]
    value_turned = v_ref[...].T
    at = 0
    for block in range(length // block_rows):
        low, high = key_range(block, block_rows, reach)
        spot = slice(block * block_rows, (block + 1) * block_rows)
        queries = q_ref[spot, :]
        bias = bias_ref[at : at + high - low, :]
        at = at + high - low
        halves = []
        for head in range(2):
            scores = nt_dot(key_heads[head][low:high], queries) + bias
            top = jnp.max(scores, axis=0, keepdims=True)
            exponent = jnp.exp(scores - top)
            total = jnp.sum(exponent, axis=0, keepdims=True)
            probs = (exponent * (1.0 / total)).astype(BF)
            lse_ref[0, head : head + 1, spot] = top + jnp.log(total)
            turned = value_turned[HEAD_DIM * head : HEAD_DIM * head + HEAD_DIM, low:high]
            halves.append(nn_dot(turned, probs))
        o_ref[spot, :] = jnp.concatenate(halves, axis=0).T.astype(BF)


def row_attend(queries, keys, values, seg_col, seg_row, reach):
    length, width = queries.shape
    block_rows = 256
    pairs = width // 128
    pair = pl.BlockSpec((length, 128), lambda p: (0, p))
    return pl.pallas_call(
        partial(attend_kernel, block_rows, reach),
        grid=(pairs,),
        in_specs=[
            pair,
            pair,
            pair,
            pl.BlockSpec(seg_col.shape, lambda p: (0, 0)),
            pl.BlockSpec(seg_row.shape, lambda p: (0, 0)),
        ],
        out_specs=[pair, pl.BlockSpec((1, 2, length), lambda p: (p, 0, 0))],
        out_shape=[
            jax.ShapeDtypeStruct((length, width), BF),
            jax.ShapeDtypeStruct((pairs, 2, length), F32),
        ],
        scratch_shapes=[pltpu.VMEM((bias_rows(length, block_rows, reach), block_rows), F32)],
        compiler_params=pltpu.CompilerParams(vmem_limit_bytes=VMEM_LIMIT),
        name="attend",
    )(queries, keys, values, seg_col, seg_row)


def attend_back_kernel(
    block_rows, reach, q_ref, k_ref, v_ref, g_ref, lse_ref, sc_ref, sr_ref, cos_ref, sin_ref,
    gq_ref, gk_ref, gv_ref, bias_ref, dq_acc, dk_acc, dv_acc,
):
    length = q_ref.shape[0]

    @pl.when(pl.program_id(0) == 0)
    def _():
        fill_bias(bias_ref, sc_ref, sr_ref, block_rows, reach)

    keys = k_ref[...]
    key_heads = [head_mask(keys, 0), head_mask(keys, 1)]
    key_turned = keys.T
    vals = v_ref[...]
    value_heads = [head_mask(vals, 0), head_mask(vals, 1)]
    dk_acc[...] = jnp.zeros_like(dk_acc)
    dv_acc[...] = jnp.zeros_like(dv_acc)
    at = 0
    for block in range(length // block_rows):
        low, high = key_range(block, block_rows, reach)
        spot = slice(block * block_rows, (block + 1) * block_rows)
        queries = q_ref[spot, :]
        grads = g_ref[spot, :]
        bias = bias_ref[at : at + high - low, :]
        at = at + high - low
        halves = []
        for head in range(2):
            scores = nt_dot(key_heads[head][low:high], queries) + bias
            probs = jnp.exp(scores - lse_ref[0, head : head + 1, spot])
            dprobs = nt_dot(value_heads[head][low:high], grads)
            inner = jnp.sum(probs * dprobs, axis=0, keepdims=True)
            dscores = (probs * (dprobs - inner)).astype(BF)
            turned = key_turned[HEAD_DIM * head : HEAD_DIM * head + HEAD_DIM, low:high]
            halves.append(nn_dot(turned, dscores))
            dk_acc[low:high, :] += nn_dot(dscores, head_mask(queries, head))
            dv_acc[low:high, :] += nn_dot(probs.astype(BF), head_mask(grads, head))
        dq_acc[spot, :] = jnp.concatenate(halves, axis=0).T * HEAD_DIM ** (-0.5)
    cosine = cos_ref[...]
    sine = sin_ref[...]
    grad_query = dq_acc[...].astype(BF).astype(F32)
    grad_key = dk_acc[...].astype(BF).astype(F32)
    gq_ref[...] = (grad_query * cosine - swap_halves(grad_query) * sine).astype(BF)
    gk_ref[...] = (grad_key * cosine - swap_halves(grad_key) * sine).astype(BF)
    gv_ref[...] = dv_acc[...].astype(BF)


def row_attend_back(queries, keys, values, grads, lse, seg_col, seg_row, cosine, sine, reach):
    length, width = queries.shape
    block_rows = 256
    pair = pl.BlockSpec((length, 128), lambda p: (0, p))
    trig = pl.BlockSpec((length, 128), lambda p: (0, 0))
    out = jax.ShapeDtypeStruct((length, width), BF)
    return pl.pallas_call(
        partial(attend_back_kernel, block_rows, reach),
        grid=(width // 128,),
        in_specs=[
            pair, pair, pair, pair,
            pl.BlockSpec((1, 2, length), lambda p: (p, 0, 0)),
            pl.BlockSpec(seg_col.shape, lambda p: (0, 0)),
            pl.BlockSpec(seg_row.shape, lambda p: (0, 0)),
            trig, trig,
        ],
        out_specs=[pair] * 3,
        out_shape=[out] * 3,
        scratch_shapes=[pltpu.VMEM((bias_rows(length, block_rows, reach), block_rows), F32)]
        + [pltpu.VMEM((length, 128), F32)] * 3,
        compiler_params=pltpu.CompilerParams(vmem_limit_bytes=VMEM_LIMIT),
        name="attend_back",
    )(queries, keys, values, grads, lse, seg_col, seg_row, cosine, sine)


gelu_root = math.sqrt(2.0 / math.pi)


def middle_kernel(
    x_ref, att_ref, cot_ref, wout_ref, wup_ref, wdown_ref, vec_ref, bup_ref, own_cot_ref, c_ref,
    ghist_ref, bout_ref, gatt_ref, ghid_ref, gwup_ref, gwdown_ref, gwout_ref, gbup_ref, gvec_ref,
    hidden_ref, n2_ref, n2t_ref, gb_ref, acc_out, acc_gn, act_ref, gup_ref,
):
    step = pl.program_id(0)
    steps = pl.num_programs(0)
    length, width = x_ref.shape
    tile = 256
    tiles = length // tile
    mix = c_ref[c_ref.shape[0] - 1]
    group = ghist_ref.shape[0]

    @pl.when(step == 0)
    def _():
        @pl.loop(0, tiles)
        def _(t):
            rows = pl.ds(pl.multiple_of(t * tile, tile), tile)
            attended = att_ref[rows, :]
            hidden = x_ref[rows, :].astype(F32) + nn_dot(attended, cols(wout_ref, 0, width // 128))
            hidden = hidden + vec_ref[2:3, :]
            hidden_ref[rows, :] = hidden
            centered, inverse = norm_parts(hidden)
            normed = (centered * inverse * vec_ref[0:1, :] + vec_ref[1:2, :]).astype(BF)
            n2_ref[rows, :] = normed
            n2t_ref[:, rows] = normed.T
            gb_ref[rows, :] = (mix * cot_ref[rows, :].astype(F32)).astype(BF)
            acc_out[rows, :] = jnp.zeros((tile, width), F32)
            acc_gn[rows, :] = jnp.zeros((tile, width), F32)

        gvec_ref[...] = jnp.zeros_like(gvec_ref)

    w_up = cols(wup_ref, 0, 2)
    w_down = cols(wdown_ref, 0, width // 128)
    gbup_ref[...] = jnp.zeros_like(gbup_ref)

    @pl.loop(0, tiles)
    def _(t):
        rows = pl.ds(pl.multiple_of(t * tile, tile), tile)
        up = nn_dot(n2_ref[rows, :], w_up) + bup_ref[0:1, :]
        square = up * up
        turn = jnp.tanh(gelu_root * up * (1.0 + 0.044715 * square))
        half = 0.5 * (1.0 + turn)
        active = (up * half).astype(BF)
        act_ref[rows, :] = active
        acc_out[rows, :] += nn_dot(active, w_down)
        slope = half + (0.5 * gelu_root) * up * (1.0 - turn * turn) * (
            1.0 + (3.0 * 0.044715) * square
        )
        grad_up = (nt_dot(gb_ref[rows, :], w_down) * slope).astype(BF)
        gup_ref[rows, :] = grad_up
        acc_gn[rows, :] += nt_dot(grad_up, w_up)
        gbup_ref[0:1, :] += jnp.sum(grad_up.astype(F32), axis=0, keepdims=True)
        own_cot = own_cot_ref[rows, :].astype(F32)
        for j in range(group):
            ghist_ref[j, rows, :] = c_ref[step * group + j] * own_cot

    grad_up_all = gup_ref[...]
    for r in range(width // 256):
        put_tiles(
            gwup_ref, 16 * r, 0, nn_dot(n2t_ref[256 * r : 256 * r + 256, :], grad_up_all).astype(BF)
        )
    active_turned = act_ref[...].T
    for r in range(width // 256):
        put_tiles(
            gwdown_ref, 0, 2 * r, nn_dot(active_turned, gb_ref[:, 256 * r : 256 * r + 256]).astype(BF)
        )

    @pl.when(step == steps - 1)
    def _():
        @pl.loop(0, tiles)
        def _(t):
            rows = pl.ds(pl.multiple_of(t * tile, tile), tile)
            hidden = hidden_ref[rows, :]
            cot = cot_ref[rows, :].astype(F32)
            block_out = hidden + acc_out[rows, :] + vec_ref[3:4, :]
            bout_ref[rows, :] = block_out.astype(bout_ref.dtype)
            gvec_ref[4:5, :] += jnp.sum(block_out * cot, axis=0, keepdims=True)
            centered, inverse = norm_parts(hidden)
            normed = centered * inverse
            grad_norm = acc_gn[rows, :]
            gvec_ref[0:1, :] += jnp.sum(normed * grad_norm, axis=0, keepdims=True)
            gvec_ref[1:2, :] += jnp.sum(grad_norm, axis=0, keepdims=True)
            scaled = grad_norm * vec_ref[0:1, :]
            grad_value = inverse * (
                scaled
                - jnp.mean(scaled, axis=1, keepdims=True)
                - normed * jnp.mean(scaled * normed, axis=1, keepdims=True)
            )
            grad_hidden = mix * cot + grad_value
            ghid_ref[rows, :] = grad_hidden
            grad_attn = grad_hidden.astype(BF)
            n2_ref[rows, :] = grad_attn
            n2t_ref[:, rows] = att_ref[rows, :].T
            gvec_ref[2:3, :] += jnp.sum(grad_attn.astype(F32), axis=0, keepdims=True)
            gvec_ref[3:4, :] += jnp.sum(gb_ref[rows, :].astype(F32), axis=0, keepdims=True)
            gatt_ref[rows, :] = nt_dot(grad_attn, cols(wout_ref, 0, width // 128)).astype(BF)

        grad_attn_all = n2_ref[...]
        for r in range(width // 256):
            for k in range(width // 256):
                put_tiles(
                    gwout_ref, 16 * r, 2 * k,
                    nn_dot(
                        n2t_ref[256 * r : 256 * r + 256, :],
                        grad_attn_all[:, 256 * k : 256 * k + 256],
                    ).astype(BF),
                )


def middle(x_row, attended, cot_row, w_out, w_up, w_down, vectors, b_up, own_cot, coefficient):
    length, width = x_row.shape
    (up_array, up_rows), (down_array, down_first), (out_array, out_rows) = w_up, w_down, w_out
    out_first = out_array.shape[0] // out_rows - 1
    inner = b_up.shape[1]
    steps = inner // 256
    terms = coefficient.shape[0] - 1
    once = pl.Buffered(1)

    def const(shape):
        return pl.BlockSpec(shape, lambda i: (0,) * len(shape), pipeline_mode=once)

    rows = const((length, width))
    row_tiles, col_tiles = width // 16, width // 128
    return pl.pallas_call(
        middle_kernel,
        grid=(steps,),
        in_specs=[
            rows, rows, rows,
            pl.BlockSpec(
                (out_rows,) + out_array.shape[1:], lambda i: (out_first, 0, 0, 0, 0), pipeline_mode=once
            ),
            pl.BlockSpec((up_rows, up_array.shape[1], 2, 16, 128), lambda i: (0, 0, i, 0, 0)),
            pl.BlockSpec((16, col_tiles, 16, 128), lambda i: (i + down_first, 0, 0, 0)),
            const(vectors.shape),
            pl.BlockSpec((1, 256), lambda i: (0, i)),
            const(own_cot.shape),
            pl.BlockSpec(memory_space=pltpu.SMEM),
        ],
        out_specs=[
            pl.BlockSpec((terms // steps,) + own_cot.shape, lambda i: (i, 0, 0)),
            rows, rows, rows,
            pl.BlockSpec((row_tiles, 2, 16, 128), lambda i: (0, i, 0, 0)),
            pl.BlockSpec((16, col_tiles, 16, 128), lambda i: (i, 0, 0, 0)),
            const((row_tiles, col_tiles, 16, 128)),
            pl.BlockSpec((8, 256), lambda i: (0, i)),
            const((8, width)),
        ],
        out_shape=[
            jax.ShapeDtypeStruct((terms,) + own_cot.shape, F32),
            jax.ShapeDtypeStruct((length, width), BF),
            jax.ShapeDtypeStruct((length, width), BF),
            jax.ShapeDtypeStruct((length, width), F32),
            jax.ShapeDtypeStruct((row_tiles, inner // 128, 16, 128), BF),
            jax.ShapeDtypeStruct((inner // 16, col_tiles, 16, 128), BF),
            jax.ShapeDtypeStruct((row_tiles, col_tiles, 16, 128), BF),
            jax.ShapeDtypeStruct((8, inner), F32),
            jax.ShapeDtypeStruct((8, width), F32),
        ],
        scratch_shapes=[
            pltpu.VMEM((length, width), F32),
            pltpu.VMEM((length, width), BF),
            pltpu.VMEM((width, length), BF),
            pltpu.VMEM((length, width), BF),
            pltpu.VMEM((length, width), F32),
            pltpu.VMEM((length, width), F32),
            pltpu.VMEM((length, 256), BF),
            pltpu.VMEM((length, 256), BF),
        ],
        compiler_params=pltpu.CompilerParams(vmem_limit_bytes=VMEM_LIMIT),
        name="middle",
    )(x_row, attended, cot_row, out_array, up_array, down_array, vectors, b_up, own_cot, coefficient)


def last_kernel(
    x_ref, n1_ref, ghid_ref, gq_ref, gk_ref, gv_ref, w_ref, vec_ref,
    gx_ref, gw_ref, gb_ref, gvec_ref, n1t_ref, acc_ref,
):
    step = pl.program_id(0)
    steps = pl.num_programs(0)
    length, width = x_ref.shape
    tile = 256
    tiles = length // tile
    per_part = steps // 3

    @pl.when(step == 0)
    def _():
        @pl.loop(0, tiles)
        def _(t):
            rows = pl.ds(pl.multiple_of(t * tile, tile), tile)
            n1t_ref[:, rows] = n1_ref[rows, :].T
            acc_ref[rows, :] = jnp.zeros((tile, width), F32)

        gvec_ref[...] = jnp.zeros_like(gvec_ref)

    def one(grad_ref):
        grads = grad_ref[...]
        for r in range(width // 256):
            put_tiles(gw_ref, 16 * r, 0, nn_dot(n1t_ref[256 * r : 256 * r + 256, :], grads).astype(BF))
        gb_ref[0:1, :] = jnp.sum(grads.astype(F32), axis=0, keepdims=True)
        weight = cols(w_ref, 0, 2)

        @pl.loop(0, tiles)
        def _(t):
            rows = pl.ds(pl.multiple_of(t * tile, tile), tile)
            acc_ref[rows, :] += nt_dot(grad_ref[rows, :], weight)

    for part, grad_ref in enumerate((gq_ref, gk_ref, gv_ref)):
        pl.when(step // per_part == part)(partial(one, grad_ref))

    @pl.when(step == steps - 1)
    def _():
        @pl.loop(0, tiles)
        def _(t):
            rows = pl.ds(pl.multiple_of(t * tile, tile), tile)
            centered, inverse = norm_parts(x_ref[rows, :].astype(F32))
            normed = centered * inverse
            grad_norm = acc_ref[rows, :]
            gvec_ref[0:1, :] += jnp.sum(normed * grad_norm, axis=0, keepdims=True)
            gvec_ref[1:2, :] += jnp.sum(grad_norm, axis=0, keepdims=True)
            scaled = grad_norm * vec_ref[0:1, :]
            grad_value = inverse * (
                scaled
                - jnp.mean(scaled, axis=1, keepdims=True)
                - normed * jnp.mean(scaled * normed, axis=1, keepdims=True)
            )
            gx_ref[rows, :] = (ghid_ref[rows, :] + grad_value).astype(gx_ref.dtype)


def last(x_row, n1, grad_hidden, gq, gk, gv, w_qkv, vectors):
    length, width = x_row.shape
    array, lead = w_qkv
    steps = 3 * width // 256
    per_part = width // 256
    once = pl.Buffered(1)

    def const(shape):
        return pl.BlockSpec(shape, lambda i: (0,) * len(shape), pipeline_mode=once)

    def part_spec(part):
        return pl.BlockSpec(
            (length, 256), lambda i: (0, jnp.clip(i - part * per_part, 0, per_part - 1))
        )

    rows = const((length, width))
    row_tiles = width // 16
    return pl.pallas_call(
        last_kernel,
        grid=(steps,),
        in_specs=[
            rows, rows, rows, part_spec(0), part_spec(1), part_spec(2),
            pl.BlockSpec((lead, array.shape[1], 2, 16, 128), lambda i: (0, 0, i, 0, 0)),
            const(vectors.shape),
        ],
        out_specs=[
            rows,
            pl.BlockSpec((row_tiles, 2, 16, 128), lambda i: (0, i, 0, 0)),
            pl.BlockSpec((8, 256), lambda i: (0, i)),
            const((8, width)),
        ],
        out_shape=[
            jax.ShapeDtypeStruct((length, width), BF),
            jax.ShapeDtypeStruct((row_tiles, 3 * width // 128, 16, 128), BF),
            jax.ShapeDtypeStruct((8, 3 * width), F32),
            jax.ShapeDtypeStruct((8, width), F32),
        ],
        scratch_shapes=[pltpu.VMEM((width, length), BF), pltpu.VMEM((length, width), F32)],
        compiler_params=pltpu.CompilerParams(vmem_limit_bytes=VMEM_LIMIT),
        name="last",
    )(x_row, n1, grad_hidden, gq, gk, gv, array, vectors)


def history_step(hist_ref, cot_ref, c_ref, first_term, part_ref, dots_ref):
    group, tile, width = hist_ref.shape
    mixes = [c_ref[first_term + j] for j in range(group)]

    def chunk(r, dots):
        rows = pl.ds(pl.multiple_of(r * 16, 16), 16)
        total = part_ref[rows, :]
        cot = cot_ref[rows, :].astype(F32)
        new = []
        for j in range(group):
            past = hist_ref[j, rows, :].astype(F32)
            total = total + mixes[j] * past
            both = past * cot
            both = both[:8] + both[8:]
            added = dots[j]
            for k in range(width // 128):
                added = added + both[:, 128 * k : 128 * k + 128]
            new.append(added)
        part_ref[rows, :] = total
        return tuple(new)

    dots = lax.fori_loop(0, tile // 16, chunk, tuple(jnp.zeros((8, 128), F32) for _ in range(group)))
    for j in range(group):
        dots_ref[0, 8 * j : 8 * j + 8, :] = dots[j]


MESH_ID = pl.DeviceIdType.MESH


class Place:
    def __init__(self, depth):
        dp, tok = lax.axis_index("dp"), lax.axis_index("tok")
        self.depth = depth
        self.z, self.x, self.y, self.c = dp // 2, dp % 2, tok // 2, tok % 2
        self.dp, self.tok = dp, tok
        self.along_x = (self.z * 2 + 1 - self.x, tok)
        self.along_y = (dp, (1 - self.y) * 2 + self.c)
        self.along_c = (dp, self.y * 2 + 1 - self.c)
        self.near_z = ((self.z + 1 - 2 * (self.z % 2)) * 2 + self.x, tok)
        self.mid_z = ((depth - 1 - self.z) * 2 + self.x, tok)
        self.across = (dp, (1 - self.y) * 2 + 1 - self.c)

    def along_z(self, step):
        return (lax.rem(self.z + step, self.depth) * 2 + self.x, self.tok)

    def partners(self):
        steps = [self.along_z(r) for r in range(1, self.depth)]
        return [self.along_x, self.along_y, self.along_c, self.across] + steps

    def row_partners(self):
        return [self.along_c, self.along_y, self.across]


def greet(place):
    barrier = pltpu.get_barrier_semaphore()
    for partner in place.partners():
        pl.semaphore_signal(barrier, inc=1, device_id=partner, device_id_type=MESH_ID)
    pl.semaphore_wait(barrier, len(place.partners()))


def remote(src, dst, send, recv, target):
    return pltpu.make_async_remote_copy(
        src_ref=src, dst_ref=dst, send_sem=send, recv_sem=recv,
        device_id=target, device_id_type=MESH_ID,
    )


def gather_kernel(
    depth, items, spread, ahead, second_rows, hist_ref, cot_ref, c_ref, *refs,
):
    arrays = 1 + max(item[0] for item in items)
    blocks = refs[:arrays]
    rows_in = refs[arrays : arrays + 2]
    part_ref, dots_ref = refs[arrays + 2 : arrays + 4]
    gathered = refs[arrays + 4 : 2 * arrays + 4]
    rows_out = refs[2 * arrays + 4 : 2 * arrays + 6]
    z_send, z_recv, m_send, m_recv, c_send, c_recv, r_send, r_recv, local = refs[2 * arrays + 6 :]
    step = pl.program_id(0) * pl.num_programs(1) + pl.program_id(1)
    me = Place(depth)
    own = (me.z, me.x, me.y, me.c)
    span = rows_in[0].shape[1]

    inner = (me.z == 1) | (me.z == 2)
    half = me.z // 2

    def z_copy(i, hop):
        which, low, _, high = items[i]
        spot = pl.ds(low, high - low)
        sems = (z_send.at[i, hop], z_recv.at[i, hop])
        if hop == 0:
            return remote(blocks[which].at[spot], gathered[which].at[own + (spot,)], *sems, me.near_z)
        first_block = 2 * half if hop == 1 else 2 * (1 - half)
        view = gathered[which].at[pl.ds(first_block, 2), me.x, me.y, me.c, spot]
        return remote(view, view, *sems, me.mid_z if hop == 1 else me.near_z)

    def middle_copy(i, stage, part):
        which, low, mid, high = items[i]
        spot = pl.ds(low, mid - low) if part == 0 else pl.ds(mid, high - mid)
        every = slice(None)
        if stage == 0:
            index = (every, me.x, me.y, me.c, spot)
        elif part == 0:
            index = (every, every, me.y, me.c, spot)
        else:
            index = (every, me.x, every, me.c, spot)
        target = me.along_x if stage == part else me.along_y
        view = gathered[which].at[index]
        at = 2 * stage + part
        return remote(view, view, m_send.at[i, at], m_recv.at[i, at], target)

    def core_copy(i):
        which, low, _, high = items[i]
        every = slice(None)
        view = gathered[which].at[every, every, every, me.c, pl.ds(low, high - low)]
        return remote(view, view, c_send.at[i], c_recv.at[i], me.along_c)

    def row_copy(k, p):
        target = me.row_partners()[p]
        return remote(
            rows_in[k].at[target[1]], rows_out[k].at[pl.ds(me.tok * span, span)],
            r_send.at[k, p], r_recv.at[k, p], target,
        )

    def row_own(k):
        return pltpu.make_async_copy(
            rows_in[k].at[me.tok], rows_out[k].at[pl.ds(me.tok * span, span)], local.at[k]
        )

    def block_own(which):
        return pltpu.make_async_copy(blocks[which], gathered[which].at[own], local.at[2 + which])

    def parts(i):
        _, low, mid, high = items[i]
        return [part for part, size in ((0, mid - low), (1, high - mid)) if size]

    def begin():
        greet(me)
        for which in range(arrays):
            block_own(which).start()
        for i in range(min(ahead, len(items))):
            line(i)
        for k in range(2):
            row_own(k).start()
        rows(0)

    def line(i):
        z_copy(i, 0).start()

    def inner_hop(i):
        if i == 0:
            for which in range(arrays):
                block_own(which).wait()
        z_copy(i, 0).wait_recv()
        pl.when(inner)(lambda: z_copy(i, 1).start())

    def outer_hop(i):
        @pl.when(inner)
        def _():
            z_copy(i, 1).wait_recv()
            z_copy(i, 2).start()

    def rows(k):
        for p in range(3):
            row_copy(k, p).start()

    def first(i):
        if i + ahead < len(items):
            line(i + ahead)
        if i == second_rows:
            rows(1)
        pl.when(jnp.logical_not(inner))(lambda: z_copy(i, 2).wait_recv())
        for part in parts(i):
            middle_copy(i, 0, part).start()

    def second(i):
        for part in parts(i):
            middle_copy(i, 0, part).wait_recv()
            middle_copy(i, 1, part).start()

    def third(i):
        for part in parts(i):
            middle_copy(i, 1, part).wait_recv()
        core_copy(i).start()

    def finish():
        for i in range(len(items)):
            core_copy(i).wait_recv()
        for k in range(2):
            row_own(k).wait()
            for p in range(3):
                row_copy(k, p).wait()
        for i in range(len(items)):
            z_copy(i, 0).wait_send()

            @pl.when(inner)
            def _():
                z_copy(i, 1).wait_send()
                z_copy(i, 2).wait_send()

            for part in parts(i):
                middle_copy(i, 0, part).wait_send()
                middle_copy(i, 1, part).wait_send()
            core_copy(i).wait_send()

    stages = (inner_hop, outer_hop, first, second, third)
    work = []
    for i in range(len(items) + len(stages) - 1):
        for at, stage in enumerate(stages):
            if 0 <= i - at < len(items):
                work.append(partial(stage, i - at))
    work.append(finish)
    pl.when(step == 0)(begin)

    @pl.when(pl.program_id(1) == 0)
    def _():
        part_ref[...] = jnp.zeros_like(part_ref)

    group = hist_ref.shape[0]
    history_step(hist_ref, cot_ref, c_ref, pl.program_id(1) * group, part_ref, dots_ref)
    for at, one in enumerate(work):
        pl.when(step == spread[at])(one)


def gather(blocks, items, inputs, history, cotangent, coefficient, depth, ahead, second_rows):
    terms, tokens, width = history.shape
    row_count, span, _ = inputs.shape
    length = span * row_count
    tile, group = 128, 6
    steps = (tokens // tile) * (terms // group)
    work = 5 * len(items) + 1
    spread = [min(steps - 1, 1 + at * 1) for at in range(work)]
    spread[-1] = steps - 1
    n, arrays = len(items), len(blocks)
    hbm = pl.BlockSpec(memory_space=pl.ANY)
    dma = pltpu.SemaphoreType.DMA
    return pl.pallas_call(
        partial(gather_kernel, depth, items, spread, ahead, second_rows),
        grid=(tokens // tile, terms // group),
        in_specs=[
            pl.BlockSpec((group, tile, width), lambda t, j: (j, t, 0)),
            pl.BlockSpec((tile, width), lambda t, j: (t, 0)),
            pl.BlockSpec(memory_space=pltpu.SMEM),
        ]
        + [hbm] * (arrays + 2),
        out_specs=[
            pl.BlockSpec((tile, width), lambda t, j: (t, 0)),
            pl.BlockSpec((1, 8 * group, 128), lambda t, j: (t, j, 0)),
        ]
        + [hbm] * (arrays + 2),
        out_shape=[
            jax.ShapeDtypeStruct((tokens, width), F32),
            jax.ShapeDtypeStruct((tokens // tile, 8 * terms, 128), F32),
        ]
        + [jax.ShapeDtypeStruct((depth, 2, 2, 2) + b.shape, b.dtype) for b in blocks]
        + [jax.ShapeDtypeStruct((length, width), BF)] * 2,
        scratch_shapes=[
            dma((n, 3)), dma((n, 3)), dma((n, 4)), dma((n, 4)),
            dma((n,)), dma((n,)), dma((2, 3)), dma((2, 3)), dma((2 + arrays,)),
        ],
        compiler_params=pltpu.CompilerParams(
            vmem_limit_bytes=VMEM_LIMIT, collective_id=0, has_side_effects=True
        ),
        name="gather",
    )(history, cotangent.reshape(tokens, width), coefficient, *blocks, inputs, cotangent)


def finish_kernel(
    depth, sources, items, mid, small_ref, *refs,
):
    grads = refs[: len(sources)]
    rows_in = refs[len(sources) : len(sources) + 2]
    refs = refs[len(sources) + 2 :]
    out_ref, small_out, back_0, back_1 = refs[:4]
    rows_out = (back_0, back_1)
    (
        own_buf, core_buf, s1a, s1b, r1a, r1b, s2a, s2b, r2a, r2b, s3, r3,
        v_buf, v_recv, v_line,
        c_send, c_recv, m_send, m_recv, z_send, z_recv, r_send, r_recv, v_send, v_sem, local,
    ) = refs[4:]
    me = Place(depth)
    span = rows_out[0].shape[1]
    sends1, recvs1, sends2, recvs2 = (s1a, s1b), (r1a, r1b), (s2a, s2b), (r2a, r2b)
    width = items[0][2]
    tiles = (slice(0, mid), slice(mid, width))
    first_bit, second_bit = (me.y, me.x), (me.x, me.y)
    first_way, second_way = (me.along_y, me.along_x), (me.along_x, me.along_y)

    def pieces(i):
        group, low, count = items[i]
        at = 0
        for which, (of, lead) in enumerate(sources):
            if of == group:
                yield which, at, lead, pl.ds(low, count)
                at = at + lead

    def core_copies(i):
        for n, (which, at, lead, spot) in enumerate(pieces(i)):
            yield remote(
                grads[which].at[:, 1 - me.c, spot], core_buf.at[i, pl.ds(at, lead)],
                c_send.at[i, n], c_recv.at[i, n], me.along_c,
            )

    def own_copies(i):
        for n, (which, at, lead, spot) in enumerate(pieces(i)):
            yield pltpu.make_async_copy(
                grads[which].at[:, me.c, spot], own_buf.at[i, pl.ds(at, lead)], local.at[i, n]
            )

    def side_copy(i, part, stage):
        send, recv = (sends1, recvs1) if stage == 0 else (sends2, recvs2)
        way = (first_way, second_way)[stage][part]
        at = 2 * stage + part
        return remote(send[part].at[i], recv[part].at[i], m_send.at[i, at], m_recv.at[i, at], way)

    def line_copy(i, r):
        return remote(
            s3.at[i, r - 1], r3.at[i, r - 1], z_send.at[i, r - 1], z_recv.at[i, r - 1], me.along_z(r)
        )

    def row_copy(k, p):
        target = me.row_partners()[p]
        return remote(
            rows_in[k].at[pl.ds(target[1] * span, span)], rows_out[k].at[me.tok],
            r_send.at[k, p], r_recv.at[k, p], target,
        )

    def row_own(k):
        return pltpu.make_async_copy(
            rows_in[k].at[pl.ds(me.tok * span, span)], rows_out[k].at[me.tok], local.at[k, 2]
        )

    ways = (me.along_c, me.along_y, me.along_x)

    def small_copy(n):
        return remote(v_buf.at[n], v_recv.at[n], v_send.at[n], v_sem.at[n], ways[n])

    def small_line(r):
        return remote(
            v_buf.at[3], v_line.at[me.z], v_send.at[2 + r], v_sem.at[2 + r], me.along_z(r)
        )

    def begin():
        greet(me)
        v_buf[0] = small_ref[...]
        small_copy(0).start()
        for i in range(len(items)):
            for copy in core_copies(i):
                copy.start()
            for copy in own_copies(i):
                copy.start()
        for k in range(2):
            row_own(k).start()
        for p in range(3):
            row_copy(0, p).start()

    def core_stage(i):
        for copy in core_copies(i):
            copy.wait_recv()
        for copy in own_copies(i):
            copy.wait()

        for part in range(2):

            def one(j, _, part=part):
                slot = first_slot(part, j, 1 - first_bit[part])
                sends1[part][i, j] = pair_sum(i, part, slot).astype(BF)
                return 0

            lax.fori_loop(0, 2 * depth, one, 0)
            side_copy(i, part, 0).start()

    def first_slot(part, j, bit):
        return 2 * j + bit if part == 0 else (j // 2) * 4 + 2 * bit + j % 2

    def pair_sum(i, part, slot):
        spot = tiles[part]
        return own_buf[i, slot, spot].astype(F32) + core_buf[i, slot, spot].astype(F32)

    def plane_sum(i, part, j):
        slot = first_slot(part, j, first_bit[part])
        return pair_sum(i, part, slot) + recvs1[part][i, j].astype(F32)

    def first_stage(i):
        for part in range(2):
            side_copy(i, part, 0).wait_recv()

            def one(k, _, part=part):
                sends2[part][i, k] = plane_sum(i, part, 2 * k + 1 - second_bit[part]).astype(BF)
                return 0

            lax.fori_loop(0, depth, one, 0)
            side_copy(i, part, 1).start()

    def chip_sum(i, part, k):
        return plane_sum(i, part, 2 * k + second_bit[part]) + recvs2[part][i, k].astype(F32)

    def second_stage(i):
        for part in range(2):
            side_copy(i, part, 1).wait_recv()
        for r in range(1, depth):
            other = lax.rem(me.z + r, depth)
            for part in range(2):
                s3[i, r - 1, tiles[part]] = chip_sum(i, part, other).astype(BF)
            line_copy(i, r).start()

    def line_stage(i):
        for r in range(1, depth):
            line_copy(i, r).wait_recv()
        for part in range(2):
            total = chip_sum(i, part, me.z)
            for r in range(1, depth):
                total = total + r3[i, r - 1, tiles[part]].astype(F32)
            out_ref[i, tiles[part]] = total

    def small_stage(n):
        if n < 3:
            small_copy(n).wait_recv()
            v_buf[n + 1] = v_buf[n] + v_recv[n]
            if n < 2:
                small_copy(n + 1).start()
            else:
                v_line[me.z] = v_buf[3]
                for r in range(1, depth):
                    small_line(r).start()
            if n == 0:
                for p in range(3):
                    row_copy(1, p).start()
        else:
            for r in range(1, depth):
                small_line(r).wait_recv()
            total = v_line[0]
            for z in range(1, depth):
                total = total + v_line[z]
            small_out[...] = total

    def last_stage():
        for k in range(2):
            row_own(k).wait()
            for p in range(3):
                row_copy(k, p).wait()
        for n in range(3):
            small_copy(n).wait_send()
        for r in range(1, depth):
            small_line(r).wait_send()
        for i in range(len(items)):
            for copy in core_copies(i):
                copy.wait_send()
            for part in range(2):
                side_copy(i, part, 0).wait_send()
                side_copy(i, part, 1).wait_send()
            for r in range(1, depth):
                line_copy(i, r).wait_send()

    begin()
    stages = (core_stage, first_stage, second_stage, line_stage)
    for i in range(max(len(items) + len(stages) - 1, 4)):
        for at, stage in enumerate(stages):
            if 0 <= i - at < len(items):
                stage(i - at)
        if i < 4:
            small_stage(i)
    last_stage()


def finish(sources, items, mid, rows, small, row_count, depth):
    length, width = rows[0].shape
    span = length // row_count
    n = len(items)
    count = items[0][2]
    hbm = pl.BlockSpec(memory_space=pl.ANY)
    vmem = pl.BlockSpec(memory_space=pltpu.VMEM)
    dma = pltpu.SemaphoreType.DMA

    def tiles(lead, size):
        return pltpu.VMEM((n, lead, size, 16, 128), BF)

    sizes = (mid, count - mid)
    scratch = [tiles(4 * depth, count), tiles(4 * depth, count)]
    for lead in (2 * depth, depth):
        scratch += [tiles(lead, size) for size in sizes] * 2
    scratch += [tiles(depth - 1, count), tiles(depth - 1, count)]
    scratch += [pltpu.VMEM((4,) + small.shape, F32), pltpu.VMEM((3,) + small.shape, F32)]
    scratch += [pltpu.VMEM((depth,) + small.shape, F32)]
    scratch += [
        dma((n, 2)), dma((n, 2)), dma((n, 4)), dma((n, 4)), dma((n, depth - 1)), dma((n, depth - 1)),
        dma((2, 3)), dma((2, 3)), dma((2 + depth,)), dma((2 + depth,)), dma((n, 3)),
    ]
    return pl.pallas_call(
        partial(finish_kernel, depth, [(g, a.shape[0]) for g, a in sources], items, mid),
        in_specs=[vmem] + [hbm] * (len(sources) + 2),
        out_specs=[vmem, vmem, hbm, hbm],
        out_shape=[
            jax.ShapeDtypeStruct((n, count, 16, 128), F32),
            jax.ShapeDtypeStruct(small.shape, F32),
        ]
        + [jax.ShapeDtypeStruct((row_count, span, width), r.dtype) for r in rows],
        scratch_shapes=scratch,
        compiler_params=pltpu.CompilerParams(
            vmem_limit_bytes=VMEM_LIMIT, collective_id=1, has_side_effects=True
        ),
        name="finish",
    )(small, *[a for _, a in sources], *rows)


HALO = 2048


class Plan:
    def __init__(self, devices, shape_list):
        sizes = [math.prod(shape) for shape in shape_list]
        starts = [sum(sizes[:i]) for i in range(len(sizes))]
        self.total = sum(sizes)
        self.devices = devices
        self.own = self.total // devices
        self.matrices = [(starts[i], shape_list[i]) for i in (2, 4)]
        self.vectors = [(0, sizes[0] + sizes[1]), (starts[3], sizes[3]), (starts[5], sizes[5])]
        first, second = (math.prod(shape) for _, shape in self.matrices)
        self.block = (first + second) // devices
        self.split = devices * first // (first + second)
        self.rows = [
            shape[0] // n if n else 0
            for (_, shape), n in zip(self.matrices, (self.split, devices - self.split))
        ]
        self.fits = self.total % devices == 0 and (first + second) % devices == 0
        for (_, shape), n, rows in zip(
            self.matrices, (self.split, devices - self.split), self.rows
        ):
            self.fits = self.fits and n > 0 and rows * n == shape[0] and rows % 16 == 0
            self.fits = self.fits and rows * shape[1] == self.block
        self.owners = [at // self.own for at, _ in self.vectors]
        if self.fits:
            for s in range(devices):
                shift = self.block_start(s) - self.own * s
                self.fits = self.fits and -HALO <= shift <= HALO
                self.fits = self.fits and shift + self.block - self.own <= HALO
                self.fits = self.fits and self.own - self.block - shift <= HALO
            for (at, size), owner in zip(self.vectors, self.owners):
                self.fits = self.fits and at + size <= self.own * (owner + 1) + HALO
            self.fits = self.fits and len(set(self.owners)) == len(self.owners)

    def block_start(self, s):
        (first, _), (second, _) = self.matrices
        if isinstance(s, int):
            return first + self.block * s if s < self.split else second + self.block * (s - self.split)
        return jnp.where(
            s < self.split, first + self.block * s, second + self.block * (s - self.split)
        )

    def tile_shapes(self):
        return [
            (rows // 16, shape[1] // 128) for (_, shape), rows in zip(self.matrices, self.rows)
        ]

    def to_tiles(self, flat, s):
        forms = [
            flat.reshape(rt, 16, ct, 128).transpose(0, 2, 1, 3).reshape(rt * ct, 16, 128)
            for rt, ct in self.tile_shapes()
        ]
        return jnp.where(s < self.split, forms[0], forms[1])

    def from_tiles(self, tiles, s):
        forms = [
            tiles.reshape(rt, ct, 16, 128).transpose(0, 2, 1, 3).reshape(-1)
            for rt, ct in self.tile_shapes()
        ]
        return jnp.where(s < self.split, forms[0], forms[1])

    def vector_rows(self):
        return -(-max(size for _, size in self.vectors) // 1024) * 8

    def blocks(self, flat, before, after, s):
        room = self.vector_rows() * 128
        joined = jnp.concatenate([before, flat, after, jnp.zeros((room,), flat.dtype)])
        aligned = lax.dynamic_slice(
            joined, (HALO + self.block_start(s) - self.own * s,), (self.block,)
        )
        place = jnp.int32(0)
        for (at, _), owner in zip(self.vectors, self.owners):
            place = jnp.where(s == owner, at - self.own * owner, place)
        extra = lax.dynamic_slice(joined, (HALO + place,), (room,))
        return self.to_tiles(aligned, s), extra.reshape(-1, 128)

    def shard(self, aligned, before, after, vectors, s):
        room = self.vector_rows() * 128
        edge = jnp.zeros((room,), aligned.dtype)
        joined = jnp.concatenate([edge, before, aligned, after, edge])
        begin = self.block_start(s)
        for (at, size), value in zip(self.vectors, vectors):
            place = jnp.clip(room + HALO + at - begin, 0, joined.shape[0] - size)
            joined = lax.dynamic_update_slice(joined, value, (place,))
        return lax.dynamic_slice(joined, (room + HALO + self.own * s - begin,), (self.own,))


def neighbour_edges(values_list, count):
    axes = ("dp", "tok")
    tails = jnp.stack([v[-HALO:] for v in values_list])
    heads = jnp.stack([v[:HALO] for v in values_list])
    before = lax.ppermute(tails, axes, [(i, (i + 1) % count) for i in range(count)])
    after = lax.ppermute(heads, axes, [(i, (i - 1) % count) for i in range(count)])
    return before, after


def plans(devices):
    return Plan(devices, attention_shapes()), Plan(devices, feedforward_shapes())


def row_tables(lengths_row, length):
    places = jnp.arange(length, dtype=jnp.int32)
    segment, position = layout(lengths_row[None], places)
    lane = jnp.arange(128, dtype=jnp.int32) % HEAD_DIM
    half_dim = HEAD_DIM // 2
    frequency = jnp.exp(
        (lane % half_dim).astype(jnp.float32) * (-2.0 * math.log(10000.0) / HEAD_DIM)
    )
    angle = position[0].astype(jnp.float32)[:, None] * frequency[None, :]
    sine = jnp.where(lane < half_dim, -1.0, 1.0)[None, :] * jnp.sin(angle)
    return segment[0], jnp.cos(angle), sine


def row_shards(
    inputs,
    history,
    document_lengths,
    cotangent,
    attention_params,
    attention_first,
    attention_second,
    feedforward_params,
    feedforward_first,
    feedforward_second,
    mixing_offsets,
    mixing_first,
    mixing_second,
    step_count,
):
    row_count, span, width = inputs.shape
    tok_size = lax.axis_size("tok")
    devices = lax.axis_size("dp") * tok_size
    length = span * tok_size
    tokens_all = row_count * span * devices
    axes = ("dp", "tok")
    s = lax.axis_index(axes)
    plan_a, plan_f = plans(devices)
    reach = length // 2

    depth = lax.axis_size("dp") // 2
    tokens = row_count * span
    term_count = mixing_offsets.shape[0]
    coefficient = mixing_offsets + (jnp.arange(term_count) == term_count - 1).astype(F32)

    low_a, low_f = attention_params.astype(BF), feedforward_params.astype(BF)
    before, after = neighbour_edges([low_a, low_f], devices)
    tiles_a, extra_a = plan_a.blocks(low_a, before[0], after[0], s)
    tiles_f, extra_f = plan_f.blocks(low_f, before[1], after[1], s)
    extra = jnp.concatenate([extra_a, extra_f]).reshape(-1, 16, 128)
    count_a, count_f = tiles_a.shape[0], tiles_f.shape[0]
    got_f = lax.all_gather(tiles_f, axes, axis=0, tiled=False)
    part = count_a // 3
    items = [(1, 0, extra.shape[0], extra.shape[0])] + [
        (0, low, low + part // 4, low + part) for low in range(0, count_a, part)
    ]
    history_part, history_dots, got_a, got_e, x_row, cot_row = gather(
        [tiles_a, extra], items, inputs, history.reshape(term_count - 1, tokens, width), cotangent,
        coefficient, depth, 4, 1,
    )
    got_a = got_a.reshape(devices, count_a, 16, 128)
    extras = got_e.reshape(devices, -1).astype(F32)
    room_a = plan_a.vector_rows() * 128

    def pick(plan, which, at):
        return extras[plan.owners[which], at : at + plan.vectors[which][1]]

    gain_one, shift_one = jnp.split(pick(plan_a, 0, 0), 2)
    b_qkv, b_out = pick(plan_a, 1, 0), pick(plan_a, 2, 0)
    gain_two, shift_two = jnp.split(pick(plan_f, 0, room_a), 2)
    b_up, b_down = pick(plan_f, 1, room_a), pick(plan_f, 2, room_a)
    (rq, cq), (ro, co) = plan_a.tile_shapes()
    (ru, cu), (rd, cd) = plan_f.tile_shapes()
    w_qkv = (got_a.reshape(devices, rq, cq, 16, 128), plan_a.split)
    w_out = (got_a.reshape(devices, ro, co, 16, 128), devices - plan_a.split)
    w_up = (got_f.reshape(devices, ru, cu, 16, 128), plan_f.split)
    w_down = (got_f.reshape(devices * rd, cd, 16, 128), plan_f.split * rd // 16)

    def stack(vectors, wide):
        vectors = [jnp.pad(v, (0, wide - v.shape[0])) for v in vectors]
        vectors = vectors + [jnp.zeros((wide,), F32)] * (8 - len(vectors))
        return jnp.stack(vectors)

    own_lengths = lax.dynamic_index_in_dim(document_lengths, lax.axis_index("tok"), 0, False)
    segment, cosine, sine = row_tables(own_lengths, length)
    seg_col, seg_row = segment[:, None], segment[None, :]

    normed_one, queries, keys, values = project(
        x_row, w_qkv, stack([gain_one, shift_one, b_qkv], 3 * width), cosine, sine
    )
    attended, lse = row_attend(queries, keys, values, seg_col, seg_row, reach)
    grad_history, block_out, grad_attended, grad_hidden, gw_up, gw_down, gw_out, gb_up, gvec_two = middle(
        x_row, attended, cot_row, w_out, w_up, w_down,
        stack([gain_two, shift_two, b_out, b_down], width), b_up[None, :],
        cotangent.reshape(tokens, width), coefficient,
    )
    gq, gk, gv = row_attend_back(
        queries, keys, values, grad_attended, lse, seg_col, seg_row, cosine, sine, reach
    )
    grad_row, gw_qkv, gb_qkv, gvec_one = last(
        x_row, normed_one, grad_hidden, gq, gk, gv, w_qkv, stack([gain_one], width)
    )
    small = jnp.concatenate(
        [
            gvec_one[0], gvec_one[1], gb_qkv[0], gvec_two[2],
            gvec_two[0], gvec_two[1], gb_up[0], gvec_two[3],
            jnp.sum(history_dots.reshape(-1, term_count - 1, 8 * 128), axis=(0, 2)),
            jnp.sum(gvec_two[4])[None],
        ]
    )
    small_size = small.shape[0]
    small = jnp.pad(small, (0, -small_size % 1024)).reshape(-1, 128)
    scale = 1.0 / tokens_all
    sources = [
        (group, array.reshape(-1, 2, *shape))
        for group, array, shape in (
            (0, gw_qkv, tiles_a.shape), (0, gw_out, tiles_a.shape),
            (1, gw_up, tiles_f.shape), (1, gw_down, tiles_f.shape),
        )
    ]
    part_f = count_a // 2
    items = [(1, low, part_f) for low in range(0, count_f, part_f)]
    items = items + [(0, low, part_f) for low in range(0, count_a, part_f)]
    sums, small, block_back, grad_back = finish(
        sources, items, part_f * 5 // 18, [block_out, grad_row], small, row_count, depth
    )
    small = small.reshape(-1)[:small_size] / tokens_all
    sum_f = sums[: count_f // part_f].reshape(tiles_f.shape)
    sum_a = sums[count_f // part_f :].reshape(tiles_a.shape)
    mixed = history_part.reshape(row_count, span, width) + coefficient[-1] * block_back.astype(F32)
    grad_inputs = grad_back.astype(F32)
    flat_a = plan_a.from_tiles(sum_a * scale, s)
    flat_f = plan_f.from_tiles(sum_f * scale, s)
    before, after = neighbour_edges([flat_a, flat_f], devices)
    at = 0
    parts = []
    for plan in (plan_a, plan_f):
        for _, size in plan.vectors:
            parts.append(small[at : at + size])
            at = at + size
    attention_share = plan_a.shard(flat_a, before[0], after[0], parts[:3], s)
    feedforward_share = plan_f.shard(flat_f, before[1], after[1], parts[3:], s)
    mixing_grad = small[at:]

    count_now = step_count[0]
    attention_places = s * plan_a.own + jnp.arange(plan_a.own, dtype=jnp.int32)
    feedforward_places = s * plan_f.own + jnp.arange(plan_f.own, dtype=jnp.int32)
    attention_step = adam_update(
        attention_params, attention_share, attention_first, attention_second, count_now,
        decay_mask(attention_places, attention_shapes()),
    )
    feedforward_step = adam_update(
        feedforward_params, feedforward_share, feedforward_first, feedforward_second, count_now,
        decay_mask(feedforward_places, feedforward_shapes()),
    )
    mixing_step = adam_update(
        mixing_offsets, mixing_grad, mixing_first, mixing_second, count_now, 0.0
    )
    return (
        mixed.astype(BF),
        grad_inputs,
        grad_history.reshape(history.shape),
        *attention_step,
        *feedforward_step,
        *mixing_step,
    )


def shards(inputs, *others):
    row_count, span, width = inputs.shape
    tok_size = lax.axis_size("tok")
    devices = lax.axis_size("dp") * tok_size
    by_rows = row_count == tok_size == 4 and lax.axis_size("dp") == 8 and width == D
    if by_rows and all(plan.fits for plan in plans(devices)):
        return row_shards(inputs, *others)
    return general_shards(inputs, *others)


def solution(mesh):
    in_specs = (
        P("dp", "tok", None),
        P(None, "dp", "tok", None),
        P("dp", None),
        P("dp", "tok", None),
        P(("dp", "tok")),
        P(("dp", "tok")),
        P(("dp", "tok")),
        P(("dp", "tok")),
        P(("dp", "tok")),
        P(("dp", "tok")),
        P(),
        P(),
        P(),
        P(),
    )
    out_specs = (
        P("dp", "tok", None),
        P("dp", "tok", None),
        P(None, "dp", "tok", None),
        P(("dp", "tok")),
        P(("dp", "tok")),
        P(("dp", "tok")),
        P(("dp", "tok")),
        P(("dp", "tok")),
        P(("dp", "tok")),
        P(),
        P(),
        P(),
    )
    return jax.shard_map(shards, mesh=mesh, in_specs=in_specs, out_specs=out_specs, check_vma=False)
```

```python
from functools import partial
import math

import jax
import jax.numpy as jnp
from jax import lax
from jax.experimental import pallas as pl
from jax.experimental.pallas import tpu as pltpu
from jax.sharding import PartitionSpec as P

D = 768
HEADS = 12
HEAD_DIM = 64
FF = 3072
DOCS = 7


beta_first = 0.9
beta_second = 0.95
learning_rate = 0.05
decay_rate = 0.1
adam_epsilon = 1e-08
norm_epsilon = 1e-05
masked_score = -1e30


def layer_norm(values, gain, shift):
    centered = values - jnp.mean(values, axis=-1, keepdims=True)
    variance = jnp.mean(centered * centered, axis=-1, keepdims=True)
    return centered * lax.rsqrt(variance + norm_epsilon) * gain + shift


def rotate(values, position):
    half_dim = values.shape[-1] // 2
    frequency = jnp.exp(
        jnp.arange(half_dim, dtype=jnp.float32) * (-2.0 * math.log(10000.0) / values.shape[-1])
    )
    angle = position.astype(jnp.float32)[..., None] * frequency
    cosine = jnp.cos(angle)[..., None, :]
    sine = jnp.sin(angle)[..., None, :]
    first_half = values[..., :half_dim]
    second_half = values[..., half_dim:]
    return jnp.concatenate(
        [first_half * cosine - second_half * sine, second_half * cosine + first_half * sine],
        axis=-1,
    )


def turn_back(gradient_part, position):
    return jax.vjp(partial(rotate, position=position), gradient_part)[1](gradient_part)[0]


def layout(lengths_rows, places):
    ends = jnp.cumsum(lengths_rows, axis=1)
    starts = ends - lengths_rows
    doc_count = lengths_rows.shape[1] - 1
    inside = places[None, :, None] >= ends[:, None, :doc_count]
    segment = jnp.sum(inside.astype(jnp.int32), axis=2)
    labels = jnp.arange(doc_count + 1, dtype=jnp.int32)
    chosen = segment[:, :, None] == labels[None, None, :]
    begin = jnp.sum(jnp.where(chosen, starts[:, None, :], 0), axis=2)
    return (segment, places[None, :] - begin)


def allowed_mask(segment_row, first_row, query_count):
    query_place = first_row + jnp.arange(query_count, dtype=jnp.int32)
    key_place = jnp.arange(segment_row.shape[0], dtype=jnp.int32)
    query_segment = lax.dynamic_slice_in_dim(segment_row, first_row, query_count, 0)
    earlier = key_place[None, :] <= query_place[:, None]
    same_doc = segment_row[None, :] == query_segment[:, None]
    real_key = (segment_row[None, :] < DOCS) | (key_place[None, :] == query_place[:, None])
    return earlier & same_doc & real_key


def block_scores(queries, keys_all, segment_row, first_row):
    scores = jnp.einsum(
        "qhd,khd->hqk", queries, keys_all, preferred_element_type=jnp.float32
    ) * HEAD_DIM ** (-0.5)
    allowed = allowed_mask(segment_row, first_row, queries.shape[0])
    return jnp.where(allowed[None], scores, masked_score)


def attention_shapes():
    return [(D,), (D,), (D, 3 * D), (3 * D,), (D, D), (D,)]


def feedforward_shapes():
    return [(D,), (D,), (D, FF), (FF,), (FF, D), (D,)]


def unpack(flat_vector, shape_list):
    pieces = []
    offset_at = 0
    for piece_shape in shape_list:
        piece_size = math.prod(piece_shape)
        pieces.append(flat_vector[offset_at : offset_at + piece_size].reshape(piece_shape))
        offset_at = offset_at + piece_size
    return pieces


def decay_mask(places, shape_list):
    mask_values = jnp.zeros(places.shape, jnp.float32)
    offset_at = 0
    for piece_shape in shape_list:
        piece_size = math.prod(piece_shape)
        if len(piece_shape) == 2:
            inside = (places >= offset_at) & (places < offset_at + piece_size)
            mask_values = mask_values + inside.astype(jnp.float32)
        offset_at = offset_at + piece_size
    return mask_values * decay_rate


def adam_update(values, gradient, moment_one, moment_two, step_number, decay_values):
    first_new = beta_first * moment_one + (1.0 - beta_first) * gradient
    second_new = beta_second * moment_two + (1.0 - beta_second) * gradient * gradient
    power_now = step_number.astype(jnp.float32)
    fix_one = 1.0 - jnp.power(beta_first, power_now)
    fix_two = 1.0 - jnp.power(beta_second, power_now)
    step_size = first_new / fix_one / (jnp.sqrt(second_new / fix_two) + adam_epsilon)
    return (values - learning_rate * (step_size + decay_values * values), first_new, second_new)


def to_groups(values, subsets):
    full_shape = values.shape
    row_total = full_shape[0]
    half_width = full_shape[-1] // 2
    split_view = values.reshape(
        (subsets, row_total // subsets) + full_shape[1:-1] + (2, half_width)
    )
    moved = jnp.moveaxis(split_view, -2, 0)
    return moved.reshape((2 * subsets, row_total // subsets) + full_shape[1:-1] + (half_width,))


def from_groups(values, subsets):
    full_shape = values.shape
    split_view = values.reshape((2, subsets) + full_shape[1:])
    moved = jnp.moveaxis(split_view, 0, -2)
    return moved.reshape((subsets * full_shape[1],) + full_shape[2:-1] + (2 * full_shape[-1],))


def attend_rows(head_qkv, head_segment):
    item_count = head_qkv.shape[1]
    length_all = head_qkv.shape[2]
    group_width = head_qkv.shape[4]
    head_count = group_width // HEAD_DIM
    block_rows = min(512, length_all)
    block_count = length_all // block_rows
    rows_qkv = head_qkv.reshape(item_count, length_all, 3, head_count, HEAD_DIM)
    rows_segment = head_segment.reshape(item_count, length_all)

    def attend_one_block(block_index):
        row_index = block_index // block_count
        first_row = block_index % block_count * block_rows
        current = rows_qkv[row_index]
        queries = lax.dynamic_slice_in_dim(current[:, 0], first_row, block_rows, 0)
        masked = block_scores(queries, current[:, 1], rows_segment[row_index], first_row)
        top_score = jnp.max(masked, axis=2, keepdims=True)
        exponent = jnp.exp(masked - top_score)
        total_weight = jnp.sum(exponent, axis=2, keepdims=True)
        soft_weights = (exponent / total_weight).astype(jnp.bfloat16)
        attended = jnp.einsum(
            "hqk,khd->qhd", soft_weights, current[:, 2], preferred_element_type=jnp.float32
        )
        log_total = (top_score + jnp.log(total_weight))[:, :, 0]
        return (attended.reshape(block_rows, group_width).astype(jnp.bfloat16), log_total)

    outputs, log_totals = lax.map(
        attend_one_block, jnp.arange(item_count * block_count, dtype=jnp.int32)
    )
    return (
        outputs.reshape(1, item_count, length_all, group_width),
        log_totals.reshape(1, item_count, block_count, head_count, block_rows),
    )


def attend_back(head_qkv, head_segment, log_totals, head_grads):
    item_count = head_qkv.shape[1]
    length_all = head_qkv.shape[2]
    group_width = head_qkv.shape[4]
    head_count = group_width // HEAD_DIM
    block_rows = min(512, length_all)
    block_count = length_all // block_rows
    scale_value = HEAD_DIM ** (-0.5)

    def one_row(pieces):
        current, segment_row, log_row, grad_row = pieces
        keys_all = current[:, 1]
        values_all = current[:, 2]

        def one_one_block(carried, block_index):
            first_row = block_index * block_rows
            queries = lax.dynamic_slice_in_dim(current[:, 0], first_row, block_rows, 0)
            grad_block = lax.dynamic_slice_in_dim(grad_row, first_row, block_rows, 0)
            masked = block_scores(queries, keys_all, segment_row, first_row)
            soft_weights = jnp.exp(masked - log_row[block_index][:, :, None])
            grad_weights = jnp.einsum(
                "qhd,khd->hqk", grad_block, values_all, preferred_element_type=jnp.float32
            )
            inner_sum = jnp.sum(soft_weights * grad_weights, axis=2, keepdims=True)
            grad_scores = (soft_weights * (grad_weights - inner_sum)).astype(jnp.bfloat16)
            grad_query = (
                jnp.einsum(
                    "hqk,khd->qhd", grad_scores, keys_all, preferred_element_type=jnp.float32
                )
                * scale_value
            )
            grad_key = (
                carried[0]
                + jnp.einsum(
                    "hqk,qhd->khd", grad_scores, queries, preferred_element_type=jnp.float32
                )
                * scale_value
            )
            grad_value = carried[1] + jnp.einsum(
                "hqk,qhd->khd",
                soft_weights.astype(jnp.bfloat16),
                grad_block,
                preferred_element_type=jnp.float32,
            )
            return ((grad_key, grad_value), grad_query)

        empty_grad = jnp.zeros((length_all, head_count, HEAD_DIM), jnp.float32)
        (grad_key, grad_value), grad_query = lax.scan(
            one_one_block, (empty_grad, empty_grad), jnp.arange(block_count, dtype=jnp.int32)
        )
        grad_query = grad_query.reshape(length_all, head_count, HEAD_DIM)
        return jnp.stack([grad_query, grad_key, grad_value], axis=1).astype(jnp.bfloat16)

    row_grads = lax.map(
        one_row,
        (
            head_qkv.reshape(item_count, length_all, 3, head_count, HEAD_DIM),
            head_segment.reshape(item_count, length_all),
            log_totals.reshape(item_count, block_count, head_count, block_rows),
            head_grads.reshape(item_count, length_all, head_count, HEAD_DIM),
        ),
    )
    return row_grads.reshape(1, item_count, length_all, 3, group_width)


def general_shards(
    inputs,
    history,
    document_lengths,
    cotangent,
    attention_params,
    attention_first,
    attention_second,
    feedforward_params,
    feedforward_first,
    feedforward_second,
    mixing_offsets,
    mixing_first,
    mixing_second,
    step_count,
):
    row_count, token_span, model_width = inputs.shape
    subsets = lax.axis_size("tok") // 2
    per_device = row_count // subsets
    tokens_all = row_count * token_span * lax.axis_size("dp") * lax.axis_size("tok")
    attention_flat, feedforward_flat = (
        lax.all_gather(attention_params.astype(jnp.bfloat16), ("dp", "tok"), axis=0, tiled=True),
        lax.all_gather(feedforward_params.astype(jnp.bfloat16), ("dp", "tok"), axis=0, tiled=True),
    )
    gain_one, shift_one, w_qkv, b_qkv, w_out, b_out = unpack(attention_flat, attention_shapes())
    gain_two, shift_two, w_up, b_up, w_down, b_down = unpack(feedforward_flat, feedforward_shapes())
    gain_one = gain_one.astype(jnp.float32)
    shift_one = shift_one.astype(jnp.float32)
    gain_two = gain_two.astype(jnp.float32)
    shift_two = shift_two.astype(jnp.float32)
    places = lax.axis_index("tok") * token_span + jnp.arange(token_span, dtype=jnp.int32)
    segment, position = layout(document_lengths, places)
    current = inputs.astype(jnp.float32)
    normed_one = layer_norm(current, gain_one, shift_one).astype(jnp.bfloat16)
    project = jnp.dot(normed_one, w_qkv, preferred_element_type=jnp.float32) + b_qkv.astype(
        jnp.float32
    )
    project = project.reshape(row_count, token_span, 3, HEADS, HEAD_DIM)
    queries = rotate(project[:, :, 0], position)
    keys_all = rotate(project[:, :, 1], position)
    packed = jnp.stack([queries, keys_all, project[:, :, 2]], axis=2).astype(jnp.bfloat16)
    send_qkv = to_groups(packed.reshape(row_count, token_span, 3, model_width), subsets)
    send_segment = jnp.broadcast_to(
        segment.reshape(1, subsets, per_device, token_span), (2, subsets, per_device, token_span)
    ).reshape(2 * subsets, per_device, token_span)
    head_qkv = lax.all_to_all(send_qkv, "tok", split_axis=0, concat_axis=2, tiled=True)
    head_segment = lax.all_to_all(send_segment, "tok", split_axis=0, concat_axis=2, tiled=True)
    outputs, log_totals = attend_rows(head_qkv, head_segment)
    returned = lax.all_to_all(outputs, "tok", split_axis=2, concat_axis=0, tiled=True)
    returned, head_qkv, head_segment, log_totals = (returned, head_qkv, head_segment, log_totals)
    attended = from_groups(returned, subsets)
    hidden = (
        current
        + jnp.dot(attended, w_out, preferred_element_type=jnp.float32)
        + b_out.astype(jnp.float32)
    )
    normed_two = layer_norm(hidden, gain_two, shift_two).astype(jnp.bfloat16)
    up_value = jnp.dot(normed_two, w_up, preferred_element_type=jnp.float32) + b_up.astype(
        jnp.float32
    )
    active = jax.nn.gelu(up_value).astype(jnp.bfloat16)
    block_out = (
        hidden
        + jnp.dot(active, w_down, preferred_element_type=jnp.float32)
        + b_down.astype(jnp.float32)
    )
    term_count = mixing_offsets.shape[0]
    coefficient = mixing_offsets + (jnp.arange(term_count) == term_count - 1).astype(jnp.float32)
    history_part = jnp.einsum(
        "j,jrtd->rtd", coefficient[:-1], history, preferred_element_type=jnp.float32
    )
    mixed = (history_part + coefficient[-1] * block_out).astype(jnp.bfloat16)
    grad_mixed = cotangent.astype(jnp.float32)
    grad_history = coefficient[:-1, None, None, None] * grad_mixed[None]
    history_terms = jnp.einsum(
        "jrtd,rtd->j", history, grad_mixed, preferred_element_type=jnp.float32
    )
    mixing_terms = jnp.concatenate([history_terms, jnp.sum(block_out * grad_mixed)[None]])
    mixing_grad = lax.psum(mixing_terms, ("dp", "tok")) / tokens_all
    grad_block = coefficient[-1] * grad_mixed
    grad_branch = grad_block.astype(jnp.bfloat16)
    grad_w_down = jnp.einsum("rtf,rtd->fd", active, grad_branch, preferred_element_type=jnp.float32)
    grad_b_down = jnp.sum(grad_branch.astype(jnp.float32), axis=(0, 1))
    grad_active = jnp.einsum("rtd,fd->rtf", grad_branch, w_down, preferred_element_type=jnp.float32)
    grad_up = jax.vjp(jax.nn.gelu, up_value)[1](grad_active)[0].astype(jnp.bfloat16)
    grad_w_up = jnp.einsum("rtd,rtf->df", normed_two, grad_up, preferred_element_type=jnp.float32)
    grad_b_up = jnp.sum(grad_up.astype(jnp.float32), axis=(0, 1))
    grad_normed_two = jnp.einsum("rtf,df->rtd", grad_up, w_up, preferred_element_type=jnp.float32)
    grad_hidden_norm, grad_gain_two, grad_shift_two = jax.vjp(
        layer_norm, hidden, gain_two, shift_two
    )[1](grad_normed_two)
    grad_hidden = grad_block + grad_hidden_norm
    feedforward_grad = jnp.concatenate(
        [
            grad_gain_two,
            grad_shift_two,
            grad_w_up.reshape(-1),
            grad_b_up,
            grad_w_down.reshape(-1),
            grad_b_down,
        ]
    )
    feedforward_share = lax.psum_scatter(
        feedforward_grad, ("dp", "tok"), scatter_dimension=0, tiled=True
    )
    grad_attn = grad_hidden.astype(jnp.bfloat16)
    grad_w_out = jnp.einsum("rtd,rte->de", attended, grad_attn, preferred_element_type=jnp.float32)
    grad_b_out = jnp.sum(grad_attn.astype(jnp.float32), axis=(0, 1))
    grad_attended = jnp.einsum(
        "rte,de->rtd", grad_attn, w_out, preferred_element_type=jnp.float32
    ).astype(jnp.bfloat16)
    head_grads = lax.all_to_all(
        to_groups(grad_attended, subsets), "tok", split_axis=0, concat_axis=2, tiled=True
    )
    head_back = attend_back(head_qkv, head_segment, log_totals, head_grads)
    token_back = from_groups(
        lax.all_to_all(head_back, "tok", split_axis=2, concat_axis=0, tiled=True), subsets
    )
    token_back = token_back.astype(jnp.float32).reshape(row_count, token_span, 3, HEADS, HEAD_DIM)
    grad_project = jnp.stack(
        [
            turn_back(token_back[:, :, 0], position),
            turn_back(token_back[:, :, 1], position),
            token_back[:, :, 2],
        ],
        axis=2,
    )
    grad_project = grad_project.reshape(row_count, token_span, 3 * model_width).astype(jnp.bfloat16)
    grad_w_qkv = jnp.einsum(
        "rtd,rte->de", normed_one, grad_project, preferred_element_type=jnp.float32
    )
    grad_b_qkv = jnp.sum(grad_project.astype(jnp.float32), axis=(0, 1))
    grad_normed_one = jnp.einsum(
        "rte,de->rtd", grad_project, w_qkv, preferred_element_type=jnp.float32
    )
    grad_current, grad_gain_one, grad_shift_one = jax.vjp(layer_norm, current, gain_one, shift_one)[
        1
    ](grad_normed_one)
    grad_inputs = grad_hidden + grad_current
    attention_grad = jnp.concatenate(
        [
            grad_gain_one,
            grad_shift_one,
            grad_w_qkv.reshape(-1),
            grad_b_qkv,
            grad_w_out.reshape(-1),
            grad_b_out,
        ]
    )
    attention_share = lax.psum_scatter(
        attention_grad, ("dp", "tok"), scatter_dimension=0, tiled=True
    )
    count_now = step_count[0]
    shard_index = lax.axis_index(("dp", "tok"))
    attention_places = shard_index * attention_params.shape[0] + jnp.arange(
        attention_params.shape[0], dtype=jnp.int32
    )
    feedforward_places = shard_index * feedforward_params.shape[0] + jnp.arange(
        feedforward_params.shape[0], dtype=jnp.int32
    )
    attention_step = adam_update(
        attention_params,
        attention_share / tokens_all,
        attention_first,
        attention_second,
        count_now,
        decay_mask(attention_places, attention_shapes()),
    )
    feedforward_step = adam_update(
        feedforward_params,
        feedforward_share / tokens_all,
        feedforward_first,
        feedforward_second,
        count_now,
        decay_mask(feedforward_places, feedforward_shapes()),
    )
    mixing_step = adam_update(
        mixing_offsets, mixing_grad, mixing_first, mixing_second, count_now, 0.0
    )
    return (
        mixed,
        grad_inputs,
        grad_history,
        attention_step[0],
        attention_step[1],
        attention_step[2],
        feedforward_step[0],
        feedforward_step[1],
        feedforward_step[2],
        mixing_step[0],
        mixing_step[1],
        mixing_step[2],
    )


VMEM_LIMIT = 58 * 1024 * 1024
BF = jnp.bfloat16
F32 = jnp.float32


def cols(ref, first, count):
    lead = math.prod(ref.shape[:-3]) * ref.shape[-2]
    pieces = []
    for at in range(first, first + count):
        index = (slice(None),) * (len(ref.shape) - 3) + (at,)
        pieces.append(ref[index].reshape(lead, 128))
    return pieces[0] if count == 1 else jnp.concatenate(pieces, axis=1)


def put_tiles(ref, row_at, col_at, value):
    rows, width = value.shape
    for at in range(width // 128):
        ref[pl.ds(row_at, rows // 16), col_at + at] = value[:, 128 * at : 128 * at + 128].reshape(
            rows // 16, 16, 128
        )


def norm_parts(values):
    mean = jnp.mean(values, axis=1, keepdims=True)
    centered = values - mean
    inverse = lax.rsqrt(jnp.mean(centered * centered, axis=1, keepdims=True) + norm_epsilon)
    return centered, inverse


def nt_dot(left, right):
    return lax.dot_general(left, right, (((1,), (1,)), ((), ())), preferred_element_type=F32)


def nn_dot(left, right):
    return lax.dot_general(left, right, (((1,), (0,)), ((), ())), preferred_element_type=F32)


def swap_halves(values):
    width = values.shape[1]
    lane = lax.broadcasted_iota(jnp.int32, values.shape, 1)
    return jnp.where(
        lane % HEAD_DIM < HEAD_DIM // 2,
        pltpu.roll(values, width - HEAD_DIM // 2, 1),
        pltpu.roll(values, HEAD_DIM // 2, 1),
    )


def key_range(block, block_rows, reach):
    return max(0, block * block_rows - reach), (block + 1) * block_rows


def fill_bias(bias_ref, seg_col_ref, seg_row_ref, block_rows, reach):
    length = seg_row_ref.shape[1]
    at = 0
    for block in range(length // block_rows):
        low, high = key_range(block, block_rows, reach)
        shape = (high - low, block_rows)
        key_place = low + lax.broadcasted_iota(jnp.int32, shape, 0)
        query_place = block * block_rows + lax.broadcasted_iota(jnp.int32, shape, 1)
        key_seg = seg_col_ref[low:high, :]
        query_seg = seg_row_ref[:, block * block_rows : (block + 1) * block_rows]
        allowed = (key_place <= query_place) & (key_seg == query_seg)
        allowed = allowed & ((key_seg < DOCS) | (key_place == query_place))
        bias_ref[at : at + high - low, :] = jnp.where(allowed, 0.0, masked_score)
        at = at + high - low


def bias_rows(length, block_rows, reach):
    return sum(
        high - low
        for low, high in (key_range(b, block_rows, reach) for b in range(length // block_rows))
    )


def head_mask(values, head):
    lane = lax.broadcasted_iota(jnp.int32, values.shape, 1)
    keep = lane < HEAD_DIM if head == 0 else lane >= HEAD_DIM
    return jnp.where(keep, values, jnp.zeros_like(values))


gelu_root = math.sqrt(2.0 / math.pi)


def middle_kernel(
    x_ref, att_ref, cot_ref, wout_ref, wup_ref, wdown_ref, vec_ref, bup_ref, own_cot_ref, c_ref,
    ghist_ref, bout_ref, gatt_ref, ghid_ref, gwup_ref, gwdown_ref, gwout_ref, gbup_ref, gvec_ref,
    hidden_ref, n2_ref, n2t_ref, gb_ref, acc_out, acc_gn, act_ref, gup_ref,
):
    step = pl.program_id(0)
    steps = pl.num_programs(0)
    length, width = x_ref.shape
    tile = 256
    tiles = length // tile
    mix = c_ref[c_ref.shape[0] - 1]
    group = ghist_ref.shape[0]

    @pl.when(step == 0)
    def _():
        @pl.loop(0, tiles)
        def _(t):
            rows = pl.ds(pl.multiple_of(t * tile, tile), tile)
            attended = att_ref[rows, :]
            hidden = x_ref[rows, :].astype(F32) + nn_dot(attended, cols(wout_ref, 0, width // 128))
            hidden = hidden + vec_ref[2:3, :]
            hidden_ref[rows, :] = hidden
            centered, inverse = norm_parts(hidden)
            normed = (centered * inverse * vec_ref[0:1, :] + vec_ref[1:2, :]).astype(BF)
            n2_ref[rows, :] = normed
            n2t_ref[:, rows] = normed.T
            gb_ref[rows, :] = (mix * cot_ref[rows, :].astype(F32)).astype(BF)
            acc_out[rows, :] = jnp.zeros((tile, width), F32)
            acc_gn[rows, :] = jnp.zeros((tile, width), F32)

        gvec_ref[...] = jnp.zeros_like(gvec_ref)

    w_up = cols(wup_ref, 0, 2)
    w_down = cols(wdown_ref, 0, width // 128)
    gbup_ref[...] = jnp.zeros_like(gbup_ref)

    @pl.loop(0, tiles)
    def _(t):
        rows = pl.ds(pl.multiple_of(t * tile, tile), tile)
        up = nn_dot(n2_ref[rows, :], w_up) + bup_ref[0:1, :]
        square = up * up
        turn = jnp.tanh(gelu_root * up * (1.0 + 0.044715 * square))
        half = 0.5 * (1.0 + turn)
        active = (up * half).astype(BF)
        act_ref[rows, :] = active
        acc_out[rows, :] += nn_dot(active, w_down)
        slope = half + (0.5 * gelu_root) * up * (1.0 - turn * turn) * (
            1.0 + (3.0 * 0.044715) * square
        )
        grad_up = (nt_dot(gb_ref[rows, :], w_down) * slope).astype(BF)
        gup_ref[rows, :] = grad_up
        acc_gn[rows, :] += nt_dot(grad_up, w_up)
        gbup_ref[0:1, :] += jnp.sum(grad_up.astype(F32), axis=0, keepdims=True)
        own_cot = own_cot_ref[rows, :].astype(F32)
        for j in range(group):
            ghist_ref[j, rows, :] = c_ref[step * group + j] * own_cot

    grad_up_all = gup_ref[...]
    for r in range(width // 256):
        put_tiles(
            gwup_ref, 16 * r, 0, nn_dot(n2t_ref[256 * r : 256 * r + 256, :], grad_up_all).astype(BF)
        )
    active_turned = act_ref[...].T
    for r in range(width // 256):
        put_tiles(
            gwdown_ref, 0, 2 * r, nn_dot(active_turned, gb_ref[:, 256 * r : 256 * r + 256]).astype(BF)
        )

    @pl.when(step == steps - 1)
    def _():
        @pl.loop(0, tiles)
        def _(t):
            rows = pl.ds(pl.multiple_of(t * tile, tile), tile)
            hidden = hidden_ref[rows, :]
            cot = cot_ref[rows, :].astype(F32)
            block_out = hidden + acc_out[rows, :] + vec_ref[3:4, :]
            bout_ref[rows, :] = block_out.astype(bout_ref.dtype)
            gvec_ref[4:5, :] += jnp.sum(block_out * cot, axis=0, keepdims=True)
            centered, inverse = norm_parts(hidden)
            normed = centered * inverse
            grad_norm = acc_gn[rows, :]
            gvec_ref[0:1, :] += jnp.sum(normed * grad_norm, axis=0, keepdims=True)
            gvec_ref[1:2, :] += jnp.sum(grad_norm, axis=0, keepdims=True)
            scaled = grad_norm * vec_ref[0:1, :]
            grad_value = inverse * (
                scaled
                - jnp.mean(scaled, axis=1, keepdims=True)
                - normed * jnp.mean(scaled * normed, axis=1, keepdims=True)
            )
            grad_hidden = mix * cot + grad_value
            ghid_ref[rows, :] = grad_hidden
            grad_attn = grad_hidden.astype(BF)
            n2_ref[rows, :] = grad_attn
            n2t_ref[:, rows] = att_ref[rows, :].T
            gvec_ref[2:3, :] += jnp.sum(grad_attn.astype(F32), axis=0, keepdims=True)
            gvec_ref[3:4, :] += jnp.sum(gb_ref[rows, :].astype(F32), axis=0, keepdims=True)
            gatt_ref[rows, :] = nt_dot(grad_attn, cols(wout_ref, 0, width // 128)).astype(BF)

        grad_attn_all = n2_ref[...]
        for r in range(width // 256):
            for k in range(width // 256):
                put_tiles(
                    gwout_ref, 16 * r, 2 * k,
                    nn_dot(
                        n2t_ref[256 * r : 256 * r + 256, :],
                        grad_attn_all[:, 256 * k : 256 * k + 256],
                    ).astype(BF),
                )


def middle(x_row, attended, cot_row, w_out, w_up, w_down, vectors, b_up, own_cot, coefficient):
    length, width = x_row.shape
    (up_array, up_rows), (down_array, down_first), (out_array, out_rows) = w_up, w_down, w_out
    out_first = out_array.shape[0] // out_rows - 1
    inner = b_up.shape[1]
    steps = inner // 256
    terms = coefficient.shape[0] - 1
    once = pl.Buffered(1)

    def const(shape):
        return pl.BlockSpec(shape, lambda i: (0,) * len(shape), pipeline_mode=once)

    rows = const((length, width))
    row_tiles, col_tiles = width // 16, width // 128
    return pl.pallas_call(
        middle_kernel,
        grid=(steps,),
        in_specs=[
            rows, rows, rows,
            pl.BlockSpec(
                (out_rows,) + out_array.shape[1:], lambda i: (out_first, 0, 0, 0, 0), pipeline_mode=once
            ),
            pl.BlockSpec((up_rows, up_array.shape[1], 2, 16, 128), lambda i: (0, 0, i, 0, 0)),
            pl.BlockSpec((16, col_tiles, 16, 128), lambda i: (i + down_first, 0, 0, 0)),
            const(vectors.shape),
            pl.BlockSpec((1, 256), lambda i: (0, i)),
            const(own_cot.shape),
            pl.BlockSpec(memory_space=pltpu.SMEM),
        ],
        out_specs=[
            pl.BlockSpec((terms // steps,) + own_cot.shape, lambda i: (i, 0, 0)),
            rows, rows, rows,
            pl.BlockSpec((row_tiles, 2, 16, 128), lambda i: (0, i, 0, 0)),
            pl.BlockSpec((16, col_tiles, 16, 128), lambda i: (i, 0, 0, 0)),
            const((row_tiles, col_tiles, 16, 128)),
            pl.BlockSpec((8, 256), lambda i: (0, i)),
            const((8, width)),
        ],
        out_shape=[
            jax.ShapeDtypeStruct((terms,) + own_cot.shape, F32),
            jax.ShapeDtypeStruct((length, width), BF),
            jax.ShapeDtypeStruct((length, width), BF),
            jax.ShapeDtypeStruct((length, width), F32),
            jax.ShapeDtypeStruct((row_tiles, inner // 128, 16, 128), BF),
            jax.ShapeDtypeStruct((inner // 16, col_tiles, 16, 128), BF),
            jax.ShapeDtypeStruct((row_tiles, col_tiles, 16, 128), BF),
            jax.ShapeDtypeStruct((8, inner), F32),
            jax.ShapeDtypeStruct((8, width), F32),
        ],
        scratch_shapes=[
            pltpu.VMEM((length, width), F32),
            pltpu.VMEM((length, width), BF),
            pltpu.VMEM((width, length), BF),
            pltpu.VMEM((length, width), BF),
            pltpu.VMEM((length, width), F32),
            pltpu.VMEM((length, width), F32),
            pltpu.VMEM((length, 256), BF),
            pltpu.VMEM((length, 256), BF),
        ],
        compiler_params=pltpu.CompilerParams(vmem_limit_bytes=VMEM_LIMIT),
        name="middle",
    )(x_row, attended, cot_row, out_array, up_array, down_array, vectors, b_up, own_cot, coefficient)


def history_step(hist_ref, cot_ref, c_ref, first_term, part_ref, dots_ref):
    group, tile, width = hist_ref.shape
    mixes = [c_ref[first_term + j] for j in range(group)]

    def chunk(r, dots):
        rows = pl.ds(pl.multiple_of(r * 16, 16), 16)
        total = part_ref[rows, :]
        cot = cot_ref[rows, :].astype(F32)
        new = []
        for j in range(group):
            past = hist_ref[j, rows, :].astype(F32)
            total = total + mixes[j] * past
            both = past * cot
            both = both[:8] + both[8:]
            added = dots[j]
            for k in range(width // 128):
                added = added + both[:, 128 * k : 128 * k + 128]
            new.append(added)
        part_ref[rows, :] = total
        return tuple(new)

    dots = lax.fori_loop(0, tile // 16, chunk, tuple(jnp.zeros((8, 128), F32) for _ in range(group)))
    for j in range(group):
        dots_ref[0, 8 * j : 8 * j + 8, :] = dots[j]


gather_cuts, gather_share, enter_share = 2, 0.5, 3
gather_steps = ((2, 3, 3, 4), (9, 9, 10), (15, 16, 18), (19,), (23, 24, 27), (28,), (31,))
enter_first_steps, enter_second_steps, enter_rows_step = (4, 7, 10, 13), (16, 19, 23, 27), 14
leave_steps, leave_share, leave_rows_steps = (4, 11, 18, 25, 31, 34, 36), 3, (0, 11, 18)
MESH_ID = pl.DeviceIdType.MESH
DMA = pltpu.SemaphoreType.DMA
HBM = pl.BlockSpec(memory_space=pl.ANY)
EVERY = slice(None)


class Place:
    def __init__(self, depth):
        dp, tok = lax.axis_index("dp"), lax.axis_index("tok")
        self.depth = depth
        self.z, self.x, self.y, self.c = dp // 2, dp % 2, tok // 2, tok % 2
        self.tok = tok
        self.along_x = (self.z * 2 + 1 - self.x, tok)
        self.along_y = (dp, (1 - self.y) * 2 + self.c)
        self.along_c = (dp, self.y * 2 + 1 - self.c)
        self.across = (dp, (1 - self.y) * 2 + 1 - self.c)
        self.near_z = ((self.z + 1 - 2 * (self.z % 2)) * 2 + self.x, tok)
        self.mid_z = ((depth - 1 - self.z) * 2 + self.x, tok)

    def along_z(self, step):
        return (lax.rem(self.z + step, self.depth) * 2 + self.x, self.tok)

    def row_partners(self):
        return [self.along_c, self.along_y, self.across]

    def greet(self):
        partners = [self.along_x] + self.row_partners()
        partners = partners + [self.along_z(r) for r in range(1, self.depth)]
        barrier = pltpu.get_barrier_semaphore()
        for partner in partners:
            pl.semaphore_signal(barrier, inc=1, device_id=partner, device_id_type=MESH_ID)
        pl.semaphore_wait(barrier, len(partners))


def remote(src, dst, send, recv, target):
    return pltpu.make_async_remote_copy(
        src_ref=src, dst_ref=dst, send_sem=send, recv_sem=recv,
        device_id=target, device_id_type=MESH_ID,
    )


class LineGather:
    def __init__(self, me, items, blocks, spots, sems):
        self.me, self.items, self.blocks, self.spots = me, items, blocks, spots
        self.send, self.recv, self.local = sems
        self.inner = (me.z == 1) | (me.z == 2)

    def scratch(items, arrays):
        return [DMA((len(items), 3)), DMA((len(items), 3)), DMA((arrays,))]

    def copy(self, i, hop):
        which, low, count = self.items[i]
        me, spot, half = self.me, pl.ds(low, count), self.me.z // 2
        sems = (self.send.at[i, hop], self.recv.at[i, hop])
        if hop == 0:
            return remote(
                self.blocks[which].at[spot], self.spots[which](me.z, spot), *sems, me.near_z
            )
        view = self.spots[which](pl.ds(2 * half if hop == 1 else 2 * (1 - half), 2), spot)
        return remote(view, view, *sems, me.mid_z if hop == 1 else me.near_z)

    def own(self, which):
        whole = pl.ds(0, self.blocks[which].shape[0])
        return pltpu.make_async_copy(
            self.blocks[which], self.spots[which](self.me.z, whole), self.local.at[which]
        )

    def begin(self):
        for which in range(len(self.blocks)):
            self.own(which).start()

    def first_hop(self, i):
        self.copy(i, 0).start()

    def own_wait(self):
        for which in range(len(self.blocks)):
            self.own(which).wait()

    def inner_hop(self, i):
        if i == 0:
            self.own_wait()
        self.copy(i, 0).wait_recv()
        pl.when(self.inner)(lambda: self.copy(i, 1).start())

    def outer_hop(self, i):
        @pl.when(self.inner)
        def _():
            self.copy(i, 1).wait_recv()
            self.copy(i, 2).start()

    def arrived(self, i):
        pl.when(jnp.logical_not(self.inner))(lambda: self.copy(i, 2).wait_recv())

    def drain(self):
        for i in range(len(self.items)):
            self.copy(i, 0).wait_send()

            @pl.when(self.inner)
            def _(i=i):
                self.copy(i, 1).wait_send()
                self.copy(i, 2).wait_send()


class PlaneGather:
    def __init__(self, me, items, gathered, sems):
        self.me, self.items, self.gathered = me, items, gathered
        self.send, self.recv, self.core_send, self.core_recv = sems

    def scratch(items):
        n = len(items)
        return [DMA((n, 4)), DMA((n, 4)), DMA((n,)), DMA((n,))]

    def parts(self, i):
        _, _, count, first = self.items[i]
        return [part for part, size in ((0, first), (1, count - first)) if size]

    def copy(self, i, stage, part):
        which, low, count, first = self.items[i]
        me = self.me
        spot = pl.ds(low, first) if part == 0 else pl.ds(low + first, count - first)
        if stage == 0:
            index = (EVERY, me.x, me.y, me.c, spot)
        elif part == 0:
            index = (EVERY, EVERY, me.y, me.c, spot)
        else:
            index = (EVERY, me.x, EVERY, me.c, spot)
        view = self.gathered[which].at[index]
        at = 2 * stage + part
        target = me.along_x if stage == part else me.along_y
        return remote(view, view, self.send.at[i, at], self.recv.at[i, at], target)

    def core_copy(self, i):
        which, low, count, _ = self.items[i]
        view = self.gathered[which].at[EVERY, EVERY, EVERY, self.me.c, pl.ds(low, count)]
        return remote(view, view, self.core_send.at[i], self.core_recv.at[i], self.me.along_c)

    def first(self, i):
        for part in self.parts(i):
            self.copy(i, 0, part).start()

    def second(self, i):
        for part in self.parts(i):
            self.copy(i, 0, part).wait_recv()
            self.copy(i, 1, part).start()

    def third(self, i):
        for part in self.parts(i):
            self.copy(i, 1, part).wait_recv()
        self.core_copy(i).start()

    def drain(self):
        for i in range(len(self.items)):
            self.core_copy(i).wait_recv()
            for part in self.parts(i):
                self.copy(i, 0, part).wait_send()
                self.copy(i, 1, part).wait_send()
            self.core_copy(i).wait_send()


class RowExchange:
    def __init__(self, me, source, target, sems, back):
        self.me, self.source, self.target, self.back = me, source, target, back
        self.send, self.recv, self.local = sems
        self.span = (target if back else source).shape[1]

    def scratch():
        return [DMA((3,)), DMA((3,)), DMA((1,))]

    def views(self, tok):
        mine = pl.ds(self.me.tok * self.span, self.span)
        if self.back:
            return self.source.at[pl.ds(tok * self.span, self.span)], self.target.at[self.me.tok]
        return self.source.at[tok], self.target.at[mine]

    def copy(self, p):
        target = self.me.row_partners()[p]
        return remote(*self.views(target[1]), self.send.at[p], self.recv.at[p], target)

    def own(self):
        return pltpu.make_async_copy(*self.views(self.me.tok), self.local.at[0])

    def begin(self, parts=(0, 1, 2)):
        for p in parts:
            if p == 0:
                self.own().start()
            self.copy(p).start()

    def drain(self):
        self.own().wait()
        for p in range(3):
            self.copy(p).wait()


class SmallSum:
    def __init__(self, me, source, out, refs):
        self.me, self.source, self.out = me, source, out
        self.held, self.got, self.line, self.send, self.recv = refs
        self.ways = (me.along_c, me.along_y, me.along_x)

    def scratch(shape, depth):
        return [
            pltpu.VMEM((4,) + shape, F32), pltpu.VMEM((3,) + shape, F32),
            pltpu.VMEM((depth,) + shape, F32), DMA((2 + depth,)), DMA((2 + depth,)),
        ]

    def copy(self, n):
        return remote(
            self.held.at[n], self.got.at[n], self.send.at[n], self.recv.at[n], self.ways[n]
        )

    def line_copy(self, r):
        return remote(
            self.held.at[3], self.line.at[self.me.z], self.send.at[2 + r], self.recv.at[2 + r],
            self.me.along_z(r),
        )

    def begin(self):
        self.held[0] = self.source[...]
        self.copy(0).start()

    def stage(self, n):
        depth = self.me.depth
        if n < 3:
            self.copy(n).wait_recv()
            self.held[n + 1] = self.held[n] + self.got[n]
        if n < 2:
            self.copy(n + 1).start()
        elif n == 2:
            self.line[self.me.z] = self.held[3]
            for r in range(1, depth):
                self.line_copy(r).start()
        else:
            for r in range(1, depth):
                self.line_copy(r).wait_recv()
            total = self.line[0]
            for z in range(1, depth):
                total = total + self.line[z]
            self.out[...] = total

    def drain(self):
        for n in range(3):
            self.copy(n).wait_send()
        for r in range(1, self.me.depth):
            self.line_copy(r).wait_send()


class Reduce:
    def __init__(self, me, items, mid, grads, out, refs):
        self.me, self.items, self.grads, self.out = me, items, grads, out
        (
            self.own_buf, self.core_buf, s1a, s1b, r1a, r1b, s2a, s2b, r2a, r2b, self.s3, self.r3,
            self.c_send, self.c_recv, self.m_send, self.m_recv, self.z_send, self.z_recv, self.local,
        ) = refs
        self.sends = ((s1a, s1b), (s2a, s2b))
        self.recvs = ((r1a, r1b), (r2a, r2b))
        self.tiles = (slice(0, mid), slice(mid, items[0][1]))
        self.bits = ((me.y, me.x), (me.x, me.y))
        self.ways = ((me.along_y, me.along_x), (me.along_x, me.along_y))

    def scratch(items, mid, depth, arrays):
        n, count = len(items), items[0][1]

        def tiles(lead, size):
            return pltpu.VMEM((n, lead, size, 16, 128), BF)

        made = [tiles(4 * depth, count), tiles(4 * depth, count)]
        for lead in (2 * depth, depth):
            made += [tiles(lead, size) for size in (mid, count - mid)] * 2
        made += [tiles(depth - 1, count), tiles(depth - 1, count)]
        made += [DMA((n, arrays)), DMA((n, arrays)), DMA((n, 4)), DMA((n, 4))]
        return made + [DMA((n, depth - 1)), DMA((n, depth - 1)), DMA((n, arrays))]

    def pieces(self, i):
        low, count = self.items[i]
        at = 0
        for n, array in enumerate(self.grads):
            yield n, array, pl.ds(low, count), pl.ds(at, array.shape[0])
            at = at + array.shape[0]

    def core_copies(self, i):
        for n, array, spot, place in self.pieces(i):
            yield remote(
                array.at[:, 1 - self.me.c, spot], self.core_buf.at[i, place],
                self.c_send.at[i, n], self.c_recv.at[i, n], self.me.along_c,
            )

    def own_copies(self, i):
        for n, array, spot, place in self.pieces(i):
            yield pltpu.make_async_copy(
                array.at[:, self.me.c, spot], self.own_buf.at[i, place], self.local.at[i, n]
            )

    def side_copy(self, i, part, stage):
        at = 2 * stage + part
        return remote(
            self.sends[stage][part].at[i], self.recvs[stage][part].at[i],
            self.m_send.at[i, at], self.m_recv.at[i, at], self.ways[part][stage],
        )

    def line_copy(self, i, r):
        return remote(
            self.s3.at[i, r - 1], self.r3.at[i, r - 1], self.z_send.at[i, r - 1],
            self.z_recv.at[i, r - 1], self.me.along_z(r),
        )

    def slot(self, part, j, bit):
        return 2 * j + bit if part == 0 else (j // 2) * 4 + 2 * bit + j % 2

    def pair_sum(self, i, part, slot):
        spot = self.tiles[part]
        return self.own_buf[i, slot, spot].astype(F32) + self.core_buf[i, slot, spot].astype(F32)

    def plane_sum(self, i, part, j):
        slot = self.slot(part, j, self.bits[part][0])
        return self.pair_sum(i, part, slot) + self.recvs[0][part][i, j].astype(F32)

    def chip_sum(self, i, part, k):
        total = self.plane_sum(i, part, 2 * k + self.bits[part][1])
        return total + self.recvs[1][part][i, k].astype(F32)

    def begin(self):
        for i in range(len(self.items)):
            for copy in self.core_copies(i):
                copy.start()
            for copy in self.own_copies(i):
                copy.start()

    def core_stage(self, i):
        for copy in self.core_copies(i):
            copy.wait_recv()
        for copy in self.own_copies(i):
            copy.wait()
        for part in range(2):

            def one(j, _, part=part):
                slot = self.slot(part, j, 1 - self.bits[part][0])
                self.sends[0][part][i, j] = self.pair_sum(i, part, slot).astype(BF)
                return 0

            lax.fori_loop(0, 2 * self.me.depth, one, 0)
            self.side_copy(i, part, 0).start()

    def first_stage(self, i):
        for part in range(2):
            self.side_copy(i, part, 0).wait_recv()

            def one(k, _, part=part):
                j = 2 * k + 1 - self.bits[part][1]
                self.sends[1][part][i, k] = self.plane_sum(i, part, j).astype(BF)
                return 0

            lax.fori_loop(0, self.me.depth, one, 0)
            self.side_copy(i, part, 1).start()

    def second_stage(self, i):
        for part in range(2):
            self.side_copy(i, part, 1).wait_recv()
        for r in range(1, self.me.depth):
            other = lax.rem(self.me.z + r, self.me.depth)
            for part in range(2):
                self.s3[i, r - 1, self.tiles[part]] = self.chip_sum(i, part, other).astype(BF)
            self.line_copy(i, r).start()

    def line_stage(self, i):
        for r in range(1, self.me.depth):
            self.line_copy(i, r).wait_recv()
        for part in range(2):
            total = self.chip_sum(i, part, self.me.z)
            for r in range(1, self.me.depth):
                total = total + self.r3[i, r - 1, self.tiles[part]].astype(F32)
            self.out[i, self.tiles[part]] = total

    def drain(self):
        for i in range(len(self.items)):
            for copy in self.core_copies(i):
                copy.wait_send()
            for part in range(2):
                self.side_copy(i, part, 0).wait_send()
                self.side_copy(i, part, 1).wait_send()
            for r in range(1, self.me.depth):
                self.line_copy(i, r).wait_send()

    def rounds(self):
        n = len(self.items)
        made = [[partial(self.core_stage, 0), partial(self.core_stage, 1)]]
        for t in range(1, n + 3):
            order = ((self.first_stage, t - 1), (self.core_stage, t + 1))
            order = order + ((self.second_stage, t - 2), (self.line_stage, t - 3))
            made.append([partial(stage, i) for stage, i in order if 0 <= i < n])
        return made


class Taker:
    def __init__(self, refs):
        self.refs, self.at = refs, 0

    def __call__(self, count=None):
        if count is None:
            return self(1)[0]
        self.at = self.at + count
        return self.refs[self.at - count : self.at]


def at_steps(step, work):
    for when, one in work:
        pl.when(step == when)(one)


def kernel_params(collective_id=None):
    if collective_id is None:
        return pltpu.CompilerParams(vmem_limit_bytes=VMEM_LIMIT)
    return pltpu.CompilerParams(
        vmem_limit_bytes=VMEM_LIMIT, collective_id=collective_id, has_side_effects=True
    )


def gather_kernel(depth, line_items, plane_items, steps, when, hist_ref, cot_ref, c_ref, *refs):
    take = Taker(refs)
    blocks = take(3)
    rows_in = take()
    part_ref, dots_ref = take(2)
    got_a, got_e, got_f, rows_out = take(4)
    step = pl.program_id(0) * pl.num_programs(1) + pl.program_id(1)
    me = Place(depth)
    spots = [
        lambda z, spot: got_a.at[z, me.x, me.y, me.c, spot],
        lambda z, spot: got_e.at[z, me.x, me.y, me.c, spot],
        lambda z, spot: got_f.at[z, me.x, me.y, me.c, spot],
    ]
    line = LineGather(me, line_items, blocks, spots, take(3))
    plane = PlaneGather(me, plane_items, [got_a, got_e], take(4))
    rows = RowExchange(me, rows_in, rows_out, take(3), False)

    few = len(plane_items)
    later = range(few, len(line_items))

    def begin():
        me.greet()
        line.begin()
        for i in range(few):
            line.first_hop(i)
        rows.begin()

    def arrived(i):
        line.arrived(i)
        if i < few:
            plane.first(i)

    def end():
        plane.drain()
        rows.drain()
        line.drain()

    at_steps(step, [(0, begin)])

    @pl.when(pl.program_id(1) == 0)
    def _():
        part_ref[...] = jnp.zeros_like(part_ref)

    group = hist_ref.shape[0]
    history_step(hist_ref, cot_ref, c_ref, pl.program_id(1) * group, part_ref, dots_ref)
    groups = [
        [partial(line.inner_hop, i) for i in range(few)] + [partial(line.first_hop, i) for i in later],
        [partial(line.outer_hop, i) for i in range(few)],
        [partial(arrived, i) for i in range(few)],
        [partial(line.inner_hop, i) for i in later],
        [partial(plane.second, i) for i in range(few)],
        [partial(line.outer_hop, i) for i in later],
        [partial(plane.third, i) for i in range(few)] + [partial(arrived, i) for i in later] + [end],
    ]
    work = []
    for starts, group_work in zip(when, groups):
        for at, one in enumerate(group_work):
            work.append((min(starts[min(at, len(starts) - 1)], steps - 1), one))
    at_steps(step, work)


def gather(blocks, inputs, history, cotangent, coefficient, depth):
    terms, tokens, width = history.shape
    row_count, span, _ = inputs.shape
    tile, group = 128, 6
    count_a, count_e, count_f = (b.shape[0] for b in blocks)
    part = count_a // gather_cuts
    half = count_f // 2
    line_items = [(1, 0, count_e)] + [(0, low, part) for low in range(0, count_a, part)]
    line_items = line_items + [(2, low, half) for low in range(0, count_f, half)]
    plane_items = [(1, 0, count_e, count_e)] + [(0, low, part, int(part * gather_share)) for low in range(0, count_a, part)]
    everyone = (depth, 2, 2, 2)
    return pl.pallas_call(
        partial(
            gather_kernel, depth, line_items, plane_items,
            (tokens // tile) * (terms // group), gather_steps,
        ),
        grid=(tokens // tile, terms // group),
        in_specs=[
            pl.BlockSpec((group, tile, width), lambda t, j: (j, t, 0)),
            pl.BlockSpec((tile, width), lambda t, j: (t, 0)),
            pl.BlockSpec(memory_space=pltpu.SMEM),
        ]
        + [pl.BlockSpec(b.shape, lambda t, j: (0, 0, 0), pipeline_mode=pl.Buffered(1)) for b in blocks]
        + [HBM],
        out_specs=[
            pl.BlockSpec((tile, width), lambda t, j: (t, 0)),
            pl.BlockSpec((1, 8 * group, 128), lambda t, j: (t, j, 0)),
        ]
        + [HBM] * 4,
        out_shape=[
            jax.ShapeDtypeStruct((tokens, width), F32),
            jax.ShapeDtypeStruct((tokens // tile, 8 * terms, 128), F32),
            jax.ShapeDtypeStruct(everyone + blocks[0].shape, BF),
            jax.ShapeDtypeStruct(everyone + blocks[1].shape, BF),
            jax.ShapeDtypeStruct(everyone + blocks[2].shape, BF),
            jax.ShapeDtypeStruct((span * row_count, width), BF),
        ],
        scratch_shapes=LineGather.scratch(line_items, 3)
        + PlaneGather.scratch(plane_items)
        + RowExchange.scratch(),
        compiler_params=kernel_params(0),
        name="gather",
    )(history, cotangent.reshape(tokens, width), coefficient, *blocks, inputs)


def finish_kernel(depth, items, mid, arrays, small_ref, *refs):
    take = Taker(refs)
    grads = take(arrays)
    rows_in = take()
    out_ref, small_out, rows_out = take(3)
    me = Place(depth)
    reduce = Reduce(me, items, mid, grads, out_ref, take(19))
    rows = RowExchange(me, rows_in, rows_out, take(3), True)
    small = SmallSum(me, small_ref, small_out, take(5))
    me.greet()
    small.begin()
    reduce.begin()
    rows.begin()
    for t, stages in enumerate(reduce.rounds()):
        for stage in stages:
            stage()
        if t < 4:
            small.stage(t)
    small.drain()
    rows.drain()
    reduce.drain()


def finish(grads, small, row, row_count, depth):
    length, width = row.shape
    count = grads[0].shape[2]
    size = count // 3
    items = [(low, size) for low in range(0, count, size)]
    mid = size // 3
    vmem = pl.BlockSpec(memory_space=pltpu.VMEM)
    return pl.pallas_call(
        partial(finish_kernel, depth, items, mid, len(grads)),
        in_specs=[vmem] + [HBM] * (len(grads) + 1),
        out_specs=[vmem, vmem, HBM],
        out_shape=[
            jax.ShapeDtypeStruct((len(items), size, 16, 128), F32),
            jax.ShapeDtypeStruct(small.shape, F32),
            jax.ShapeDtypeStruct((row_count, length // row_count, width), row.dtype),
        ],
        scratch_shapes=Reduce.scratch(items, mid, depth, len(grads))
        + RowExchange.scratch()
        + SmallSum.scratch(small.shape, depth),
        compiler_params=kernel_params(1),
        name="finish",
    )(small, *grads, row)


def enter_kernel(depth, items, ready, rows_at, reach, x_ref, w_ref, vec_ref, cos_ref, sin_ref, sc_ref, sr_ref, *refs):
    take = Taker(refs)
    _, rows_in = take(2)
    n1_ref, q_ref, k_ref, v_ref, o_ref, lse_ref, got_f, rows_out = take(8)
    bias_ref, turned_ref = take(2)
    me = Place(depth)
    plane = PlaneGather(me, items, [got_f], take(4))
    rows = RowExchange(me, rows_in, rows_out, take(3), False)
    step = pl.program_id(0)
    tile, width = x_ref.shape
    length = q_ref.shape[1]
    tiles = length // tile
    pairs = width // 128
    block_rows = 256
    blocks = length // block_rows

    def begin():
        me.greet()
        for i in range(len(items)):
            plane.first(i)

    def second(i):
        if i == 0:
            own.wait()
        plane.second(i)
    def finish_all():
        plane.drain()
        rows.drain()

    at_steps(step, [(0, begin)])

    @pl.when(step == 0)
    def _():
        fill_bias(bias_ref, sc_ref, sr_ref, block_rows, reach)

    @pl.when(step < tiles)
    def _():
        centered, inverse = norm_parts(x_ref[...].astype(F32))
        normed = (centered * inverse * vec_ref[0:1, :width] + vec_ref[1:2, :width]).astype(BF)
        n1_ref[...] = normed
        cosine = jnp.concatenate([cos_ref[...]] * 2, axis=1)
        sine = jnp.concatenate([sin_ref[...]] * 2, axis=1)
        spot = pl.ds(pl.multiple_of(step * tile, tile), tile)
        per_part = width // 256
        for at in range(3 * per_part):
            part = nn_dot(normed, cols(w_ref, 2 * at, 2)) + vec_ref[2:3, 256 * at : 256 * at + 256]
            if at < 2 * per_part:
                part = part * cosine + swap_halves(part) * sine
            if at < per_part:
                part = part * HEAD_DIM ** (-0.5)
            target = (q_ref, k_ref, v_ref)[at // per_part]
            first = 2 * (at % per_part)
            target[first, spot, :] = part[:, :128].astype(BF)
            target[first + 1, spot, :] = part[:, 128:].astype(BF)

    pair = jnp.maximum(step - tiles, 0) // blocks
    current = jnp.maximum(step - tiles, 0) % blocks

    def attend_block(block):
        if block == 0:
            turned_ref[...] = v_ref[pair].T
        low, high = key_range(block, block_rows, reach)
        at = sum(h - l for l, h in (key_range(b, block_rows, reach) for b in range(block)))
        spot = slice(block * block_rows, (block + 1) * block_rows)
        keys = k_ref[pair, low:high, :]
        queries = q_ref[pair, spot, :]
        bias = bias_ref[at : at + high - low, :]
        halves = []
        for head in range(2):
            scores = nt_dot(head_mask(keys, head), queries) + bias
            top = jnp.max(scores, axis=0, keepdims=True)
            exponent = jnp.exp(scores - top)
            total = jnp.sum(exponent, axis=0, keepdims=True)
            probs = (exponent * (1.0 / total)).astype(BF)
            lse_ref[pair, head : head + 1, spot] = top + jnp.log(total)
            turned = turned_ref[HEAD_DIM * head : HEAD_DIM * head + HEAD_DIM, low:high]
            halves.append(nn_dot(turned, probs))
        lanes = pl.ds(pl.multiple_of(pair * 128, 128), 128)
        o_ref[spot, lanes] = jnp.concatenate(halves, axis=0).T.astype(BF)

    for block in range(blocks):
        pl.when((step >= tiles) & (current == block))(partial(attend_block, block))

    n = len(items)
    work = [(ready[0][i], partial(plane.second, i)) for i in range(n)]
    work += [(ready[1][i], partial(plane.third, i)) for i in range(n)]
    work.sort(key=lambda item: item[0])
    work += [(rows_at, rows.begin)]
    at_steps(step, work + [(tiles + pairs * blocks - 1, finish_all)])


def enter(x_row, w_qkv, vectors, cosine, sine, seg_col, seg_row, got_f, cotangent, reach, depth):
    length, width = x_row.shape
    array, lead = w_qkv
    tile = 256
    tiles, pairs = length // tile, width // 128
    steps = tiles + pairs * (length // 256)
    once = pl.Buffered(1)
    count = got_f.shape[4]
    size = count // 4
    items = [(0, low, size, size // enter_share) for low in range(0, count, size)]
    ready = (enter_first_steps, enter_second_steps)

    def const(shape):
        return pl.BlockSpec(shape, lambda i: (0,) * len(shape), pipeline_mode=once)

    def rows(lanes):
        return pl.BlockSpec((tile, lanes), lambda i: (jnp.minimum(i, tiles - 1), 0))

    heads = jax.ShapeDtypeStruct((pairs, length, 128), BF)
    return pl.pallas_call(
        partial(enter_kernel, depth, items, ready, enter_rows_step, reach),
        grid=(steps,),
        in_specs=[
            rows(width), const((lead,) + array.shape[1:]), const(vectors.shape), rows(128), rows(128),
            const(seg_col.shape), const(seg_row.shape), HBM, HBM,
        ],
        out_specs=[
            rows(width), const(heads.shape), const(heads.shape), const(heads.shape),
            const((length, width)), const((pairs, 2, length)), HBM, HBM,
        ],
        out_shape=[
            jax.ShapeDtypeStruct((length, width), BF), heads, heads, heads,
            jax.ShapeDtypeStruct((length, width), BF),
            jax.ShapeDtypeStruct((pairs, 2, length), F32),
            jax.ShapeDtypeStruct(got_f.shape, BF),
            jax.ShapeDtypeStruct((length, width), BF),
        ],
        scratch_shapes=[
            pltpu.VMEM((bias_rows(length, 256, reach), 256), F32),
            pltpu.VMEM((128, length), BF),
        ]
        + PlaneGather.scratch(items)
        + RowExchange.scratch(),
        input_output_aliases={7: 6},
        compiler_params=kernel_params(2),
        name="enter",
    )(x_row, array, vectors, cosine, sine, seg_col, seg_row, got_f, cotangent)


def leave_kernel(
    depth, items, mid, starts, rows_at, reach, arrays,
    q_ref, k_ref, v_ref, g_ref, lse_ref, sc_ref, sr_ref, cos_ref, sin_ref,
    x_ref, n1_ref, ghid_ref, w_ref, vec_ref, *refs,
):
    take = Taker(refs)
    grads = take(arrays)
    rows_in = take()
    gx_ref, gw_ref, gb_ref, gvec_ref, out_ref, rows_out = take(6)
    bias_ref, turned_ref, dk_acc, dv_acc, gp_ref, n1t_ref = take(6)
    me = Place(depth)
    reduce = Reduce(me, items, mid, grads, out_ref, take(19))
    rows = RowExchange(me, rows_in, rows_out, take(3), True)
    step = pl.program_id(0)
    length, width = x_ref.shape
    pairs = width // 128
    block_rows = 256
    blocks = length // block_rows
    attend_steps = pairs * blocks
    chunks = 3 * width // 256
    tile = 256
    tiles = length // tile

    def begin():
        me.greet()
        reduce.begin()
        rows.begin((0,))

    def end():
        rows.drain()
        reduce.drain()

    at_steps(step, [(0, begin)])

    @pl.when(step == 0)
    def _():
        fill_bias(bias_ref, sc_ref, sr_ref, block_rows, reach)

    pair = jnp.minimum(step // blocks, pairs - 1)
    current = step % blocks

    def attend_block(block):
        if block == 0:
            turned_ref[...] = k_ref[0].T
            dk_acc[...] = jnp.zeros_like(dk_acc)
            dv_acc[...] = jnp.zeros_like(dv_acc)
        low, high = key_range(block, block_rows, reach)
        at = sum(h - l for l, h in (key_range(b, block_rows, reach) for b in range(block)))
        spot = slice(block * block_rows, (block + 1) * block_rows)
        keys, vals = k_ref[0, low:high, :], v_ref[0, low:high, :]
        queries, grad = q_ref[0, spot, :], g_ref[spot, :]
        bias = bias_ref[at : at + high - low, :]
        halves = []
        for head in range(2):
            scores = nt_dot(head_mask(keys, head), queries) + bias
            probs = jnp.exp(scores - lse_ref[0, head : head + 1, spot])
            dprobs = nt_dot(head_mask(vals, head), grad)
            inner = jnp.sum(probs * dprobs, axis=0, keepdims=True)
            dscores = (probs * (dprobs - inner)).astype(BF)
            turned = turned_ref[HEAD_DIM * head : HEAD_DIM * head + HEAD_DIM, low:high]
            halves.append(nn_dot(turned, dscores))
            dk_acc[low:high, :] += nn_dot(dscores, head_mask(queries, head))
            dv_acc[low:high, :] += nn_dot(probs.astype(BF), head_mask(grad, head))
        grad_query = jnp.concatenate(halves, axis=0).T * HEAD_DIM ** (-0.5)
        turn(grad_query, pair, spot)
        if block == blocks - 1:
            turn(dk_acc[...], pairs + pair, slice(0, length))
            gp_ref[2 * pairs + pair] = dv_acc[...].astype(BF)

    def turn(values, place, spot):
        values = values.astype(BF).astype(F32)
        values = values * cos_ref[spot, :] - swap_halves(values) * sin_ref[spot, :]
        gp_ref[place, spot, :] = values.astype(BF)

    for block in range(blocks):
        pl.when((step < attend_steps) & (current == block))(partial(attend_block, block))

    @pl.when(step == attend_steps)
    def _():
        @pl.loop(0, tiles)
        def _(t):
            spot = pl.ds(pl.multiple_of(t * tile, tile), tile)
            n1t_ref[:, spot] = n1_ref[spot, :].T

        gvec_ref[...] = jnp.zeros_like(gvec_ref)

    @pl.when((step >= attend_steps) & (step < attend_steps + chunks))
    def _():
        at = jnp.clip(step - attend_steps, 0, chunks - 1)
        grad = jnp.concatenate([gp_ref[2 * at], gp_ref[2 * at + 1]], axis=1)
        for r in range(width // 256):
            put_tiles(gw_ref, 16 * r, 0, nn_dot(n1t_ref[256 * r : 256 * r + 256, :], grad).astype(BF))
        gb_ref[0:1, :] = jnp.sum(grad.astype(F32), axis=0, keepdims=True)

    @pl.when(step >= attend_steps + chunks)
    def _():
        t = jnp.maximum(step - attend_steps - chunks, 0)
        spot = pl.ds(pl.multiple_of(t * tile, tile), tile)
        grad = jnp.concatenate([gp_ref[p, spot, :] for p in range(3 * pairs)], axis=1)
        grad_norm = nt_dot(grad, cols(w_ref, 0, 3 * pairs))
        centered, inverse = norm_parts(x_ref[spot, :].astype(F32))
        normed = centered * inverse
        gvec_ref[0:1, :] += jnp.sum(normed * grad_norm, axis=0, keepdims=True)
        gvec_ref[1:2, :] += jnp.sum(grad_norm, axis=0, keepdims=True)
        scaled = grad_norm * vec_ref[0:1, :]
        grad_value = inverse * (
            scaled
            - jnp.mean(scaled, axis=1, keepdims=True)
            - normed * jnp.mean(scaled * normed, axis=1, keepdims=True)
        )
        gx_ref[spot, :] = (ghid_ref[spot, :] + grad_value).astype(gx_ref.dtype)

    work = [(when, partial(rows.begin, (p,))) for p, when in enumerate(rows_at) if p]
    for start, stages in zip(starts, reduce.rounds()):
        for at, stage in enumerate(stages):
            work.append((min(start + at, attend_steps + chunks + tiles - 1), stage))
    at_steps(step, work + [(attend_steps + chunks + tiles - 1, end)])


def leave(
    queries, keys, values, grad_attended, lse, seg_col, seg_row, cosine, sine,
    x_row, n1, grad_hidden, w_qkv, vectors, grads, row, row_count, reach, depth,
):
    length, width = x_row.shape
    array, lead = w_qkv
    pairs, blocks = width // 128, length // 256
    attend_steps, chunks, tiles = pairs * blocks, 3 * width // 256, length // 256
    steps = attend_steps + chunks + tiles
    once = pl.Buffered(1)
    count = grads[0].shape[2]
    size = count // 4
    items = [(low, size) for low in range(0, count, size)]
    mid = size // leave_share
    starts = leave_steps

    def const(shape):
        return pl.BlockSpec(shape, lambda i: (0,) * len(shape), pipeline_mode=once)

    def pair_at(i):
        return jnp.minimum(i // blocks, pairs - 1)

    def chunk_at(i):
        return jnp.clip(i - attend_steps, 0, chunks - 1)

    heads = pl.BlockSpec((1, length, 128), lambda i: (pair_at(i), 0, 0))
    rows = const((length, width))
    row_tiles = width // 16
    return pl.pallas_call(
        partial(leave_kernel, depth, items, mid, starts, leave_rows_steps, reach, len(grads)),
        grid=(steps,),
        in_specs=[
            heads, heads, heads,
            pl.BlockSpec((length, 128), lambda i: (0, pair_at(i))),
            pl.BlockSpec((1, 2, length), lambda i: (pair_at(i), 0, 0)),
            const(seg_col.shape), const(seg_row.shape), const(cosine.shape), const(sine.shape),
            rows, rows, rows, const((lead,) + array.shape[1:]), const(vectors.shape),
        ]
        + [HBM] * (len(grads) + 1),
        out_specs=[
            rows,
            pl.BlockSpec((row_tiles, 2, 16, 128), lambda i: (0, chunk_at(i), 0, 0)),
            pl.BlockSpec((8, 256), lambda i: (0, chunk_at(i))),
            const((8, width)),
            const((len(items), size, 16, 128)),
            HBM,
        ],
        out_shape=[
            jax.ShapeDtypeStruct((length, width), BF),
            jax.ShapeDtypeStruct((row_tiles, 3 * width // 128, 16, 128), BF),
            jax.ShapeDtypeStruct((8, 3 * width), F32),
            jax.ShapeDtypeStruct((8, width), F32),
            jax.ShapeDtypeStruct((len(items), size, 16, 128), F32),
            jax.ShapeDtypeStruct((row_count, length // row_count, width), row.dtype),
        ],
        scratch_shapes=[
            pltpu.VMEM((bias_rows(length, 256, reach), 256), F32),
            pltpu.VMEM((128, length), BF),
            pltpu.VMEM((length, 128), F32),
            pltpu.VMEM((length, 128), F32),
            pltpu.VMEM((3 * pairs, length, 128), BF),
            pltpu.VMEM((width, length), BF),
        ]
        + Reduce.scratch(items, mid, depth, len(grads))
        + RowExchange.scratch(),
        compiler_params=kernel_params(3),
        name="leave",
    )(
        queries, keys, values, grad_attended, lse, seg_col, seg_row, cosine, sine,
        x_row, n1, grad_hidden, array, vectors, *grads, row,
    )


HALO = 2048


class Plan:
    def __init__(self, devices, shape_list):
        sizes = [math.prod(shape) for shape in shape_list]
        starts = [sum(sizes[:i]) for i in range(len(sizes))]
        self.total = sum(sizes)
        self.devices = devices
        self.own = self.total // devices
        self.matrices = [(starts[i], shape_list[i]) for i in (2, 4)]
        self.vectors = [(0, sizes[0] + sizes[1]), (starts[3], sizes[3]), (starts[5], sizes[5])]
        first, second = (math.prod(shape) for _, shape in self.matrices)
        self.block = (first + second) // devices
        self.split = devices * first // (first + second)
        self.rows = [
            shape[0] // n if n else 0
            for (_, shape), n in zip(self.matrices, (self.split, devices - self.split))
        ]
        self.fits = self.total % devices == 0 and (first + second) % devices == 0
        for (_, shape), n, rows in zip(
            self.matrices, (self.split, devices - self.split), self.rows
        ):
            self.fits = self.fits and n > 0 and rows * n == shape[0] and rows % 16 == 0
            self.fits = self.fits and rows * shape[1] == self.block
        self.owners = [at // self.own for at, _ in self.vectors]
        if self.fits:
            for s in range(devices):
                shift = self.block_start(s) - self.own * s
                self.fits = self.fits and -HALO <= shift <= HALO
                self.fits = self.fits and shift + self.block - self.own <= HALO
                self.fits = self.fits and self.own - self.block - shift <= HALO
            for (at, size), owner in zip(self.vectors, self.owners):
                self.fits = self.fits and at + size <= self.own * (owner + 1) + HALO
            self.fits = self.fits and len(set(self.owners)) == len(self.owners)

    def block_start(self, s):
        (first, _), (second, _) = self.matrices
        if isinstance(s, int):
            return first + self.block * s if s < self.split else second + self.block * (s - self.split)
        return jnp.where(
            s < self.split, first + self.block * s, second + self.block * (s - self.split)
        )

    def tile_shapes(self):
        return [
            (rows // 16, shape[1] // 128) for (_, shape), rows in zip(self.matrices, self.rows)
        ]

    def to_tiles(self, flat, s):
        forms = [
            flat.reshape(rt, 16, ct, 128).transpose(0, 2, 1, 3).reshape(rt * ct, 16, 128)
            for rt, ct in self.tile_shapes()
        ]
        return jnp.where(s < self.split, forms[0], forms[1])

    def from_tiles(self, tiles, s):
        forms = [
            tiles.reshape(rt, ct, 16, 128).transpose(0, 2, 1, 3).reshape(-1)
            for rt, ct in self.tile_shapes()
        ]
        return jnp.where(s < self.split, forms[0], forms[1])

    def vector_rows(self):
        return -(-max(size for _, size in self.vectors) // 1024) * 8

    def blocks(self, flat, before, after, s):
        room = self.vector_rows() * 128
        joined = jnp.concatenate([before, flat, after, jnp.zeros((room,), flat.dtype)])
        aligned = lax.dynamic_slice(
            joined, (HALO + self.block_start(s) - self.own * s,), (self.block,)
        )
        place = jnp.int32(0)
        for (at, _), owner in zip(self.vectors, self.owners):
            place = jnp.where(s == owner, at - self.own * owner, place)
        extra = lax.dynamic_slice(joined, (HALO + place,), (room,))
        return self.to_tiles(aligned, s), extra.reshape(-1, 128)

    def shard(self, aligned, before, after, vectors, s):
        room = self.vector_rows() * 128
        edge = jnp.zeros((room,), aligned.dtype)
        joined = jnp.concatenate([edge, before, aligned, after, edge])
        begin = self.block_start(s)
        for (at, size), value in zip(self.vectors, vectors):
            place = jnp.clip(room + HALO + at - begin, 0, joined.shape[0] - size)
            joined = lax.dynamic_update_slice(joined, value, (place,))
        return lax.dynamic_slice(joined, (room + HALO + self.own * s - begin,), (self.own,))


def neighbour_edges(values_list, count):
    axes = ("dp", "tok")
    tails = jnp.stack([v[-HALO:] for v in values_list])
    heads = jnp.stack([v[:HALO] for v in values_list])
    before = lax.ppermute(tails, axes, [(i, (i + 1) % count) for i in range(count)])
    after = lax.ppermute(heads, axes, [(i, (i - 1) % count) for i in range(count)])
    return before, after


def plans(devices):
    return Plan(devices, attention_shapes()), Plan(devices, feedforward_shapes())


def row_tables(lengths_row, length):
    places = jnp.arange(length, dtype=jnp.int32)
    segment, position = layout(lengths_row[None], places)
    lane = jnp.arange(128, dtype=jnp.int32) % HEAD_DIM
    half_dim = HEAD_DIM // 2
    frequency = jnp.exp(
        (lane % half_dim).astype(jnp.float32) * (-2.0 * math.log(10000.0) / HEAD_DIM)
    )
    angle = position[0].astype(jnp.float32)[:, None] * frequency[None, :]
    sine = jnp.where(lane < half_dim, -1.0, 1.0)[None, :] * jnp.sin(angle)
    return segment[0], jnp.cos(angle), sine


def row_shards(
    inputs,
    history,
    document_lengths,
    cotangent,
    attention_params,
    attention_first,
    attention_second,
    feedforward_params,
    feedforward_first,
    feedforward_second,
    mixing_offsets,
    mixing_first,
    mixing_second,
    step_count,
):
    row_count, span, width = inputs.shape
    tok_size = lax.axis_size("tok")
    devices = lax.axis_size("dp") * tok_size
    length = span * tok_size
    tokens_all = row_count * span * devices
    axes = ("dp", "tok")
    s = lax.axis_index(axes)
    plan_a, plan_f = plans(devices)
    reach = length // 2

    depth = lax.axis_size("dp") // 2
    tokens = row_count * span
    term_count = mixing_offsets.shape[0]
    coefficient = mixing_offsets + (jnp.arange(term_count) == term_count - 1).astype(F32)

    low_a, low_f = attention_params.astype(BF), feedforward_params.astype(BF)
    before, after = neighbour_edges([low_a, low_f], devices)
    tiles_a, extra_a = plan_a.blocks(low_a, before[0], after[0], s)
    tiles_f, extra_f = plan_f.blocks(low_f, before[1], after[1], s)
    extra = jnp.concatenate([extra_a, extra_f]).reshape(-1, 16, 128)
    count_a, count_f = tiles_a.shape[0], tiles_f.shape[0]
    history_part, history_dots, got_a, got_e, got_f, x_row = gather(
        [tiles_a, extra, tiles_f], inputs, history.reshape(term_count - 1, tokens, width), cotangent,
        coefficient, depth,
    )
    got_a = got_a.reshape(devices, count_a, 16, 128)
    extras = got_e.reshape(devices, -1).astype(F32)
    room_a = plan_a.vector_rows() * 128

    def pick(plan, which, at):
        return extras[plan.owners[which], at : at + plan.vectors[which][1]]

    gain_one, shift_one = jnp.split(pick(plan_a, 0, 0), 2)
    b_qkv, b_out = pick(plan_a, 1, 0), pick(plan_a, 2, 0)
    gain_two, shift_two = jnp.split(pick(plan_f, 0, room_a), 2)
    b_up, b_down = pick(plan_f, 1, room_a), pick(plan_f, 2, room_a)
    (rq, cq), (ro, co) = plan_a.tile_shapes()
    (ru, cu), (rd, cd) = plan_f.tile_shapes()
    w_qkv = (got_a.reshape(devices, rq, cq, 16, 128), plan_a.split)
    w_out = (got_a.reshape(devices, ro, co, 16, 128), devices - plan_a.split)
    def stack(vectors, wide):
        vectors = [jnp.pad(v, (0, wide - v.shape[0])) for v in vectors]
        vectors = vectors + [jnp.zeros((wide,), F32)] * (8 - len(vectors))
        return jnp.stack(vectors)

    own_lengths = lax.dynamic_index_in_dim(document_lengths, lax.axis_index("tok"), 0, False)
    segment, cosine, sine = row_tables(own_lengths, length)
    seg_col, seg_row = segment[:, None], segment[None, :]

    normed_one, queries, keys, values, attended, lse, got_f, cot_row = enter(
        x_row, w_qkv, stack([gain_one, shift_one, b_qkv], 3 * width), cosine, sine, seg_col, seg_row,
        got_f, cotangent, reach, depth,
    )
    w_up = (got_f.reshape(devices, ru, cu, 16, 128), plan_f.split)
    w_down = (got_f.reshape(devices * rd, cd, 16, 128), plan_f.split * rd // 16)
    grad_history, block_out, grad_attended, grad_hidden, gw_up, gw_down, gw_out, gb_up, gvec_two = middle(
        x_row, attended, cot_row, w_out, w_up, w_down,
        stack([gain_two, shift_two, b_out, b_down], width), b_up[None, :],
        cotangent.reshape(tokens, width), coefficient,
    )
    def by_core(array, tiles):
        return array.reshape(-1, 2, *tiles.shape)

    grad_row, gw_qkv, gb_qkv, gvec_one, sum_f, block_back = leave(
        queries, keys, values, grad_attended, lse, seg_col, seg_row, cosine, sine,
        x_row, normed_one, grad_hidden, w_qkv, stack([gain_one], width),
        [by_core(gw_up, tiles_f), by_core(gw_down, tiles_f)], block_out, row_count, reach, depth,
    )
    mixed = history_part.reshape(row_count, span, width) + coefficient[-1] * block_back.astype(F32)

    small = jnp.concatenate(
        [
            gvec_one[0], gvec_one[1], gb_qkv[0], gvec_two[2],
            gvec_two[0], gvec_two[1], gb_up[0], gvec_two[3],
            jnp.sum(history_dots.reshape(-1, term_count - 1, 8 * 128), axis=(0, 2)),
            jnp.sum(gvec_two[4])[None],
        ]
    )
    small_size = small.shape[0]
    small = jnp.pad(small, (0, -small_size % 1024)).reshape(-1, 128)
    scale = 1.0 / tokens_all
    sum_a, small, grad_back = finish(
        [by_core(gw_qkv, tiles_a), by_core(gw_out, tiles_a)], small, grad_row, row_count, depth
    )
    small = small.reshape(-1)[:small_size] / tokens_all
    grad_inputs = grad_back.astype(F32)
    flat_a = plan_a.from_tiles(sum_a.reshape(tiles_a.shape) * scale, s)
    flat_f = plan_f.from_tiles(sum_f.reshape(tiles_f.shape) * scale, s)
    before, after = neighbour_edges([flat_a, flat_f], devices)
    at = 0
    parts = []
    for plan in (plan_a, plan_f):
        for _, size in plan.vectors:
            parts.append(small[at : at + size])
            at = at + size
    attention_share = plan_a.shard(flat_a, before[0], after[0], parts[:3], s)
    feedforward_share = plan_f.shard(flat_f, before[1], after[1], parts[3:], s)
    mixing_grad = small[at:]

    count_now = step_count[0]
    attention_places = s * plan_a.own + jnp.arange(plan_a.own, dtype=jnp.int32)
    feedforward_places = s * plan_f.own + jnp.arange(plan_f.own, dtype=jnp.int32)
    attention_step = adam_update(
        attention_params, attention_share, attention_first, attention_second, count_now,
        decay_mask(attention_places, attention_shapes()),
    )
    feedforward_step = adam_update(
        feedforward_params, feedforward_share, feedforward_first, feedforward_second, count_now,
        decay_mask(feedforward_places, feedforward_shapes()),
    )
    mixing_step = adam_update(
        mixing_offsets, mixing_grad, mixing_first, mixing_second, count_now, 0.0
    )
    return (
        mixed.astype(BF),
        grad_inputs,
        grad_history.reshape(history.shape),
        *attention_step,
        *feedforward_step,
        *mixing_step,
    )


def shards(inputs, *others):
    row_count, span, width = inputs.shape
    tok_size = lax.axis_size("tok")
    devices = lax.axis_size("dp") * tok_size
    by_rows = row_count == tok_size == 4 and lax.axis_size("dp") == 8 and width == D
    if by_rows and all(plan.fits for plan in plans(devices)):
        return row_shards(inputs, *others)
    return general_shards(inputs, *others)


def solution(mesh):
    in_specs = (
        P("dp", "tok", None),
        P(None, "dp", "tok", None),
        P("dp", None),
        P("dp", "tok", None),
        P(("dp", "tok")),
        P(("dp", "tok")),
        P(("dp", "tok")),
        P(("dp", "tok")),
        P(("dp", "tok")),
        P(("dp", "tok")),
        P(),
        P(),
        P(),
        P(),
    )
    out_specs = (
        P("dp", "tok", None),
        P("dp", "tok", None),
        P(None, "dp", "tok", None),
        P(("dp", "tok")),
        P(("dp", "tok")),
        P(("dp", "tok")),
        P(("dp", "tok")),
        P(("dp", "tok")),
        P(("dp", "tok")),
        P(),
        P(),
        P(),
    )
    return jax.shard_map(shards, mesh=mesh, in_specs=in_specs, out_specs=out_specs, check_vma=False)
```

```python
from functools import partial
import math

import jax
import jax.numpy as jnp
from jax import lax
from jax.experimental import pallas as pl
from jax.experimental.pallas import tpu as pltpu
from jax.sharding import PartitionSpec as P

D = 768
HEADS = 12
HEAD_DIM = 64
FF = 3072
DOCS = 7


beta_first = 0.9
beta_second = 0.95
learning_rate = 0.05
decay_rate = 0.1
adam_epsilon = 1e-08
norm_epsilon = 1e-05
masked_score = -1e30


def layer_norm(values, gain, shift):
    centered = values - jnp.mean(values, axis=-1, keepdims=True)
    variance = jnp.mean(centered * centered, axis=-1, keepdims=True)
    return centered * lax.rsqrt(variance + norm_epsilon) * gain + shift


def rotate(values, position):
    half_dim = values.shape[-1] // 2
    frequency = jnp.exp(
        jnp.arange(half_dim, dtype=jnp.float32) * (-2.0 * math.log(10000.0) / values.shape[-1])
    )
    angle = position.astype(jnp.float32)[..., None] * frequency
    cosine = jnp.cos(angle)[..., None, :]
    sine = jnp.sin(angle)[..., None, :]
    first_half = values[..., :half_dim]
    second_half = values[..., half_dim:]
    return jnp.concatenate(
        [first_half * cosine - second_half * sine, second_half * cosine + first_half * sine],
        axis=-1,
    )


def turn_back(gradient_part, position):
    return jax.vjp(partial(rotate, position=position), gradient_part)[1](gradient_part)[0]


def layout(lengths_rows, places):
    ends = jnp.cumsum(lengths_rows, axis=1)
    starts = ends - lengths_rows
    doc_count = lengths_rows.shape[1] - 1
    inside = places[None, :, None] >= ends[:, None, :doc_count]
    segment = jnp.sum(inside.astype(jnp.int32), axis=2)
    labels = jnp.arange(doc_count + 1, dtype=jnp.int32)
    chosen = segment[:, :, None] == labels[None, None, :]
    begin = jnp.sum(jnp.where(chosen, starts[:, None, :], 0), axis=2)
    return (segment, places[None, :] - begin)


def allowed_mask(segment_row, first_row, query_count):
    query_place = first_row + jnp.arange(query_count, dtype=jnp.int32)
    key_place = jnp.arange(segment_row.shape[0], dtype=jnp.int32)
    query_segment = lax.dynamic_slice_in_dim(segment_row, first_row, query_count, 0)
    earlier = key_place[None, :] <= query_place[:, None]
    same_doc = segment_row[None, :] == query_segment[:, None]
    real_key = (segment_row[None, :] < DOCS) | (key_place[None, :] == query_place[:, None])
    return earlier & same_doc & real_key


def block_scores(queries, keys_all, segment_row, first_row):
    scores = jnp.einsum(
        "qhd,khd->hqk", queries, keys_all, preferred_element_type=jnp.float32
    ) * HEAD_DIM ** (-0.5)
    allowed = allowed_mask(segment_row, first_row, queries.shape[0])
    return jnp.where(allowed[None], scores, masked_score)


def attention_shapes():
    return [(D,), (D,), (D, 3 * D), (3 * D,), (D, D), (D,)]


def feedforward_shapes():
    return [(D,), (D,), (D, FF), (FF,), (FF, D), (D,)]


def unpack(flat_vector, shape_list):
    pieces = []
    offset_at = 0
    for piece_shape in shape_list:
        piece_size = math.prod(piece_shape)
        pieces.append(flat_vector[offset_at : offset_at + piece_size].reshape(piece_shape))
        offset_at = offset_at + piece_size
    return pieces


def decay_mask(places, shape_list):
    mask_values = jnp.zeros(places.shape, jnp.float32)
    offset_at = 0
    for piece_shape in shape_list:
        piece_size = math.prod(piece_shape)
        if len(piece_shape) == 2:
            inside = (places >= offset_at) & (places < offset_at + piece_size)
            mask_values = mask_values + inside.astype(jnp.float32)
        offset_at = offset_at + piece_size
    return mask_values * decay_rate


def adam_update(values, gradient, moment_one, moment_two, step_number, decay_values):
    first_new = beta_first * moment_one + (1.0 - beta_first) * gradient
    second_new = beta_second * moment_two + (1.0 - beta_second) * gradient * gradient
    power_now = step_number.astype(jnp.float32)
    fix_one = 1.0 - jnp.power(beta_first, power_now)
    fix_two = 1.0 - jnp.power(beta_second, power_now)
    step_size = first_new / fix_one / (jnp.sqrt(second_new / fix_two) + adam_epsilon)
    return (values - learning_rate * (step_size + decay_values * values), first_new, second_new)


def to_groups(values, subsets):
    full_shape = values.shape
    row_total = full_shape[0]
    half_width = full_shape[-1] // 2
    split_view = values.reshape(
        (subsets, row_total // subsets) + full_shape[1:-1] + (2, half_width)
    )
    moved = jnp.moveaxis(split_view, -2, 0)
    return moved.reshape((2 * subsets, row_total // subsets) + full_shape[1:-1] + (half_width,))


def from_groups(values, subsets):
    full_shape = values.shape
    split_view = values.reshape((2, subsets) + full_shape[1:])
    moved = jnp.moveaxis(split_view, 0, -2)
    return moved.reshape((subsets * full_shape[1],) + full_shape[2:-1] + (2 * full_shape[-1],))


def attend_rows(head_qkv, head_segment):
    item_count = head_qkv.shape[1]
    length_all = head_qkv.shape[2]
    group_width = head_qkv.shape[4]
    head_count = group_width // HEAD_DIM
    block_rows = min(512, length_all)
    block_count = length_all // block_rows
    rows_qkv = head_qkv.reshape(item_count, length_all, 3, head_count, HEAD_DIM)
    rows_segment = head_segment.reshape(item_count, length_all)

    def attend_one_block(block_index):
        row_index = block_index // block_count
        first_row = block_index % block_count * block_rows
        current = rows_qkv[row_index]
        queries = lax.dynamic_slice_in_dim(current[:, 0], first_row, block_rows, 0)
        masked = block_scores(queries, current[:, 1], rows_segment[row_index], first_row)
        top_score = jnp.max(masked, axis=2, keepdims=True)
        exponent = jnp.exp(masked - top_score)
        total_weight = jnp.sum(exponent, axis=2, keepdims=True)
        soft_weights = (exponent / total_weight).astype(jnp.bfloat16)
        attended = jnp.einsum(
            "hqk,khd->qhd", soft_weights, current[:, 2], preferred_element_type=jnp.float32
        )
        log_total = (top_score + jnp.log(total_weight))[:, :, 0]
        return (attended.reshape(block_rows, group_width).astype(jnp.bfloat16), log_total)

    outputs, log_totals = lax.map(
        attend_one_block, jnp.arange(item_count * block_count, dtype=jnp.int32)
    )
    return (
        outputs.reshape(1, item_count, length_all, group_width),
        log_totals.reshape(1, item_count, block_count, head_count, block_rows),
    )


def attend_back(head_qkv, head_segment, log_totals, head_grads):
    item_count = head_qkv.shape[1]
    length_all = head_qkv.shape[2]
    group_width = head_qkv.shape[4]
    head_count = group_width // HEAD_DIM
    block_rows = min(512, length_all)
    block_count = length_all // block_rows
    scale_value = HEAD_DIM ** (-0.5)

    def one_row(pieces):
        current, segment_row, log_row, grad_row = pieces
        keys_all = current[:, 1]
        values_all = current[:, 2]

        def one_one_block(carried, block_index):
            first_row = block_index * block_rows
            queries = lax.dynamic_slice_in_dim(current[:, 0], first_row, block_rows, 0)
            grad_block = lax.dynamic_slice_in_dim(grad_row, first_row, block_rows, 0)
            masked = block_scores(queries, keys_all, segment_row, first_row)
            soft_weights = jnp.exp(masked - log_row[block_index][:, :, None])
            grad_weights = jnp.einsum(
                "qhd,khd->hqk", grad_block, values_all, preferred_element_type=jnp.float32
            )
            inner_sum = jnp.sum(soft_weights * grad_weights, axis=2, keepdims=True)
            grad_scores = (soft_weights * (grad_weights - inner_sum)).astype(jnp.bfloat16)
            grad_query = (
                jnp.einsum(
                    "hqk,khd->qhd", grad_scores, keys_all, preferred_element_type=jnp.float32
                )
                * scale_value
            )
            grad_key = (
                carried[0]
                + jnp.einsum(
                    "hqk,qhd->khd", grad_scores, queries, preferred_element_type=jnp.float32
                )
                * scale_value
            )
            grad_value = carried[1] + jnp.einsum(
                "hqk,qhd->khd",
                soft_weights.astype(jnp.bfloat16),
                grad_block,
                preferred_element_type=jnp.float32,
            )
            return ((grad_key, grad_value), grad_query)

        empty_grad = jnp.zeros((length_all, head_count, HEAD_DIM), jnp.float32)
        (grad_key, grad_value), grad_query = lax.scan(
            one_one_block, (empty_grad, empty_grad), jnp.arange(block_count, dtype=jnp.int32)
        )
        grad_query = grad_query.reshape(length_all, head_count, HEAD_DIM)
        return jnp.stack([grad_query, grad_key, grad_value], axis=1).astype(jnp.bfloat16)

    row_grads = lax.map(
        one_row,
        (
            head_qkv.reshape(item_count, length_all, 3, head_count, HEAD_DIM),
            head_segment.reshape(item_count, length_all),
            log_totals.reshape(item_count, block_count, head_count, block_rows),
            head_grads.reshape(item_count, length_all, head_count, HEAD_DIM),
        ),
    )
    return row_grads.reshape(1, item_count, length_all, 3, group_width)


def general_shards(
    inputs,
    history,
    document_lengths,
    cotangent,
    attention_params,
    attention_first,
    attention_second,
    feedforward_params,
    feedforward_first,
    feedforward_second,
    mixing_offsets,
    mixing_first,
    mixing_second,
    step_count,
):
    row_count, token_span, model_width = inputs.shape
    subsets = lax.axis_size("tok") // 2
    per_device = row_count // subsets
    tokens_all = row_count * token_span * lax.axis_size("dp") * lax.axis_size("tok")
    attention_flat, feedforward_flat = (
        lax.all_gather(attention_params.astype(jnp.bfloat16), ("dp", "tok"), axis=0, tiled=True),
        lax.all_gather(feedforward_params.astype(jnp.bfloat16), ("dp", "tok"), axis=0, tiled=True),
    )
    gain_one, shift_one, w_qkv, b_qkv, w_out, b_out = unpack(attention_flat, attention_shapes())
    gain_two, shift_two, w_up, b_up, w_down, b_down = unpack(feedforward_flat, feedforward_shapes())
    gain_one = gain_one.astype(jnp.float32)
    shift_one = shift_one.astype(jnp.float32)
    gain_two = gain_two.astype(jnp.float32)
    shift_two = shift_two.astype(jnp.float32)
    places = lax.axis_index("tok") * token_span + jnp.arange(token_span, dtype=jnp.int32)
    segment, position = layout(document_lengths, places)
    current = inputs.astype(jnp.float32)
    normed_one = layer_norm(current, gain_one, shift_one).astype(jnp.bfloat16)
    project = jnp.dot(normed_one, w_qkv, preferred_element_type=jnp.float32) + b_qkv.astype(
        jnp.float32
    )
    project = project.reshape(row_count, token_span, 3, HEADS, HEAD_DIM)
    queries = rotate(project[:, :, 0], position)
    keys_all = rotate(project[:, :, 1], position)
    packed = jnp.stack([queries, keys_all, project[:, :, 2]], axis=2).astype(jnp.bfloat16)
    send_qkv = to_groups(packed.reshape(row_count, token_span, 3, model_width), subsets)
    send_segment = jnp.broadcast_to(
        segment.reshape(1, subsets, per_device, token_span), (2, subsets, per_device, token_span)
    ).reshape(2 * subsets, per_device, token_span)
    head_qkv = lax.all_to_all(send_qkv, "tok", split_axis=0, concat_axis=2, tiled=True)
    head_segment = lax.all_to_all(send_segment, "tok", split_axis=0, concat_axis=2, tiled=True)
    outputs, log_totals = attend_rows(head_qkv, head_segment)
    returned = lax.all_to_all(outputs, "tok", split_axis=2, concat_axis=0, tiled=True)
    returned, head_qkv, head_segment, log_totals = (returned, head_qkv, head_segment, log_totals)
    attended = from_groups(returned, subsets)
    hidden = (
        current
        + jnp.dot(attended, w_out, preferred_element_type=jnp.float32)
        + b_out.astype(jnp.float32)
    )
    normed_two = layer_norm(hidden, gain_two, shift_two).astype(jnp.bfloat16)
    up_value = jnp.dot(normed_two, w_up, preferred_element_type=jnp.float32) + b_up.astype(
        jnp.float32
    )
    active = jax.nn.gelu(up_value).astype(jnp.bfloat16)
    block_out = (
        hidden
        + jnp.dot(active, w_down, preferred_element_type=jnp.float32)
        + b_down.astype(jnp.float32)
    )
    term_count = mixing_offsets.shape[0]
    coefficient = mixing_offsets + (jnp.arange(term_count) == term_count - 1).astype(jnp.float32)
    history_part = jnp.einsum(
        "j,jrtd->rtd", coefficient[:-1], history, preferred_element_type=jnp.float32
    )
    mixed = (history_part + coefficient[-1] * block_out).astype(jnp.bfloat16)
    grad_mixed = cotangent.astype(jnp.float32)
    grad_history = coefficient[:-1, None, None, None] * grad_mixed[None]
    history_terms = jnp.einsum(
        "jrtd,rtd->j", history, grad_mixed, preferred_element_type=jnp.float32
    )
    mixing_terms = jnp.concatenate([history_terms, jnp.sum(block_out * grad_mixed)[None]])
    mixing_grad = lax.psum(mixing_terms, ("dp", "tok")) / tokens_all
    grad_block = coefficient[-1] * grad_mixed
    grad_branch = grad_block.astype(jnp.bfloat16)
    grad_w_down = jnp.einsum("rtf,rtd->fd", active, grad_branch, preferred_element_type=jnp.float32)
    grad_b_down = jnp.sum(grad_branch.astype(jnp.float32), axis=(0, 1))
    grad_active = jnp.einsum("rtd,fd->rtf", grad_branch, w_down, preferred_element_type=jnp.float32)
    grad_up = jax.vjp(jax.nn.gelu, up_value)[1](grad_active)[0].astype(jnp.bfloat16)
    grad_w_up = jnp.einsum("rtd,rtf->df", normed_two, grad_up, preferred_element_type=jnp.float32)
    grad_b_up = jnp.sum(grad_up.astype(jnp.float32), axis=(0, 1))
    grad_normed_two = jnp.einsum("rtf,df->rtd", grad_up, w_up, preferred_element_type=jnp.float32)
    grad_hidden_norm, grad_gain_two, grad_shift_two = jax.vjp(
        layer_norm, hidden, gain_two, shift_two
    )[1](grad_normed_two)
    grad_hidden = grad_block + grad_hidden_norm
    feedforward_grad = jnp.concatenate(
        [
            grad_gain_two,
            grad_shift_two,
            grad_w_up.reshape(-1),
            grad_b_up,
            grad_w_down.reshape(-1),
            grad_b_down,
        ]
    )
    feedforward_share = lax.psum_scatter(
        feedforward_grad, ("dp", "tok"), scatter_dimension=0, tiled=True
    )
    grad_attn = grad_hidden.astype(jnp.bfloat16)
    grad_w_out = jnp.einsum("rtd,rte->de", attended, grad_attn, preferred_element_type=jnp.float32)
    grad_b_out = jnp.sum(grad_attn.astype(jnp.float32), axis=(0, 1))
    grad_attended = jnp.einsum(
        "rte,de->rtd", grad_attn, w_out, preferred_element_type=jnp.float32
    ).astype(jnp.bfloat16)
    head_grads = lax.all_to_all(
        to_groups(grad_attended, subsets), "tok", split_axis=0, concat_axis=2, tiled=True
    )
    head_back = attend_back(head_qkv, head_segment, log_totals, head_grads)
    token_back = from_groups(
        lax.all_to_all(head_back, "tok", split_axis=2, concat_axis=0, tiled=True), subsets
    )
    token_back = token_back.astype(jnp.float32).reshape(row_count, token_span, 3, HEADS, HEAD_DIM)
    grad_project = jnp.stack(
        [
            turn_back(token_back[:, :, 0], position),
            turn_back(token_back[:, :, 1], position),
            token_back[:, :, 2],
        ],
        axis=2,
    )
    grad_project = grad_project.reshape(row_count, token_span, 3 * model_width).astype(jnp.bfloat16)
    grad_w_qkv = jnp.einsum(
        "rtd,rte->de", normed_one, grad_project, preferred_element_type=jnp.float32
    )
    grad_b_qkv = jnp.sum(grad_project.astype(jnp.float32), axis=(0, 1))
    grad_normed_one = jnp.einsum(
        "rte,de->rtd", grad_project, w_qkv, preferred_element_type=jnp.float32
    )
    grad_current, grad_gain_one, grad_shift_one = jax.vjp(layer_norm, current, gain_one, shift_one)[
        1
    ](grad_normed_one)
    grad_inputs = grad_hidden + grad_current
    attention_grad = jnp.concatenate(
        [
            grad_gain_one,
            grad_shift_one,
            grad_w_qkv.reshape(-1),
            grad_b_qkv,
            grad_w_out.reshape(-1),
            grad_b_out,
        ]
    )
    attention_share = lax.psum_scatter(
        attention_grad, ("dp", "tok"), scatter_dimension=0, tiled=True
    )
    count_now = step_count[0]
    shard_index = lax.axis_index(("dp", "tok"))
    attention_places = shard_index * attention_params.shape[0] + jnp.arange(
        attention_params.shape[0], dtype=jnp.int32
    )
    feedforward_places = shard_index * feedforward_params.shape[0] + jnp.arange(
        feedforward_params.shape[0], dtype=jnp.int32
    )
    attention_step = adam_update(
        attention_params,
        attention_share / tokens_all,
        attention_first,
        attention_second,
        count_now,
        decay_mask(attention_places, attention_shapes()),
    )
    feedforward_step = adam_update(
        feedforward_params,
        feedforward_share / tokens_all,
        feedforward_first,
        feedforward_second,
        count_now,
        decay_mask(feedforward_places, feedforward_shapes()),
    )
    mixing_step = adam_update(
        mixing_offsets, mixing_grad, mixing_first, mixing_second, count_now, 0.0
    )
    return (
        mixed,
        grad_inputs,
        grad_history,
        attention_step[0],
        attention_step[1],
        attention_step[2],
        feedforward_step[0],
        feedforward_step[1],
        feedforward_step[2],
        mixing_step[0],
        mixing_step[1],
        mixing_step[2],
    )


VMEM_LIMIT = 58 * 1024 * 1024
BF = jnp.bfloat16
F32 = jnp.float32


def cols(ref, first, count):
    lead = math.prod(ref.shape[:-3]) * ref.shape[-2]
    pieces = []
    for at in range(first, first + count):
        index = (slice(None),) * (len(ref.shape) - 3) + (at,)
        pieces.append(ref[index].reshape(lead, 128))
    return pieces[0] if count == 1 else jnp.concatenate(pieces, axis=1)


def put_tiles(ref, row_at, col_at, value):
    rows, width = value.shape
    for at in range(width // 128):
        ref[pl.ds(row_at, rows // 16), col_at + at] = value[:, 128 * at : 128 * at + 128].reshape(
            rows // 16, 16, 128
        )


def norm_parts(values):
    mean = jnp.mean(values, axis=1, keepdims=True)
    centered = values - mean
    inverse = lax.rsqrt(jnp.mean(centered * centered, axis=1, keepdims=True) + norm_epsilon)
    return centered, inverse


def nt_dot(left, right):
    return lax.dot_general(left, right, (((1,), (1,)), ((), ())), preferred_element_type=F32)


def nn_dot(left, right):
    return lax.dot_general(left, right, (((1,), (0,)), ((), ())), preferred_element_type=F32)


def swap_halves(values):
    width = values.shape[1]
    lane = lax.broadcasted_iota(jnp.int32, values.shape, 1)
    return jnp.where(
        lane % HEAD_DIM < HEAD_DIM // 2,
        pltpu.roll(values, width - HEAD_DIM // 2, 1),
        pltpu.roll(values, HEAD_DIM // 2, 1),
    )


def key_range(block, block_rows, reach):
    return max(0, block * block_rows - reach), (block + 1) * block_rows


def fill_bias(bias_ref, seg_col_ref, seg_row_ref, block_rows, reach):
    length = seg_row_ref.shape[1]
    at = 0
    for block in range(length // block_rows):
        low, high = key_range(block, block_rows, reach)
        shape = (high - low, block_rows)
        key_place = low + lax.broadcasted_iota(jnp.int32, shape, 0)
        query_place = block * block_rows + lax.broadcasted_iota(jnp.int32, shape, 1)
        key_seg = seg_col_ref[low:high, :]
        query_seg = seg_row_ref[:, block * block_rows : (block + 1) * block_rows]
        allowed = (key_place <= query_place) & (key_seg == query_seg)
        allowed = allowed & ((key_seg < DOCS) | (key_place == query_place))
        bias_ref[at : at + high - low, :] = jnp.where(allowed, 0.0, masked_score)
        at = at + high - low


def bias_rows(length, block_rows, reach):
    return sum(
        high - low
        for low, high in (key_range(b, block_rows, reach) for b in range(length // block_rows))
    )


def head_mask(values, head):
    lane = lax.broadcasted_iota(jnp.int32, values.shape, 1)
    keep = lane < HEAD_DIM if head == 0 else lane >= HEAD_DIM
    return jnp.where(keep, values, jnp.zeros_like(values))


gelu_root = math.sqrt(2.0 / math.pi)


def middle_kernel(
    x_ref, att_ref, cot_ref, wout_ref, wup_ref, wdown_ref, vec_ref, bup_ref, own_cot_ref, c_ref,
    ghist_ref, bout_ref, gatt_ref, ghid_ref, gwup_ref, gwdown_ref, gwout_ref, gbup_ref, gvec_ref,
    hidden_ref, n2_ref, n2t_ref, gb_ref, acc_out, acc_gn, act_ref, gup_ref,
):
    step = pl.program_id(0)
    steps = pl.num_programs(0)
    length, width = x_ref.shape
    tile = 256
    tiles = length // tile
    mix = c_ref[c_ref.shape[0] - 1]
    group = ghist_ref.shape[0]

    @pl.when(step == 0)
    def _():
        @pl.loop(0, tiles)
        def _(t):
            rows = pl.ds(pl.multiple_of(t * tile, tile), tile)
            attended = att_ref[rows, :]
            hidden = x_ref[rows, :].astype(F32) + nn_dot(attended, cols(wout_ref, 0, width // 128))
            hidden = hidden + vec_ref[2:3, :]
            hidden_ref[rows, :] = hidden
            centered, inverse = norm_parts(hidden)
            normed = (centered * inverse * vec_ref[0:1, :] + vec_ref[1:2, :]).astype(BF)
            n2_ref[rows, :] = normed
            n2t_ref[:, rows] = normed.T
            gb_ref[rows, :] = (mix * cot_ref[rows, :].astype(F32)).astype(BF)
            acc_out[rows, :] = jnp.zeros((tile, width), F32)
            acc_gn[rows, :] = jnp.zeros((tile, width), F32)

        gvec_ref[...] = jnp.zeros_like(gvec_ref)

    w_up = cols(wup_ref, 0, 4)
    w_down = cols(wdown_ref, 0, width // 128)
    part = step % 2
    rows = pl.ds(pl.multiple_of(part * (length // 2), length // 2), length // 2)
    up = nn_dot(n2_ref[rows, :], w_up) + bup_ref[0:1, :]
    square = up * up
    turn = jnp.tanh(gelu_root * up * (1.0 + 0.044715 * square))
    half = 0.5 * (1.0 + turn)
    active = (up * half).astype(BF)
    act_ref[rows, :] = active
    acc_out[rows, :] += nn_dot(active, w_down)
    slope = half + (0.5 * gelu_root) * up * (1.0 - turn * turn) * (1.0 + (3.0 * 0.044715) * square)
    grad_up = (nt_dot(gb_ref[rows, :], w_down) * slope).astype(BF)
    gup_ref[rows, :] = grad_up
    acc_gn[rows, :] += nt_dot(grad_up, w_up)
    part_sum = jnp.sum(grad_up.astype(F32), axis=0, keepdims=True)
    gbup_ref[0:1, :] = jnp.where(part == 0, 0.0, gbup_ref[0:1, :]) + part_sum

    @pl.loop(0, tiles)
    def _(t):
        rows = pl.ds(pl.multiple_of(t * tile, tile), tile)
        own_cot = own_cot_ref[rows, :].astype(F32)
        for j in range(group):
            ghist_ref[j, rows, :] = c_ref[step * group + j] * own_cot

    @pl.when(part == 1)
    def _():
        grad_up_all = gup_ref[...]
        for r in range(width // 256):
            turned = n2t_ref[256 * r : 256 * r + 256, :]
            put_tiles(gwup_ref, 16 * r, 0, nn_dot(turned, grad_up_all).astype(BF))
        active_turned = act_ref[...].T
        for r in range(width // 256):
            columns = gb_ref[:, 256 * r : 256 * r + 256]
            put_tiles(gwdown_ref, 0, 2 * r, nn_dot(active_turned, columns).astype(BF))

    @pl.when(step == steps - 1)
    def _():
        @pl.loop(0, tiles)
        def _(t):
            rows = pl.ds(pl.multiple_of(t * tile, tile), tile)
            hidden = hidden_ref[rows, :]
            cot = cot_ref[rows, :].astype(F32)
            block_out = hidden + acc_out[rows, :] + vec_ref[3:4, :]
            bout_ref[rows, :] = block_out.astype(bout_ref.dtype)
            gvec_ref[4:5, :] += jnp.sum(block_out * cot, axis=0, keepdims=True)
            centered, inverse = norm_parts(hidden)
            normed = centered * inverse
            grad_norm = acc_gn[rows, :]
            gvec_ref[0:1, :] += jnp.sum(normed * grad_norm, axis=0, keepdims=True)
            gvec_ref[1:2, :] += jnp.sum(grad_norm, axis=0, keepdims=True)
            scaled = grad_norm * vec_ref[0:1, :]
            grad_value = inverse * (
                scaled
                - jnp.mean(scaled, axis=1, keepdims=True)
                - normed * jnp.mean(scaled * normed, axis=1, keepdims=True)
            )
            grad_hidden = mix * cot + grad_value
            ghid_ref[rows, :] = grad_hidden
            grad_attn = grad_hidden.astype(BF)
            n2_ref[rows, :] = grad_attn
            n2t_ref[:, rows] = att_ref[rows, :].T
            gvec_ref[2:3, :] += jnp.sum(grad_attn.astype(F32), axis=0, keepdims=True)
            gvec_ref[3:4, :] += jnp.sum(gb_ref[rows, :].astype(F32), axis=0, keepdims=True)
            gatt_ref[rows, :] = nt_dot(grad_attn, cols(wout_ref, 0, width // 128)).astype(BF)

        grad_attn_all = n2_ref[...]
        for r in range(width // 256):
            for k in range(width // 256):
                put_tiles(
                    gwout_ref, 16 * r, 2 * k,
                    nn_dot(
                        n2t_ref[256 * r : 256 * r + 256, :],
                        grad_attn_all[:, 256 * k : 256 * k + 256],
                    ).astype(BF),
                )


def middle(x_row, attended, cot_row, w_out, w_up, w_down, vectors, b_up, own_cot, coefficient):
    length, width = x_row.shape
    (up_array, up_rows), (down_array, down_first), (out_array, out_rows) = w_up, w_down, w_out
    out_first = out_array.shape[0] // out_rows - 1
    inner = b_up.shape[1]
    steps = 2 * inner // 512
    terms = coefficient.shape[0] - 1
    once = pl.Buffered(1)

    def const(shape):
        return pl.BlockSpec(shape, lambda i: (0,) * len(shape), pipeline_mode=once)

    rows = const((length, width))
    row_tiles, col_tiles = width // 16, width // 128
    return pl.pallas_call(
        middle_kernel,
        grid=(steps,),
        in_specs=[
            rows, rows, rows,
            pl.BlockSpec(
                (out_rows,) + out_array.shape[1:], lambda i: (out_first, 0, 0, 0, 0), pipeline_mode=once
            ),
            pl.BlockSpec((up_rows, up_array.shape[1], 4, 16, 128), lambda i: (0, 0, i // 2, 0, 0)),
            pl.BlockSpec((32, col_tiles, 16, 128), lambda i: (i // 2 + down_first // 2, 0, 0, 0)),
            const(vectors.shape),
            pl.BlockSpec((1, 512), lambda i: (0, i // 2)),
            const(own_cot.shape),
            pl.BlockSpec(memory_space=pltpu.SMEM),
        ],
        out_specs=[
            pl.BlockSpec((terms // steps,) + own_cot.shape, lambda i: (i, 0, 0)),
            rows, rows, rows,
            pl.BlockSpec((row_tiles, 4, 16, 128), lambda i: (0, i // 2, 0, 0)),
            pl.BlockSpec((32, col_tiles, 16, 128), lambda i: (i // 2, 0, 0, 0)),
            const((row_tiles, col_tiles, 16, 128)),
            pl.BlockSpec((8, 512), lambda i: (0, i // 2)),
            const((8, width)),
        ],
        out_shape=[
            jax.ShapeDtypeStruct((terms,) + own_cot.shape, F32),
            jax.ShapeDtypeStruct((length, width), BF),
            jax.ShapeDtypeStruct((length, width), BF),
            jax.ShapeDtypeStruct((length, width), F32),
            jax.ShapeDtypeStruct((row_tiles, inner // 128, 16, 128), BF),
            jax.ShapeDtypeStruct((inner // 16, col_tiles, 16, 128), BF),
            jax.ShapeDtypeStruct((row_tiles, col_tiles, 16, 128), BF),
            jax.ShapeDtypeStruct((8, inner), F32),
            jax.ShapeDtypeStruct((8, width), F32),
        ],
        scratch_shapes=[
            pltpu.VMEM((length, width), F32),
            pltpu.VMEM((length, width), BF),
            pltpu.VMEM((width, length), BF),
            pltpu.VMEM((length, width), BF),
            pltpu.VMEM((length, width), F32),
            pltpu.VMEM((length, width), F32),
            pltpu.VMEM((length, 512), BF),
            pltpu.VMEM((length, 512), BF),
        ],
        compiler_params=pltpu.CompilerParams(vmem_limit_bytes=VMEM_LIMIT),
        name="middle",
    )(x_row, attended, cot_row, out_array, up_array, down_array, vectors, b_up, own_cot, coefficient)


def history_step(hist_ref, cot_ref, c_ref, first_term, part_ref, dots_ref):
    group, tile, width = hist_ref.shape
    mixes = [c_ref[first_term + j] for j in range(group)]

    def chunk(r, dots):
        rows = pl.ds(pl.multiple_of(r * 16, 16), 16)
        total = part_ref[rows, :]
        cot = cot_ref[rows, :].astype(F32)
        new = []
        for j in range(group):
            past = hist_ref[j, rows, :].astype(F32)
            total = total + mixes[j] * past
            both = past * cot
            both = both[:8] + both[8:]
            added = dots[j]
            for k in range(width // 128):
                added = added + both[:, 128 * k : 128 * k + 128]
            new.append(added)
        part_ref[rows, :] = total
        return tuple(new)

    dots = lax.fori_loop(0, tile // 16, chunk, tuple(jnp.zeros((8, 128), F32) for _ in range(group)))
    for j in range(group):
        dots_ref[0, 8 * j : 8 * j + 8, :] = dots[j]


gather_cuts, gather_share, enter_share = 2, 0.5, 3
gather_steps = ((2, 3, 3, 4), (9, 9, 10), (15, 16, 18), (19,), (23, 24, 27), (28,), (31,))
enter_first_steps, enter_second_steps, enter_rows_step = (4, 7, 10, 13), (16, 19, 23, 27), 14
finish_cuts, finish_share = 3, 3
leave_steps, leave_share, leave_rows_steps = (5, 10, 16, 22, 29, 33, 36), 3, (0, 18, 25)
MESH_ID = pl.DeviceIdType.MESH
DMA = pltpu.SemaphoreType.DMA
HBM = pl.BlockSpec(memory_space=pl.ANY)
EVERY = slice(None)


class Place:
    def __init__(self, depth):
        dp, tok = lax.axis_index("dp"), lax.axis_index("tok")
        self.depth = depth
        self.z, self.x, self.y, self.c = dp // 2, dp % 2, tok // 2, tok % 2
        self.tok = tok
        self.along_x = (self.z * 2 + 1 - self.x, tok)
        self.along_y = (dp, (1 - self.y) * 2 + self.c)
        self.along_c = (dp, self.y * 2 + 1 - self.c)
        self.across = (dp, (1 - self.y) * 2 + 1 - self.c)
        self.near_z = ((self.z + 1 - 2 * (self.z % 2)) * 2 + self.x, tok)
        self.mid_z = ((depth - 1 - self.z) * 2 + self.x, tok)

    def along_z(self, step):
        return (lax.rem(self.z + step, self.depth) * 2 + self.x, self.tok)

    def row_partners(self):
        return [self.along_c, self.along_y, self.across]

    def greet(self):
        partners = [self.along_x] + self.row_partners()
        partners = partners + [self.along_z(r) for r in range(1, self.depth)]
        barrier = pltpu.get_barrier_semaphore()
        for partner in partners:
            pl.semaphore_signal(barrier, inc=1, device_id=partner, device_id_type=MESH_ID)
        pl.semaphore_wait(barrier, len(partners))


def remote(src, dst, send, recv, target):
    return pltpu.make_async_remote_copy(
        src_ref=src, dst_ref=dst, send_sem=send, recv_sem=recv,
        device_id=target, device_id_type=MESH_ID,
    )


class LineGather:
    def __init__(self, me, items, blocks, spots, sems):
        self.me, self.items, self.blocks, self.spots = me, items, blocks, spots
        self.send, self.recv, self.local = sems
        self.inner = (me.z == 1) | (me.z == 2)

    def scratch(items, arrays):
        return [DMA((len(items), 3)), DMA((len(items), 3)), DMA((arrays,))]

    def copy(self, i, hop):
        which, low, count = self.items[i]
        me, spot, half = self.me, pl.ds(low, count), self.me.z // 2
        sems = (self.send.at[i, hop], self.recv.at[i, hop])
        if hop == 0:
            return remote(
                self.blocks[which].at[spot], self.spots[which](me.z, spot), *sems, me.near_z
            )
        view = self.spots[which](pl.ds(2 * half if hop == 1 else 2 * (1 - half), 2), spot)
        return remote(view, view, *sems, me.mid_z if hop == 1 else me.near_z)

    def own(self, which):
        whole = pl.ds(0, self.blocks[which].shape[0])
        return pltpu.make_async_copy(
            self.blocks[which], self.spots[which](self.me.z, whole), self.local.at[which]
        )

    def begin(self):
        for which in range(len(self.blocks)):
            self.own(which).start()

    def first_hop(self, i):
        self.copy(i, 0).start()

    def own_wait(self):
        for which in range(len(self.blocks)):
            self.own(which).wait()

    def inner_hop(self, i):
        if i == 0:
            self.own_wait()
        self.copy(i, 0).wait_recv()
        pl.when(self.inner)(lambda: self.copy(i, 1).start())

    def outer_hop(self, i):
        @pl.when(self.inner)
        def _():
            self.copy(i, 1).wait_recv()
            self.copy(i, 2).start()

    def arrived(self, i):
        pl.when(jnp.logical_not(self.inner))(lambda: self.copy(i, 2).wait_recv())

    def drain(self):
        for i in range(len(self.items)):
            self.copy(i, 0).wait_send()

            @pl.when(self.inner)
            def _(i=i):
                self.copy(i, 1).wait_send()
                self.copy(i, 2).wait_send()


class PlaneGather:
    def __init__(self, me, items, gathered, sems):
        self.me, self.items, self.gathered = me, items, gathered
        self.send, self.recv, self.core_send, self.core_recv = sems

    def scratch(items):
        n = len(items)
        return [DMA((n, 4)), DMA((n, 4)), DMA((n,)), DMA((n,))]

    def parts(self, i):
        _, _, count, first = self.items[i]
        return [part for part, size in ((0, first), (1, count - first)) if size]

    def copy(self, i, stage, part):
        which, low, count, first = self.items[i]
        me = self.me
        spot = pl.ds(low, first) if part == 0 else pl.ds(low + first, count - first)
        if stage == 0:
            index = (EVERY, me.x, me.y, me.c, spot)
        elif part == 0:
            index = (EVERY, EVERY, me.y, me.c, spot)
        else:
            index = (EVERY, me.x, EVERY, me.c, spot)
        view = self.gathered[which].at[index]
        at = 2 * stage + part
        target = me.along_x if stage == part else me.along_y
        return remote(view, view, self.send.at[i, at], self.recv.at[i, at], target)

    def core_copy(self, i):
        which, low, count, _ = self.items[i]
        view = self.gathered[which].at[EVERY, EVERY, EVERY, self.me.c, pl.ds(low, count)]
        return remote(view, view, self.core_send.at[i], self.core_recv.at[i], self.me.along_c)

    def first(self, i):
        for part in self.parts(i):
            self.copy(i, 0, part).start()

    def second(self, i):
        for part in self.parts(i):
            self.copy(i, 0, part).wait_recv()
            self.copy(i, 1, part).start()

    def third(self, i):
        for part in self.parts(i):
            self.copy(i, 1, part).wait_recv()
        self.core_copy(i).start()

    def drain(self):
        for i in range(len(self.items)):
            self.core_copy(i).wait_recv()
            for part in self.parts(i):
                self.copy(i, 0, part).wait_send()
                self.copy(i, 1, part).wait_send()
            self.core_copy(i).wait_send()


class RowExchange:
    def __init__(self, me, source, target, sems, back):
        self.me, self.source, self.target, self.back = me, source, target, back
        self.send, self.recv, self.local = sems
        self.span = (target if back else source).shape[1]

    def scratch():
        return [DMA((3,)), DMA((3,)), DMA((1,))]

    def views(self, tok):
        mine = pl.ds(self.me.tok * self.span, self.span)
        if self.back:
            return self.source.at[pl.ds(tok * self.span, self.span)], self.target.at[self.me.tok]
        return self.source.at[tok], self.target.at[mine]

    def copy(self, p):
        target = self.me.row_partners()[p]
        return remote(*self.views(target[1]), self.send.at[p], self.recv.at[p], target)

    def own(self):
        return pltpu.make_async_copy(*self.views(self.me.tok), self.local.at[0])

    def begin(self, parts=(0, 1, 2)):
        for p in parts:
            if p == 0:
                self.own().start()
            self.copy(p).start()

    def drain(self):
        self.own().wait()
        for p in range(3):
            self.copy(p).wait()


class SmallSum:
    def __init__(self, me, source, out, refs):
        self.me, self.source, self.out = me, source, out
        self.held, self.got, self.line, self.send, self.recv = refs
        self.ways = (me.along_c, me.along_y, me.along_x)

    def scratch(shape, depth):
        return [
            pltpu.VMEM((4,) + shape, F32), pltpu.VMEM((3,) + shape, F32),
            pltpu.VMEM((depth,) + shape, F32), DMA((2 + depth,)), DMA((2 + depth,)),
        ]

    def copy(self, n):
        return remote(
            self.held.at[n], self.got.at[n], self.send.at[n], self.recv.at[n], self.ways[n]
        )

    def line_copy(self, r):
        return remote(
            self.held.at[3], self.line.at[self.me.z], self.send.at[2 + r], self.recv.at[2 + r],
            self.me.along_z(r),
        )

    def begin(self):
        self.held[0] = self.source[...]
        self.copy(0).start()

    def stage(self, n):
        depth = self.me.depth
        if n < 3:
            self.copy(n).wait_recv()
            self.held[n + 1] = self.held[n] + self.got[n]
        if n < 2:
            self.copy(n + 1).start()
        elif n == 2:
            self.line[self.me.z] = self.held[3]
            for r in range(1, depth):
                self.line_copy(r).start()
        else:
            for r in range(1, depth):
                self.line_copy(r).wait_recv()
            total = self.line[0]
            for z in range(1, depth):
                total = total + self.line[z]
            self.out[...] = total

    def drain(self):
        for n in range(3):
            self.copy(n).wait_send()
        for r in range(1, self.me.depth):
            self.line_copy(r).wait_send()


class Reduce:
    def __init__(self, me, items, mid, grads, out, refs):
        self.me, self.items, self.grads, self.out = me, items, grads, out
        (
            self.own_buf, self.core_buf, s1a, s1b, r1a, r1b, s2a, s2b, r2a, r2b, self.s3, self.r3,
            self.c_send, self.c_recv, self.m_send, self.m_recv, self.z_send, self.z_recv, self.local,
        ) = refs
        self.sends = ((s1a, s1b), (s2a, s2b))
        self.recvs = ((r1a, r1b), (r2a, r2b))
        self.tiles = (slice(0, mid), slice(mid, items[0][1]))
        self.bits = ((me.y, me.x), (me.x, me.y))
        self.ways = ((me.along_y, me.along_x), (me.along_x, me.along_y))

    def scratch(items, mid, depth, arrays):
        n, count = len(items), items[0][1]

        def tiles(lead, size):
            return pltpu.VMEM((n, lead, size, 16, 128), BF)

        made = [tiles(4 * depth, count), tiles(4 * depth, count)]
        for lead in (2 * depth, depth):
            made += [tiles(lead, size) for size in (mid, count - mid)] * 2
        made += [tiles(depth - 1, count), tiles(depth - 1, count)]
        made += [DMA((n, arrays)), DMA((n, arrays)), DMA((n, 4)), DMA((n, 4))]
        return made + [DMA((n, depth - 1)), DMA((n, depth - 1)), DMA((n, arrays))]

    def pieces(self, i):
        low, count = self.items[i]
        at = 0
        for n, array in enumerate(self.grads):
            yield n, array, pl.ds(low, count), pl.ds(at, array.shape[0])
            at = at + array.shape[0]

    def core_copies(self, i):
        for n, array, spot, place in self.pieces(i):
            yield remote(
                array.at[:, 1 - self.me.c, spot], self.core_buf.at[i, place],
                self.c_send.at[i, n], self.c_recv.at[i, n], self.me.along_c,
            )

    def own_copies(self, i):
        for n, array, spot, place in self.pieces(i):
            yield pltpu.make_async_copy(
                array.at[:, self.me.c, spot], self.own_buf.at[i, place], self.local.at[i, n]
            )

    def side_copy(self, i, part, stage):
        at = 2 * stage + part
        return remote(
            self.sends[stage][part].at[i], self.recvs[stage][part].at[i],
            self.m_send.at[i, at], self.m_recv.at[i, at], self.ways[part][stage],
        )

    def line_copy(self, i, r):
        return remote(
            self.s3.at[i, r - 1], self.r3.at[i, r - 1], self.z_send.at[i, r - 1],
            self.z_recv.at[i, r - 1], self.me.along_z(r),
        )

    def slot(self, part, j, bit):
        return 2 * j + bit if part == 0 else (j // 2) * 4 + 2 * bit + j % 2

    def pair_sum(self, i, part, slot):
        spot = self.tiles[part]
        return self.own_buf[i, slot, spot].astype(F32) + self.core_buf[i, slot, spot].astype(F32)

    def plane_sum(self, i, part, j):
        slot = self.slot(part, j, self.bits[part][0])
        return self.pair_sum(i, part, slot) + self.recvs[0][part][i, j].astype(F32)

    def chip_sum(self, i, part, k):
        total = self.plane_sum(i, part, 2 * k + self.bits[part][1])
        return total + self.recvs[1][part][i, k].astype(F32)

    def begin(self):
        for i in range(len(self.items)):
            for copy in self.core_copies(i):
                copy.start()
            for copy in self.own_copies(i):
                copy.start()

    def core_stage(self, i):
        for copy in self.core_copies(i):
            copy.wait_recv()
        for copy in self.own_copies(i):
            copy.wait()
        for part in range(2):

            def one(j, _, part=part):
                slot = self.slot(part, j, 1 - self.bits[part][0])
                self.sends[0][part][i, j] = self.pair_sum(i, part, slot).astype(BF)
                return 0

            lax.fori_loop(0, 2 * self.me.depth, one, 0)
            self.side_copy(i, part, 0).start()

    def first_stage(self, i):
        for part in range(2):
            self.side_copy(i, part, 0).wait_recv()

            def one(k, _, part=part):
                j = 2 * k + 1 - self.bits[part][1]
                self.sends[1][part][i, k] = self.plane_sum(i, part, j).astype(BF)
                return 0

            lax.fori_loop(0, self.me.depth, one, 0)
            self.side_copy(i, part, 1).start()

    def second_stage(self, i):
        for part in range(2):
            self.side_copy(i, part, 1).wait_recv()
        for r in range(1, self.me.depth):
            other = lax.rem(self.me.z + r, self.me.depth)
            for part in range(2):
                self.s3[i, r - 1, self.tiles[part]] = self.chip_sum(i, part, other).astype(BF)
            self.line_copy(i, r).start()

    def line_stage(self, i):
        for r in range(1, self.me.depth):
            self.line_copy(i, r).wait_recv()
        for part in range(2):
            total = self.chip_sum(i, part, self.me.z)
            for r in range(1, self.me.depth):
                total = total + self.r3[i, r - 1, self.tiles[part]].astype(F32)
            self.out[i, self.tiles[part]] = total

    def drain(self):
        for i in range(len(self.items)):
            for copy in self.core_copies(i):
                copy.wait_send()
            for part in range(2):
                self.side_copy(i, part, 0).wait_send()
                self.side_copy(i, part, 1).wait_send()
            for r in range(1, self.me.depth):
                self.line_copy(i, r).wait_send()

    def rounds(self):
        n = len(self.items)
        made = [[partial(self.core_stage, 0), partial(self.core_stage, 1)]]
        for t in range(1, n + 3):
            order = ((self.first_stage, t - 1), (self.core_stage, t + 1))
            order = order + ((self.second_stage, t - 2), (self.line_stage, t - 3))
            made.append([partial(stage, i) for stage, i in order if 0 <= i < n])
        return made


class Taker:
    def __init__(self, refs):
        self.refs, self.at = refs, 0

    def __call__(self, count=None):
        if count is None:
            return self(1)[0]
        self.at = self.at + count
        return self.refs[self.at - count : self.at]


def at_steps(step, work):
    for when, one in work:
        pl.when(step == when)(one)


def kernel_params(collective_id=None):
    if collective_id is None:
        return pltpu.CompilerParams(vmem_limit_bytes=VMEM_LIMIT)
    return pltpu.CompilerParams(
        vmem_limit_bytes=VMEM_LIMIT, collective_id=collective_id, has_side_effects=True
    )


def gather_kernel(depth, line_items, plane_items, steps, when, hist_ref, cot_ref, c_ref, *refs):
    take = Taker(refs)
    blocks = take(3)
    rows_in = take()
    part_ref, dots_ref = take(2)
    got_a, got_e, got_f, rows_out = take(4)
    step = pl.program_id(0) * pl.num_programs(1) + pl.program_id(1)
    me = Place(depth)
    spots = [
        lambda z, spot: got_a.at[z, me.x, me.y, me.c, spot],
        lambda z, spot: got_e.at[z, me.x, me.y, me.c, spot],
        lambda z, spot: got_f.at[z, me.x, me.y, me.c, spot],
    ]
    line = LineGather(me, line_items, blocks, spots, take(3))
    plane = PlaneGather(me, plane_items, [got_a, got_e], take(4))
    rows = RowExchange(me, rows_in, rows_out, take(3), False)

    few = len(plane_items)
    later = range(few, len(line_items))

    def begin():
        me.greet()
        line.begin()
        for i in range(few):
            line.first_hop(i)
        rows.begin()

    def arrived(i):
        line.arrived(i)
        if i < few:
            plane.first(i)

    def end():
        plane.drain()
        rows.drain()
        line.drain()

    at_steps(step, [(0, begin)])

    @pl.when(pl.program_id(1) == 0)
    def _():
        part_ref[...] = jnp.zeros_like(part_ref)

    group = hist_ref.shape[0]
    history_step(hist_ref, cot_ref, c_ref, pl.program_id(1) * group, part_ref, dots_ref)
    groups = [
        [partial(line.inner_hop, i) for i in range(few)] + [partial(line.first_hop, i) for i in later],
        [partial(line.outer_hop, i) for i in range(few)],
        [partial(arrived, i) for i in range(few)],
        [partial(line.inner_hop, i) for i in later],
        [partial(plane.second, i) for i in range(few)],
        [partial(line.outer_hop, i) for i in later],
        [partial(plane.third, i) for i in range(few)] + [partial(arrived, i) for i in later] + [end],
    ]
    work = []
    for starts, group_work in zip(when, groups):
        for at, one in enumerate(group_work):
            work.append((min(starts[min(at, len(starts) - 1)], steps - 1), one))
    at_steps(step, work)


def gather(blocks, inputs, history, cotangent, coefficient, depth):
    terms, tokens, width = history.shape
    row_count, span, _ = inputs.shape
    tile, group = 128, 6
    count_a, count_e, count_f = (b.shape[0] for b in blocks)
    part = count_a // gather_cuts
    half = count_f // 2
    line_items = [(1, 0, count_e)] + [(0, low, part) for low in range(0, count_a, part)]
    line_items = line_items + [(2, low, half) for low in range(0, count_f, half)]
    plane_items = [(1, 0, count_e, count_e)] + [(0, low, part, int(part * gather_share)) for low in range(0, count_a, part)]
    everyone = (depth, 2, 2, 2)
    return pl.pallas_call(
        partial(
            gather_kernel, depth, line_items, plane_items,
            (tokens // tile) * (terms // group), gather_steps,
        ),
        grid=(tokens // tile, terms // group),
        in_specs=[
            pl.BlockSpec((group, tile, width), lambda t, j: (j, t, 0)),
            pl.BlockSpec((tile, width), lambda t, j: (t, 0)),
            pl.BlockSpec(memory_space=pltpu.SMEM),
        ]
        + [pl.BlockSpec(b.shape, lambda t, j: (0, 0, 0), pipeline_mode=pl.Buffered(1)) for b in blocks]
        + [HBM],
        out_specs=[
            pl.BlockSpec((tile, width), lambda t, j: (t, 0)),
            pl.BlockSpec((1, 8 * group, 128), lambda t, j: (t, j, 0)),
        ]
        + [HBM] * 4,
        out_shape=[
            jax.ShapeDtypeStruct((tokens, width), F32),
            jax.ShapeDtypeStruct((tokens // tile, 8 * terms, 128), F32),
            jax.ShapeDtypeStruct(everyone + blocks[0].shape, BF),
            jax.ShapeDtypeStruct(everyone + blocks[1].shape, BF),
            jax.ShapeDtypeStruct(everyone + blocks[2].shape, BF),
            jax.ShapeDtypeStruct((span * row_count, width), BF),
        ],
        scratch_shapes=LineGather.scratch(line_items, 3)
        + PlaneGather.scratch(plane_items)
        + RowExchange.scratch(),
        compiler_params=kernel_params(0),
        name="gather",
    )(history, cotangent.reshape(tokens, width), coefficient, *blocks, inputs)


def finish_kernel(depth, items, mid, arrays, small_ref, *refs):
    take = Taker(refs)
    grads = take(arrays)
    rows_in = take()
    out_ref, small_out, rows_out = take(3)
    me = Place(depth)
    reduce = Reduce(me, items, mid, grads, out_ref, take(19))
    rows = RowExchange(me, rows_in, rows_out, take(3), True)
    small = SmallSum(me, small_ref, small_out, take(5))
    me.greet()
    small.begin()
    reduce.begin()
    rows.begin()
    for t, stages in enumerate(reduce.rounds()):
        for stage in stages:
            stage()
        if t < 4:
            small.stage(t)
    small.drain()
    rows.drain()
    reduce.drain()


def finish(grads, small, row, row_count, depth):
    length, width = row.shape
    count = grads[0].shape[2]
    size = count // finish_cuts
    items = [(low, size) for low in range(0, count, size)]
    mid = size // finish_share
    vmem = pl.BlockSpec(memory_space=pltpu.VMEM)
    return pl.pallas_call(
        partial(finish_kernel, depth, items, mid, len(grads)),
        in_specs=[vmem] + [HBM] * (len(grads) + 1),
        out_specs=[vmem, vmem, HBM],
        out_shape=[
            jax.ShapeDtypeStruct((len(items), size, 16, 128), F32),
            jax.ShapeDtypeStruct(small.shape, F32),
            jax.ShapeDtypeStruct((row_count, length // row_count, width), row.dtype),
        ],
        scratch_shapes=Reduce.scratch(items, mid, depth, len(grads))
        + RowExchange.scratch()
        + SmallSum.scratch(small.shape, depth),
        compiler_params=kernel_params(1),
        name="finish",
    )(small, *grads, row)


def enter_kernel(depth, items, ready, rows_at, reach, x_ref, w_ref, vec_ref, cos_ref, sin_ref, sc_ref, sr_ref, *refs):
    take = Taker(refs)
    _, rows_in = take(2)
    n1_ref, q_ref, k_ref, v_ref, o_ref, lse_ref, got_f, rows_out = take(8)
    bias_ref, turned_ref = take(2)
    me = Place(depth)
    plane = PlaneGather(me, items, [got_f], take(4))
    rows = RowExchange(me, rows_in, rows_out, take(3), False)
    step = pl.program_id(0)
    tile, width = x_ref.shape
    length = q_ref.shape[1]
    tiles = length // tile
    pairs = width // 128
    block_rows = 256
    blocks = length // block_rows

    def begin():
        me.greet()
        for i in range(len(items)):
            plane.first(i)

    def second(i):
        if i == 0:
            own.wait()
        plane.second(i)
    def finish_all():
        plane.drain()
        rows.drain()

    at_steps(step, [(0, begin)])

    @pl.when(step == 0)
    def _():
        fill_bias(bias_ref, sc_ref, sr_ref, block_rows, reach)

    @pl.when(step < tiles)
    def _():
        centered, inverse = norm_parts(x_ref[...].astype(F32))
        normed = (centered * inverse * vec_ref[0:1, :width] + vec_ref[1:2, :width]).astype(BF)
        n1_ref[...] = normed
        cosine = jnp.concatenate([cos_ref[...]] * 2, axis=1)
        sine = jnp.concatenate([sin_ref[...]] * 2, axis=1)
        spot = pl.ds(pl.multiple_of(step * tile, tile), tile)
        per_part = width // 256
        for at in range(3 * per_part):
            part = nn_dot(normed, cols(w_ref, 2 * at, 2)) + vec_ref[2:3, 256 * at : 256 * at + 256]
            if at < 2 * per_part:
                part = part * cosine + swap_halves(part) * sine
            if at < per_part:
                part = part * HEAD_DIM ** (-0.5)
            target = (q_ref, k_ref, v_ref)[at // per_part]
            first = 2 * (at % per_part)
            target[first, spot, :] = part[:, :128].astype(BF)
            target[first + 1, spot, :] = part[:, 128:].astype(BF)

    pair = jnp.maximum(step - tiles, 0) // blocks
    current = jnp.maximum(step - tiles, 0) % blocks

    def attend_block(block):
        if block == 0:
            turned_ref[...] = v_ref[pair].T
        low, high = key_range(block, block_rows, reach)
        at = sum(h - l for l, h in (key_range(b, block_rows, reach) for b in range(block)))
        spot = slice(block * block_rows, (block + 1) * block_rows)
        keys = k_ref[pair, low:high, :]
        queries = q_ref[pair, spot, :]
        bias = bias_ref[at : at + high - low, :]
        halves = []
        for head in range(2):
            scores = nt_dot(head_mask(keys, head), queries) + bias
            top = jnp.max(scores, axis=0, keepdims=True)
            exponent = jnp.exp(scores - top)
            total = jnp.sum(exponent, axis=0, keepdims=True)
            probs = (exponent * (1.0 / total)).astype(BF)
            lse_ref[pair, head : head + 1, spot] = top + jnp.log(total)
            turned = turned_ref[HEAD_DIM * head : HEAD_DIM * head + HEAD_DIM, low:high]
            halves.append(nn_dot(turned, probs))
        lanes = pl.ds(pl.multiple_of(pair * 128, 128), 128)
        o_ref[spot, lanes] = jnp.concatenate(halves, axis=0).T.astype(BF)

    for block in range(blocks):
        pl.when((step >= tiles) & (current == block))(partial(attend_block, block))

    n = len(items)
    work = [(ready[0][i], partial(plane.second, i)) for i in range(n)]
    work += [(ready[1][i], partial(plane.third, i)) for i in range(n)]
    work.sort(key=lambda item: item[0])
    work += [(rows_at, rows.begin)]
    at_steps(step, work + [(tiles + pairs * blocks - 1, finish_all)])


def enter(x_row, w_qkv, vectors, cosine, sine, seg_col, seg_row, got_f, cotangent, reach, depth):
    length, width = x_row.shape
    array, lead = w_qkv
    tile = 256
    tiles, pairs = length // tile, width // 128
    steps = tiles + pairs * (length // 256)
    once = pl.Buffered(1)
    count = got_f.shape[4]
    size = count // 4
    items = [(0, low, size, size // enter_share) for low in range(0, count, size)]
    ready = (enter_first_steps, enter_second_steps)

    def const(shape):
        return pl.BlockSpec(shape, lambda i: (0,) * len(shape), pipeline_mode=once)

    def rows(lanes):
        return pl.BlockSpec((tile, lanes), lambda i: (jnp.minimum(i, tiles - 1), 0))

    heads = jax.ShapeDtypeStruct((pairs, length, 128), BF)
    return pl.pallas_call(
        partial(enter_kernel, depth, items, ready, enter_rows_step, reach),
        grid=(steps,),
        in_specs=[
            rows(width), const((lead,) + array.shape[1:]), const(vectors.shape), rows(128), rows(128),
            const(seg_col.shape), const(seg_row.shape), HBM, HBM,
        ],
        out_specs=[
            rows(width), const(heads.shape), const(heads.shape), const(heads.shape),
            const((length, width)), const((pairs, 2, length)), HBM, HBM,
        ],
        out_shape=[
            jax.ShapeDtypeStruct((length, width), BF), heads, heads, heads,
            jax.ShapeDtypeStruct((length, width), BF),
            jax.ShapeDtypeStruct((pairs, 2, length), F32),
            jax.ShapeDtypeStruct(got_f.shape, BF),
            jax.ShapeDtypeStruct((length, width), BF),
        ],
        scratch_shapes=[
            pltpu.VMEM((bias_rows(length, 256, reach), 256), F32),
            pltpu.VMEM((128, length), BF),
        ]
        + PlaneGather.scratch(items)
        + RowExchange.scratch(),
        input_output_aliases={7: 6},
        compiler_params=kernel_params(2),
        name="enter",
    )(x_row, array, vectors, cosine, sine, seg_col, seg_row, got_f, cotangent)


def leave_kernel(
    depth, items, mid, starts, rows_at, reach, arrays,
    q_ref, k_ref, v_ref, g_ref, lse_ref, sc_ref, sr_ref, cos_ref, sin_ref,
    x_ref, n1_ref, ghid_ref, w_ref, vec_ref, *refs,
):
    take = Taker(refs)
    grads = take(arrays)
    rows_in = take()
    gx_ref, gw_ref, gb_ref, gvec_ref, out_ref, rows_out = take(6)
    bias_ref, turned_ref, dk_acc, dv_acc, gp_ref, n1t_ref = take(6)
    me = Place(depth)
    reduce = Reduce(me, items, mid, grads, out_ref, take(19))
    rows = RowExchange(me, rows_in, rows_out, take(3), True)
    step = pl.program_id(0)
    length, width = x_ref.shape
    pairs = width // 128
    block_rows = 256
    blocks = length // block_rows
    attend_steps = pairs * blocks
    chunks = 3 * width // 256
    tile = 256
    tiles = length // tile

    def begin():
        me.greet()
        reduce.begin()
        rows.begin((0,))

    def end():
        rows.drain()
        reduce.drain()

    at_steps(step, [(0, begin)])

    @pl.when(step == 0)
    def _():
        fill_bias(bias_ref, sc_ref, sr_ref, block_rows, reach)

    pair = jnp.minimum(step // blocks, pairs - 1)
    current = step % blocks

    def attend_block(block):
        if block == 0:
            turned_ref[...] = k_ref[0].T
            dk_acc[...] = jnp.zeros_like(dk_acc)
            dv_acc[...] = jnp.zeros_like(dv_acc)
        low, high = key_range(block, block_rows, reach)
        at = sum(h - l for l, h in (key_range(b, block_rows, reach) for b in range(block)))
        spot = slice(block * block_rows, (block + 1) * block_rows)
        keys, vals = k_ref[0, low:high, :], v_ref[0, low:high, :]
        queries, grad = q_ref[0, spot, :], g_ref[spot, :]
        bias = bias_ref[at : at + high - low, :]
        halves = []
        for head in range(2):
            scores = nt_dot(head_mask(keys, head), queries) + bias
            probs = jnp.exp(scores - lse_ref[0, head : head + 1, spot])
            dprobs = nt_dot(head_mask(vals, head), grad)
            inner = jnp.sum(probs * dprobs, axis=0, keepdims=True)
            dscores = (probs * (dprobs - inner)).astype(BF)
            turned = turned_ref[HEAD_DIM * head : HEAD_DIM * head + HEAD_DIM, low:high]
            halves.append(nn_dot(turned, dscores))
            dk_acc[low:high, :] += nn_dot(dscores, head_mask(queries, head))
            dv_acc[low:high, :] += nn_dot(probs.astype(BF), head_mask(grad, head))
        grad_query = jnp.concatenate(halves, axis=0).T * HEAD_DIM ** (-0.5)
        turn(grad_query, pair, spot)
        if block == blocks - 1:
            turn(dk_acc[...], pairs + pair, slice(0, length))
            gp_ref[2 * pairs + pair] = dv_acc[...].astype(BF)

    def turn(values, place, spot):
        values = values.astype(BF).astype(F32)
        values = values * cos_ref[spot, :] - swap_halves(values) * sin_ref[spot, :]
        gp_ref[place, spot, :] = values.astype(BF)

    for block in range(blocks):
        pl.when((step < attend_steps) & (current == block))(partial(attend_block, block))

    @pl.when(step == attend_steps)
    def _():
        @pl.loop(0, tiles)
        def _(t):
            spot = pl.ds(pl.multiple_of(t * tile, tile), tile)
            n1t_ref[:, spot] = n1_ref[spot, :].T

        gvec_ref[...] = jnp.zeros_like(gvec_ref)

    @pl.when((step >= attend_steps) & (step < attend_steps + chunks))
    def _():
        at = jnp.clip(step - attend_steps, 0, chunks - 1)
        grad = jnp.concatenate([gp_ref[2 * at], gp_ref[2 * at + 1]], axis=1)
        for r in range(width // 256):
            put_tiles(gw_ref, 16 * r, 0, nn_dot(n1t_ref[256 * r : 256 * r + 256, :], grad).astype(BF))
        gb_ref[0:1, :] = jnp.sum(grad.astype(F32), axis=0, keepdims=True)

    @pl.when(step >= attend_steps + chunks)
    def _():
        t = jnp.maximum(step - attend_steps - chunks, 0)
        spot = pl.ds(pl.multiple_of(t * tile, tile), tile)
        grad = jnp.concatenate([gp_ref[p, spot, :] for p in range(3 * pairs)], axis=1)
        grad_norm = nt_dot(grad, cols(w_ref, 0, 3 * pairs))
        centered, inverse = norm_parts(x_ref[spot, :].astype(F32))
        normed = centered * inverse
        gvec_ref[0:1, :] += jnp.sum(normed * grad_norm, axis=0, keepdims=True)
        gvec_ref[1:2, :] += jnp.sum(grad_norm, axis=0, keepdims=True)
        scaled = grad_norm * vec_ref[0:1, :]
        grad_value = inverse * (
            scaled
            - jnp.mean(scaled, axis=1, keepdims=True)
            - normed * jnp.mean(scaled * normed, axis=1, keepdims=True)
        )
        gx_ref[spot, :] = (ghid_ref[spot, :] + grad_value).astype(gx_ref.dtype)

    work = [(when, partial(rows.begin, (p,))) for p, when in enumerate(rows_at) if p]
    for start, stages in zip(starts, reduce.rounds()):
        for at, stage in enumerate(stages):
            work.append((min(start + at, attend_steps + chunks + tiles - 1), stage))
    at_steps(step, work + [(attend_steps + chunks + tiles - 1, end)])


def leave(
    queries, keys, values, grad_attended, lse, seg_col, seg_row, cosine, sine,
    x_row, n1, grad_hidden, w_qkv, vectors, grads, row, row_count, reach, depth,
):
    length, width = x_row.shape
    array, lead = w_qkv
    pairs, blocks = width // 128, length // 256
    attend_steps, chunks, tiles = pairs * blocks, 3 * width // 256, length // 256
    steps = attend_steps + chunks + tiles
    once = pl.Buffered(1)
    count = grads[0].shape[2]
    size = count // 4
    items = [(low, size) for low in range(0, count, size)]
    mid = size // leave_share
    starts = leave_steps

    def const(shape):
        return pl.BlockSpec(shape, lambda i: (0,) * len(shape), pipeline_mode=once)

    def pair_at(i):
        return jnp.minimum(i // blocks, pairs - 1)

    def chunk_at(i):
        return jnp.clip(i - attend_steps, 0, chunks - 1)

    heads = pl.BlockSpec((1, length, 128), lambda i: (pair_at(i), 0, 0))
    rows = const((length, width))
    row_tiles = width // 16
    return pl.pallas_call(
        partial(leave_kernel, depth, items, mid, starts, leave_rows_steps, reach, len(grads)),
        grid=(steps,),
        in_specs=[
            heads, heads, heads,
            pl.BlockSpec((length, 128), lambda i: (0, pair_at(i))),
            pl.BlockSpec((1, 2, length), lambda i: (pair_at(i), 0, 0)),
            const(seg_col.shape), const(seg_row.shape), const(cosine.shape), const(sine.shape),
            rows, rows, rows, const((lead,) + array.shape[1:]), const(vectors.shape),
        ]
        + [HBM] * (len(grads) + 1),
        out_specs=[
            rows,
            pl.BlockSpec((row_tiles, 2, 16, 128), lambda i: (0, chunk_at(i), 0, 0)),
            pl.BlockSpec((8, 256), lambda i: (0, chunk_at(i))),
            const((8, width)),
            const((len(items), size, 16, 128)),
            HBM,
        ],
        out_shape=[
            jax.ShapeDtypeStruct((length, width), BF),
            jax.ShapeDtypeStruct((row_tiles, 3 * width // 128, 16, 128), BF),
            jax.ShapeDtypeStruct((8, 3 * width), F32),
            jax.ShapeDtypeStruct((8, width), F32),
            jax.ShapeDtypeStruct((len(items), size, 16, 128), F32),
            jax.ShapeDtypeStruct((row_count, length // row_count, width), row.dtype),
        ],
        scratch_shapes=[
            pltpu.VMEM((bias_rows(length, 256, reach), 256), F32),
            pltpu.VMEM((128, length), BF),
            pltpu.VMEM((length, 128), F32),
            pltpu.VMEM((length, 128), F32),
            pltpu.VMEM((3 * pairs, length, 128), BF),
            pltpu.VMEM((width, length), BF),
        ]
        + Reduce.scratch(items, mid, depth, len(grads))
        + RowExchange.scratch(),
        compiler_params=kernel_params(3),
        name="leave",
    )(
        queries, keys, values, grad_attended, lse, seg_col, seg_row, cosine, sine,
        x_row, n1, grad_hidden, array, vectors, *grads, row,
    )


HALO = 2048


class Plan:
    def __init__(self, devices, shape_list):
        sizes = [math.prod(shape) for shape in shape_list]
        starts = [sum(sizes[:i]) for i in range(len(sizes))]
        self.total = sum(sizes)
        self.devices = devices
        self.own = self.total // devices
        self.matrices = [(starts[i], shape_list[i]) for i in (2, 4)]
        self.vectors = [(0, sizes[0] + sizes[1]), (starts[3], sizes[3]), (starts[5], sizes[5])]
        first, second = (math.prod(shape) for _, shape in self.matrices)
        self.block = (first + second) // devices
        self.split = devices * first // (first + second)
        self.rows = [
            shape[0] // n if n else 0
            for (_, shape), n in zip(self.matrices, (self.split, devices - self.split))
        ]
        self.fits = self.total % devices == 0 and (first + second) % devices == 0
        for (_, shape), n, rows in zip(
            self.matrices, (self.split, devices - self.split), self.rows
        ):
            self.fits = self.fits and n > 0 and rows * n == shape[0] and rows % 16 == 0
            self.fits = self.fits and rows * shape[1] == self.block
        self.owners = [at // self.own for at, _ in self.vectors]
        if self.fits:
            for s in range(devices):
                shift = self.block_start(s) - self.own * s
                self.fits = self.fits and -HALO <= shift <= HALO
                self.fits = self.fits and shift + self.block - self.own <= HALO
                self.fits = self.fits and self.own - self.block - shift <= HALO
            for (at, size), owner in zip(self.vectors, self.owners):
                self.fits = self.fits and at + size <= self.own * (owner + 1) + HALO
            self.fits = self.fits and len(set(self.owners)) == len(self.owners)

    def block_start(self, s):
        (first, _), (second, _) = self.matrices
        if isinstance(s, int):
            return first + self.block * s if s < self.split else second + self.block * (s - self.split)
        return jnp.where(
            s < self.split, first + self.block * s, second + self.block * (s - self.split)
        )

    def tile_shapes(self):
        return [
            (rows // 16, shape[1] // 128) for (_, shape), rows in zip(self.matrices, self.rows)
        ]

    def to_tiles(self, flat, s):
        forms = [
            flat.reshape(rt, 16, ct, 128).transpose(0, 2, 1, 3).reshape(rt * ct, 16, 128)
            for rt, ct in self.tile_shapes()
        ]
        return jnp.where(s < self.split, forms[0], forms[1])

    def from_tiles(self, tiles, s):
        forms = [
            tiles.reshape(rt, ct, 16, 128).transpose(0, 2, 1, 3).reshape(-1)
            for rt, ct in self.tile_shapes()
        ]
        return jnp.where(s < self.split, forms[0], forms[1])

    def vector_rows(self):
        return -(-max(size for _, size in self.vectors) // 1024) * 8

    def blocks(self, flat, before, after, s):
        room = self.vector_rows() * 128
        joined = jnp.concatenate([before, flat, after, jnp.zeros((room,), flat.dtype)])
        aligned = lax.dynamic_slice(
            joined, (HALO + self.block_start(s) - self.own * s,), (self.block,)
        )
        place = jnp.int32(0)
        for (at, _), owner in zip(self.vectors, self.owners):
            place = jnp.where(s == owner, at - self.own * owner, place)
        extra = lax.dynamic_slice(joined, (HALO + place,), (room,))
        return self.to_tiles(aligned, s), extra.reshape(-1, 128)

    def shard(self, aligned, before, after, vectors, s):
        room = self.vector_rows() * 128
        edge = jnp.zeros((room,), aligned.dtype)
        joined = jnp.concatenate([edge, before, aligned, after, edge])
        begin = self.block_start(s)
        for (at, size), value in zip(self.vectors, vectors):
            place = jnp.clip(room + HALO + at - begin, 0, joined.shape[0] - size)
            joined = lax.dynamic_update_slice(joined, value, (place,))
        return lax.dynamic_slice(joined, (room + HALO + self.own * s - begin,), (self.own,))


def neighbour_edges(values_list, count):
    axes = ("dp", "tok")
    tails = jnp.stack([v[-HALO:] for v in values_list])
    heads = jnp.stack([v[:HALO] for v in values_list])
    before = lax.ppermute(tails, axes, [(i, (i + 1) % count) for i in range(count)])
    after = lax.ppermute(heads, axes, [(i, (i - 1) % count) for i in range(count)])
    return before, after


def plans(devices):
    return Plan(devices, attention_shapes()), Plan(devices, feedforward_shapes())


def row_tables(lengths_row, length):
    places = jnp.arange(length, dtype=jnp.int32)
    segment, position = layout(lengths_row[None], places)
    lane = jnp.arange(128, dtype=jnp.int32) % HEAD_DIM
    half_dim = HEAD_DIM // 2
    frequency = jnp.exp(
        (lane % half_dim).astype(jnp.float32) * (-2.0 * math.log(10000.0) / HEAD_DIM)
    )
    angle = position[0].astype(jnp.float32)[:, None] * frequency[None, :]
    sine = jnp.where(lane < half_dim, -1.0, 1.0)[None, :] * jnp.sin(angle)
    return segment[0], jnp.cos(angle), sine


def row_shards(
    inputs,
    history,
    document_lengths,
    cotangent,
    attention_params,
    attention_first,
    attention_second,
    feedforward_params,
    feedforward_first,
    feedforward_second,
    mixing_offsets,
    mixing_first,
    mixing_second,
    step_count,
):
    row_count, span, width = inputs.shape
    tok_size = lax.axis_size("tok")
    devices = lax.axis_size("dp") * tok_size
    length = span * tok_size
    tokens_all = row_count * span * devices
    axes = ("dp", "tok")
    s = lax.axis_index(axes)
    plan_a, plan_f = plans(devices)
    reach = length // 2

    depth = lax.axis_size("dp") // 2
    tokens = row_count * span
    term_count = mixing_offsets.shape[0]
    coefficient = mixing_offsets + (jnp.arange(term_count) == term_count - 1).astype(F32)

    low_a, low_f = attention_params.astype(BF), feedforward_params.astype(BF)
    before, after = neighbour_edges([low_a, low_f], devices)
    tiles_a, extra_a = plan_a.blocks(low_a, before[0], after[0], s)
    tiles_f, extra_f = plan_f.blocks(low_f, before[1], after[1], s)
    extra = jnp.concatenate([extra_a, extra_f]).reshape(-1, 16, 128)
    count_a, count_f = tiles_a.shape[0], tiles_f.shape[0]
    history_part, history_dots, got_a, got_e, got_f, x_row = gather(
        [tiles_a, extra, tiles_f], inputs, history.reshape(term_count - 1, tokens, width), cotangent,
        coefficient, depth,
    )
    got_a = got_a.reshape(devices, count_a, 16, 128)
    extras = got_e.reshape(devices, -1).astype(F32)
    room_a = plan_a.vector_rows() * 128

    def pick(plan, which, at):
        return extras[plan.owners[which], at : at + plan.vectors[which][1]]

    gain_one, shift_one = jnp.split(pick(plan_a, 0, 0), 2)
    b_qkv, b_out = pick(plan_a, 1, 0), pick(plan_a, 2, 0)
    gain_two, shift_two = jnp.split(pick(plan_f, 0, room_a), 2)
    b_up, b_down = pick(plan_f, 1, room_a), pick(plan_f, 2, room_a)
    (rq, cq), (ro, co) = plan_a.tile_shapes()
    (ru, cu), (rd, cd) = plan_f.tile_shapes()
    w_qkv = (got_a.reshape(devices, rq, cq, 16, 128), plan_a.split)
    w_out = (got_a.reshape(devices, ro, co, 16, 128), devices - plan_a.split)
    def stack(vectors, wide):
        vectors = [jnp.pad(v, (0, wide - v.shape[0])) for v in vectors]
        vectors = vectors + [jnp.zeros((wide,), F32)] * (8 - len(vectors))
        return jnp.stack(vectors)

    own_lengths = lax.dynamic_index_in_dim(document_lengths, lax.axis_index("tok"), 0, False)
    segment, cosine, sine = row_tables(own_lengths, length)
    seg_col, seg_row = segment[:, None], segment[None, :]

    normed_one, queries, keys, values, attended, lse, got_f, cot_row = enter(
        x_row, w_qkv, stack([gain_one, shift_one, b_qkv], 3 * width), cosine, sine, seg_col, seg_row,
        got_f, cotangent, reach, depth,
    )
    w_up = (got_f.reshape(devices, ru, cu, 16, 128), plan_f.split)
    w_down = (got_f.reshape(devices * rd, cd, 16, 128), plan_f.split * rd // 16)
    grad_history, block_out, grad_attended, grad_hidden, gw_up, gw_down, gw_out, gb_up, gvec_two = middle(
        x_row, attended, cot_row, w_out, w_up, w_down,
        stack([gain_two, shift_two, b_out, b_down], width), b_up[None, :],
        cotangent.reshape(tokens, width), coefficient,
    )
    def by_core(array, tiles):
        return array.reshape(-1, 2, *tiles.shape)

    grad_row, gw_qkv, gb_qkv, gvec_one, sum_f, block_back = leave(
        queries, keys, values, grad_attended, lse, seg_col, seg_row, cosine, sine,
        x_row, normed_one, grad_hidden, w_qkv, stack([gain_one], width),
        [by_core(gw_up, tiles_f), by_core(gw_down, tiles_f)], block_out, row_count, reach, depth,
    )
    mixed = history_part.reshape(row_count, span, width) + coefficient[-1] * block_back.astype(F32)

    small = jnp.concatenate(
        [
            gvec_one[0], gvec_one[1], gb_qkv[0], gvec_two[2],
            gvec_two[0], gvec_two[1], gb_up[0], gvec_two[3],
            jnp.sum(history_dots.reshape(-1, term_count - 1, 8 * 128), axis=(0, 2)),
            jnp.sum(gvec_two[4])[None],
        ]
    )
    small_size = small.shape[0]
    small = jnp.pad(small, (0, -small_size % 1024)).reshape(-1, 128)
    scale = 1.0 / tokens_all
    sum_a, small, grad_back = finish(
        [by_core(gw_qkv, tiles_a), by_core(gw_out, tiles_a)], small, grad_row, row_count, depth
    )
    small = small.reshape(-1)[:small_size] / tokens_all
    grad_inputs = grad_back.astype(F32)
    flat_a = plan_a.from_tiles(sum_a.reshape(tiles_a.shape) * scale, s)
    flat_f = plan_f.from_tiles(sum_f.reshape(tiles_f.shape) * scale, s)
    before, after = neighbour_edges([flat_a, flat_f], devices)
    at = 0
    parts = []
    for plan in (plan_a, plan_f):
        for _, size in plan.vectors:
            parts.append(small[at : at + size])
            at = at + size
    attention_share = plan_a.shard(flat_a, before[0], after[0], parts[:3], s)
    feedforward_share = plan_f.shard(flat_f, before[1], after[1], parts[3:], s)
    mixing_grad = small[at:]

    count_now = step_count[0]
    attention_places = s * plan_a.own + jnp.arange(plan_a.own, dtype=jnp.int32)
    feedforward_places = s * plan_f.own + jnp.arange(plan_f.own, dtype=jnp.int32)
    attention_step = adam_update(
        attention_params, attention_share, attention_first, attention_second, count_now,
        decay_mask(attention_places, attention_shapes()),
    )
    feedforward_step = adam_update(
        feedforward_params, feedforward_share, feedforward_first, feedforward_second, count_now,
        decay_mask(feedforward_places, feedforward_shapes()),
    )
    mixing_step = adam_update(
        mixing_offsets, mixing_grad, mixing_first, mixing_second, count_now, 0.0
    )
    return (
        mixed.astype(BF),
        grad_inputs,
        grad_history.reshape(history.shape),
        *attention_step,
        *feedforward_step,
        *mixing_step,
    )


def shards(inputs, *others):
    row_count, span, width = inputs.shape
    tok_size = lax.axis_size("tok")
    devices = lax.axis_size("dp") * tok_size
    by_rows = row_count == tok_size == 4 and lax.axis_size("dp") == 8 and width == D
    if by_rows and all(plan.fits for plan in plans(devices)):
        return row_shards(inputs, *others)
    return general_shards(inputs, *others)


def solution(mesh):
    in_specs = (
        P("dp", "tok", None),
        P(None, "dp", "tok", None),
        P("dp", None),
        P("dp", "tok", None),
        P(("dp", "tok")),
        P(("dp", "tok")),
        P(("dp", "tok")),
        P(("dp", "tok")),
        P(("dp", "tok")),
        P(("dp", "tok")),
        P(),
        P(),
        P(),
        P(),
    )
    out_specs = (
        P("dp", "tok", None),
        P("dp", "tok", None),
        P(None, "dp", "tok", None),
        P(("dp", "tok")),
        P(("dp", "tok")),
        P(("dp", "tok")),
        P(("dp", "tok")),
        P(("dp", "tok")),
        P(("dp", "tok")),
        P(),
        P(),
        P(),
    )
    return jax.shard_map(shards, mesh=mesh, in_specs=in_specs, out_specs=out_specs, check_vma=False)
```
